512 devices in a mesh: lon: 64 (over y_lo, z, core), lat: 8 (over y_hi, x).
Axes of the slice: x: 4, y: 8 (y_hi: 2, y_lo: 4; y = y_hi * 4 + y_lo), z: 8, core: 2. Of those that a mesh axis runs over, the one named last changes fastest.
Arguments:
- final_adjoint: float32 [2, 38, 64, 8192], P(None, None, 'lat', 'lon'), may hold values from -6 to 6
- store: bfloat16 [4, 38, 16, 8, 8192], P(None, None, None, 'lat', 'lon'), may hold values from -6 to 6
- holder_offset: int32 [2, 8, 64], replicated, may hold values from 0 to 7
- holder_slot: int32 [2, 8, 64], replicated, may hold values from 0 to 15, as said below
- bottom_level: int32 [64, 8192], P('lat', 'lon'), may hold values from 0 to 38
- mix_class: int32 [37, 64, 8192], P(None, 'lat', 'lon'), may hold values from 0 to 7
- mix_table: float32 [8], replicated, may hold values from 0.02 to 0.4
Outputs:
- tracer_adjoint: float32 [2, 38, 64, 8192], P(None, None, 'lat', 'lon')
- velocity_adjoint: float32 [2, 38, 64, 8192], P(None, None, 'lat', 'lon')
The draws below stay inside these ranges and needn't reach their ends.
Inputs may be any that keep to these rules, and one draw needn't show every extreme that they name: `holder_slot`: for every longitude tile, the 16 entries over all steps and bands are all different.
All inputs are finite; a program needn't handle non-finite values.
Results may differ from the reference program's by a relative error of at most 0.0014.
Values may be sent and summed in bfloat16 or wider, within the bound.
No kernel may reach another device: no remote copies, remote signals or barrier semaphores. Data moves between devices by JAX's collectives and lax.ppermute only.
A program may use at most 64 MiB of HBM per device.

```python
import math
import jax
import jax.numpy as jnp

K = 38
CLASSES = 8
STEPS = 2
CJ = 8
CI = 128
BANDS = 8
TILES = 64
PIECE = 1
SLOTS = 16
NJ = 64
NI = 8192
KM = 37


def draw_holder_slot(key, part):
    keys = jax.random.split(key, TILES)
    orders = jax.vmap(lambda single: jax.random.permutation(single, SLOTS))(keys)
    return orders.reshape(TILES, STEPS, BANDS).transpose(1, 2, 0).astype(jnp.int32)


def draw_bottom_level(key, part):
    first_key, second_key = jax.random.split(key)
    depth = jax.random.randint(first_key, (NJ, NI), 1, K + 1)
    coin = jax.random.randint(second_key, (NJ, NI), 0, 10)
    return jnp.where(coin < 3, 0, depth).astype(jnp.int32)


def touch_ends(values, own_key, smallest, top_value):
    spot = [jax.random.randint(jax.random.fold_in(own_key, axis), (), 0, length) for axis, length in enumerate(values.shape)]
    main_axis = values.shape.index(max(values.shape))
    beside = spot[:main_axis] + [(spot[main_axis] + 1) % values.shape[main_axis]] + spot[main_axis + 1:]
    return values.at[tuple(spot)].set(smallest).at[tuple(beside)].set(top_value)


def steps_of(own_key, extent, pieces, low, high):
    def one(axis_at, blocks):
        draws = jax.random.uniform(jax.random.fold_in(jax.random.fold_in(own_key, 6), axis_at), (blocks,), jnp.float32, low / len(pieces), high / len(pieces))
        return jnp.repeat(jnp.exp(draws), extent[axis_at] // blocks).reshape((-1,) + (1,) * (len(extent) - axis_at - 1))

    loudness = one(*pieces[0])
    for cut in pieces[1:]:
        loudness = loudness * one(*cut)
    return loudness


def gaussian(rng, extent, deviation, bound, cuts=(), held_as=jnp.bfloat16):
    array = deviation * jax.random.normal(rng, extent, jnp.float32)
    if cuts:
        array = array * steps_of(rng, extent, cuts, -0.22, 0.18)
    return jnp.clip(array, -bound, bound).astype(held_as)


def setup_inputs(seed: int = 0) -> dict:
    key_of = jax.random.split(jax.random.key(seed), 8)
    final_adjoint = gaussian(key_of[0], (2, K, NJ, NI), 1.0, 6.0, ((2, 8), (3, 64)), jnp.float32)
    store = gaussian(key_of[1], (4, K, SLOTS, CJ, NI), 1.0, 6.0, ((3, 8), (4, 64)))
    holder_offset = touch_ends(jax.random.randint(key_of[2], (STEPS, BANDS, TILES), 0, BANDS), jax.random.fold_in(key_of[2], 1), 0, BANDS - 1).astype(jnp.int32)
    holder_slot = draw_holder_slot(jax.random.fold_in(key_of[7], 71), 0)
    bottom_level = draw_bottom_level(jax.random.fold_in(key_of[7], 71), 0)
    mix_class = touch_ends(jax.random.randint(key_of[5], (KM, NJ, NI), 0, CLASSES), jax.random.fold_in(key_of[5], 1), 0, CLASSES - 1).astype(jnp.int32)
    mix_table = jnp.clip(jnp.exp(jax.random.uniform(key_of[6], (CLASSES,), jnp.float32, math.log(0.02), math.log(0.4))), 0.02, 0.4)
    return {"final_adjoint": final_adjoint, "store": store, "holder_offset": holder_offset, "holder_slot": holder_slot, "bottom_level": bottom_level, "mix_class": mix_class, "mix_table": mix_table}


ADVECT_HALF = 0.125
DIFFUSE = 0.1


def transpose_step(masked, east, west, north, south, tracer, tracer_east, tracer_north, zonal, zonal_west, meridional, meridional_south, south_open, kappa_below, kappa_above):
    below = jnp.concatenate([masked[:, 1:], jnp.zeros_like(masked[:, :1])], axis=1)
    above = jnp.concatenate([jnp.zeros_like(masked[:, :1]), masked[:, :-1]], axis=1)
    advect = zonal * (east - masked) + zonal_west * (masked - west) + meridional * (north - masked) + meridional_south * (masked - south)
    spread = (east - masked) + (west - masked) + (north - masked) + south_open * (south - masked)
    mixing = kappa_below * (below - masked) + kappa_above * (above - masked)
    result = masked + ADVECT_HALF * advect + DIFFUSE * spread + mixing
    zonal_grad = ADVECT_HALF * jnp.sum((tracer + tracer_east) * (east - masked), axis=0)
    merid_grad = ADVECT_HALF * jnp.sum((tracer + tracer_north) * (north - masked), axis=0)
    return result, zonal_grad, merid_grad


def neighbours(field):
    east = jnp.roll(field, -1, axis=-1)
    west = jnp.roll(field, 1, axis=-1)
    north = jnp.concatenate([field[..., 1:, :], jnp.flip(field[..., -1:, :], axis=-1)], axis=-2)
    south = jnp.concatenate([jnp.zeros_like(field[..., :1, :]), field[..., :-1, :]], axis=-2)
    return east, west, north, south


def fetch_state(store, holder_offset, holder_slot, step_index):
    row_index = jnp.arange(NJ, dtype=jnp.int32)
    col_index = jnp.arange(NI, dtype=jnp.int32)
    band_of = row_index // CJ
    piece_of = (row_index % CJ) // PIECE
    within = row_index % PIECE
    tile_of = col_index // CI
    slots = holder_slot[step_index][band_of[:, None], tile_of[None, :]]
    offsets = holder_offset[step_index][band_of[:, None], tile_of[None, :]]
    source_row = ((piece_of[:, None] + offsets) % BANDS) * PIECE + within[:, None]
    return store[:, :, slots, source_row, col_index[None, :]]


def reference(final_adjoint, store, holder_offset, holder_slot, bottom_level, mix_class, mix_table):
    ocean_mask = (jnp.arange(K, dtype=jnp.int32)[:, None, None] < bottom_level[None]).astype(jnp.float32)
    kappa = mix_table[mix_class]
    zero_level = jnp.zeros((1, NJ, NI), jnp.float32)
    kappa_below = jnp.concatenate([kappa, zero_level], axis=0)
    kappa_above = jnp.concatenate([zero_level, kappa], axis=0)
    south_open = (jnp.arange(NJ, dtype=jnp.int32) > 0).astype(jnp.float32)[:, None]
    adjoint = final_adjoint
    zonal_total = jnp.zeros((K, NJ, NI), jnp.float32)
    merid_total = jnp.zeros((K, NJ, NI), jnp.float32)
    for step_index in range(STEPS - 1, -1, -1):
        trajectory = fetch_state(store, holder_offset, holder_slot, step_index).astype(jnp.float32)
        tracer = trajectory[0:2]
        zonal = trajectory[2]
        meridional = trajectory[3]
        masked = ocean_mask * adjoint
        east, west, north, south = neighbours(masked)
        tracer_east, unused_west, tracer_north, unused_south = neighbours(tracer)
        zonal_west = jnp.roll(zonal, 1, axis=-1)
        meridional_south = jnp.concatenate([jnp.zeros_like(meridional[:, :1]), meridional[:, :-1]], axis=1)
        fold_velocity = jnp.concatenate([jnp.zeros_like(meridional[:, :-1]), jnp.flip(meridional[:, -1:], axis=-1)], axis=1)
        meridional_net = meridional - fold_velocity
        adjoint, zonal_grad, merid_grad = transpose_step(masked, east, west, north, south, tracer, tracer_east, tracer_north, zonal, zonal_west, meridional_net, meridional_south, south_open, kappa_below, kappa_above)
        zonal_total = zonal_total + zonal_grad
        merid_total = merid_total + merid_grad
    return adjoint, jnp.stack([zonal_total, merid_total])
```

```python
import functools

import jax
import jax.numpy as jnp
from jax import lax
from jax.experimental import pallas as pl
from jax.experimental.pallas import tpu as pltpu
from jax.sharding import PartitionSpec as P

STEP_ORDER = (1, 0)
FIELDS = 4
ADVECT_HALF = 0.125
DIFFUSE = 0.1

ROWS = 8
LANES = 128

EDGE_STATE = (0, 256)
EDGE_MASKED = 512
EDGE_PART = 640
EDGE_LANES = 768


class Layout:
    def __init__(self, levels):
        self.tracer = (0, 3 * levels)
        self.merid = (2 * levels, 5 * levels)
        self.masked = 6 * levels
        self.part = 8 * levels
        self.corner = 10 * levels
        self.bottom = 11 * levels
        self.rows = (11 * levels + 1 + 15) // 16 * 16


def shift(block, amount, axis):
    return pltpu.roll(block, amount % block.shape[axis], axis)


def lanes_of(shape):
    return lax.broadcasted_iota(jnp.int32, shape, 1)


def rows_of(shape):
    return lax.broadcasted_iota(jnp.int32, shape, 0)


def strided(ref, start, count):
    return ref[pl.ds(start, count, stride=ROWS), :]


def request_kernel(slot_ref, store_ref, out_ref, wide_ref):
    tile = lax.axis_index("lon")
    bands, steps, pieces, lanes = out_ref.shape
    slots = store_ref.shape[0] // pieces
    wide_ref[...] = store_ref[...].astype(jnp.float32)
    for band in range(bands):
        for at, step in enumerate(STEP_ORDER):
            slot = slot_ref[step, band, tile]
            rows = wide_ref[pl.ds(slot, pieces, stride=slots), :]
            out_ref[band, at] = rows.astype(jnp.bfloat16)


def prepare_kernel(table_ref, adjoint_ref, bottom_ref, mix_ref, masked_ref, base_ref, kappa_ref):
    levels = adjoint_ref.shape[0] // (2 * ROWS)
    bottom = bottom_ref[...]
    edge = jnp.zeros((ROWS, LANES), jnp.float32)
    kappa_ref[0:ROWS] = edge
    kappa_ref[levels * ROWS : (levels + 1) * ROWS] = edge
    for level in range(levels - 1):
        classes = mix_ref[level * ROWS : (level + 1) * ROWS]
        kappa = jnp.full((ROWS, LANES), table_ref[0], jnp.float32)
        for index in range(1, table_ref.shape[0]):
            kappa = jnp.where(classes == index, table_ref[index], kappa)
        kappa_ref[(level + 1) * ROWS : (level + 2) * ROWS] = kappa
    for tracer in range(2):
        start = tracer * levels * ROWS
        for level in range(levels):
            here = slice(start + level * ROWS, start + (level + 1) * ROWS)
            masked_ref[here] = jnp.where(level < bottom, adjoint_ref[here], 0.0)
        for level in range(levels):
            base_ref[start + level * ROWS : start + (level + 1) * ROWS] = mixed(
                masked_ref, kappa_ref, start, level, levels
            )


def mixed(masked_ref, kappa_ref, start, level, levels):
    def at(index):
        return masked_ref[start + index * ROWS : start + (index + 1) * ROWS]

    masked = at(level)
    below = at(level + 1) if level + 1 < levels else jnp.zeros_like(masked)
    above = at(level - 1) if level > 0 else jnp.zeros_like(masked)
    kappa_above = kappa_ref[level * ROWS : (level + 1) * ROWS]
    kappa_below = kappa_ref[(level + 1) * ROWS : (level + 2) * ROWS]
    return masked + kappa_below * (below - masked) + kappa_above * (above - masked)


def edges_kernel(
    offset_ref,
    piece_ref,
    masked_ref,
    base_ref,
    bottom_ref,
    state_ref,
    to_west_ref,
    to_east_ref,
    top_ref,
    bot_ref,
    part_ref,
    column_ref,
):
    tile = lax.axis_index("lon")
    band = lax.axis_index("lat")
    levels = masked_ref.shape[0] // (2 * ROWS)
    pieces = FIELDS * levels
    holders = piece_ref.shape[0]
    lane = lanes_of((ROWS, LANES))
    sources = []
    for at, step in enumerate(STEP_ORDER):
        offset = offset_ref[step, band, tile]
        chunks = []
        for row in range(ROWS):
            chunk = piece_ref[lax.rem(row + offset, holders), at]
            state_ref[pl.ds(at * pieces * ROWS + row, pieces, stride=ROWS), :] = chunk.astype(
                jnp.float32
            )
            chunks.append(chunk)
        sources.append((EDGE_STATE[at], jnp.concatenate(chunks, axis=1)))
    for level in range(levels):
        zonal = state_ref[(2 * levels + level) * ROWS : (2 * levels + level + 1) * ROWS]
        east_factor = ADVECT_HALF * zonal + DIFFUSE
        west_factor = ADVECT_HALF * shift(zonal, 1, 1) - DIFFUSE
        for tracer in range(2):
            here = slice((tracer * levels + level) * ROWS, (tracer * levels + level + 1) * ROWS)
            masked = masked_ref[here]
            face = jnp.where(
                lane < LANES // 2,
                east_factor * (shift(masked, -1, 1) - masked),
                west_factor * (masked - shift(masked, 1, 1)),
            )
            part_ref[here] = base_ref[here] + face
    for start, ref in ((EDGE_MASKED, masked_ref), (EDGE_PART, part_ref)):
        columns = [strided(ref, row, 2 * levels).astype(jnp.bfloat16) for row in range(ROWS)]
        sources.append((start, jnp.concatenate(columns, axis=1)))
    place = (ROWS * LANES, LANES)
    from_row, from_lane = rows_of(place) // LANES, rows_of(place) % LANES
    chosen = ((from_lane == 0) & (lanes_of(place) == from_row)) | (
        (from_lane == LANES - 1) & (lanes_of(place) == from_row + ROWS)
    )
    pick = jnp.where(chosen, 1.0, 0.0).astype(jnp.bfloat16)
    column_ref[...] = jnp.zeros_like(column_ref)
    for start, source in sources:
        column_ref[start : start + source.shape[0]] = jnp.dot(
            source, pick, preferred_element_type=jnp.float32
        )
    edge = jnp.transpose(column_ref[...])
    bottom = bottom_ref[...].astype(jnp.float32)
    spot = lanes_of((ROWS, EDGE_LANES)) == EDGE_MASKED + 2 * levels
    to_west_ref[...] = jnp.where(spot, bottom[:, 0:1], edge[0:ROWS]).astype(jnp.bfloat16)
    to_east_ref[...] = jnp.where(spot, bottom[:, LANES - 1 :], edge[ROWS : 2 * ROWS]).astype(
        jnp.bfloat16
    )
    layout = Layout(levels)
    wide = lanes_of((levels, LANES))
    for row, inner, draft_ref in ((ROWS - 1, ROWS - 2, top_ref), (0, 1, bot_ref)):
        for at in range(2):
            begin = at * pieces * ROWS
            draft_ref[layout.tracer[at] : layout.tracer[at] + 2 * levels] = strided(
                state_ref, begin + row, 2 * levels
            )
            draft_ref[layout.merid[at] : layout.merid[at] + levels] = strided(
                state_ref, begin + 3 * levels * ROWS + row, levels
            )
        zonal = strided(state_ref, 2 * levels * ROWS + row, levels)
        merid = strided(state_ref, 3 * levels * ROWS + min(row, inner), levels)
        east_factor = ADVECT_HALF * zonal + DIFFUSE
        west_factor = ADVECT_HALF * shift(zonal, 1, 1) - DIFFUSE
        for tracer in range(2):
            begin = tracer * levels * ROWS
            masked = strided(masked_ref, begin + row, levels)
            next_row = strided(masked_ref, begin + inner, levels)
            if row > inner:
                along = (ADVECT_HALF * merid - DIFFUSE) * (masked - next_row)
            else:
                along = (ADVECT_HALF * merid + DIFFUSE) * (next_row - masked)
            east = east_factor * (shift(masked, -1, 1) - masked)
            west = west_factor * (masked - shift(masked, 1, 1))
            part = strided(base_ref, begin + row, levels) + along
            part = part + jnp.where(wide < LANES - 1, east, 0.0) + jnp.where(wide > 0, west, 0.0)
            at_masked = layout.masked + tracer * levels
            at_part = layout.part + tracer * levels
            draft_ref[at_masked : at_masked + levels] = masked
            draft_ref[at_part : at_part + levels] = part
        draft_ref[layout.corner : layout.corner + levels] = zonal
        draft_ref[layout.bottom : layout.rows] = jnp.broadcast_to(
            bottom[row : row + 1], (layout.rows - layout.bottom, LANES)
        )


def complete_kernel(
    levels,
    west_ref,
    east_ref,
    top_draft_ref,
    bot_draft_ref,
    first_ref,
    second_ref,
    edge_ref,
    column_ref,
    top_ref,
    bot_ref,
):
    layout = Layout(levels)
    low_half = lax.axis_index("lon") < lax.axis_size("lon") // 2
    top_ref[...] = top_draft_ref[...]
    bot_ref[...] = bot_draft_ref[...]
    edge_ref[...] = jnp.zeros_like(edge_ref)
    edge_ref[0:ROWS] = west_ref[...].astype(jnp.float32)
    edge_ref[ROWS : 2 * ROWS] = east_ref[...].astype(jnp.float32)
    column_ref[...] = jnp.transpose(edge_ref[...])
    lane = lanes_of((levels, LANES))

    def pair(start, row):
        block = column_ref[start : start + levels]
        return block[:, row : row + 1], block[:, ROWS + row : ROWS + row + 1]

    for row, draft_ref in ((ROWS - 1, top_ref), (0, bot_ref)):
        zonal = draft_ref[layout.corner : layout.corner + levels]
        zonal_west, _ = pair(EDGE_STATE[0] + 2 * levels, row)
        merid_west, merid_east = pair(EDGE_STATE[0] + 3 * levels, row)
        east_factor = ADVECT_HALF * zonal + DIFFUSE
        west_factor = ADVECT_HALF * zonal_west - DIFFUSE
        corner = jnp.where((lane == 32) | (lane == 96), merid_west, 0.0)
        corner = jnp.where((lane == 31) | (lane == 95), merid_east, corner)
        for tracer in range(2):
            west, east = pair(EDGE_MASKED + tracer * levels, row)
            at_masked = layout.masked + tracer * levels
            at_part = layout.part + tracer * levels
            masked = draft_ref[at_masked : at_masked + levels]
            face = jnp.where(lane == LANES - 1, east_factor * (east - masked), 0.0)
            face = jnp.where(lane == 0, west_factor * (masked - west), face)
            draft_ref[at_part : at_part + levels] = draft_ref[at_part : at_part + levels] + face
            corner = jnp.where(lane == (0, LANES // 2)[tracer], west, corner)
            corner = jnp.where(lane == (LANES - 1, LANES // 2 - 1)[tracer], east, corner)
        draft_ref[layout.corner : layout.corner + levels] = corner

    @pl.when(low_half)
    def _():
        first_ref[...] = top_ref[...].astype(jnp.bfloat16)
        second_ref[...] = bot_ref[...].astype(jnp.bfloat16)

    @pl.when(jnp.logical_not(low_half))
    def _():
        first_ref[...] = bot_ref[...].astype(jnp.bfloat16)
        second_ref[...] = top_ref[...].astype(jnp.bfloat16)


def steps_kernel(
    first_ref,
    second_ref,
    west_ref,
    east_ref,
    state_ref,
    masked_ref,
    base_ref,
    kappa_ref,
    bottom_ref,
    adjoint_ref,
    velocity_ref,
    north_ref,
    south_ref,
    corner_ref,
    next_ref,
    side_ref,
    ring_ref,
):
    levels = masked_ref.shape[0] // (2 * ROWS)
    layout = Layout(levels)
    band = lax.axis_index("lat")
    low_half = lax.axis_index("lon") < lax.axis_size("lon") // 2
    top_band = (band == lax.axis_size("lat") - 1).astype(jnp.int32)
    folded = top_band.astype(jnp.float32)
    square = (LANES, LANES)
    from_lane = rows_of(square)
    turned = from_lane + top_band * (LANES - 1 - 2 * from_lane)
    turn = jnp.where(lanes_of(square) == turned, 1.0, 0.0).astype(jnp.bfloat16)

    @pl.when(low_half)
    def _():
        north_ref[...] = jnp.dot(second_ref[...], turn, preferred_element_type=jnp.float32)
        south_ref[...] = first_ref[...].astype(jnp.float32)

    @pl.when(jnp.logical_not(low_half))
    def _():
        north_ref[...] = jnp.dot(first_ref[...], turn, preferred_element_type=jnp.float32)
        south_ref[...] = second_ref[...].astype(jnp.float32)

    for at in range(2):
        here = slice(layout.merid[at], layout.merid[at] + levels)
        north_ref[here] = north_ref[here] * folded
    for side, (ref, scale) in enumerate(((north_ref, folded), (south_ref, None))):
        packed = ref[layout.corner : layout.corner + levels]
        merid = shift(packed, 96, 1)
        merid = merid if scale is None else merid * scale
        for item, block in enumerate((packed, shift(packed, LANES // 2, 1), merid)):
            begin = (side * 3 + item) * levels
            corner_ref[begin : begin + levels] = block

    tile_shape = (ROWS, LANES)
    lane = lanes_of(tile_shape)
    row = rows_of(tile_shape)
    first_lane, last_lane = lane == 0, lane == LANES - 1
    bottom_row, top_row = row == 0, row == ROWS - 1
    closed = (band == 0).astype(jnp.int32)
    open_south = jnp.where(row >= closed, DIFFUSE, 0.0)
    bottom = bottom_ref[...]

    def spread(ref, index):
        return jnp.broadcast_to(ref[:, index : index + 1].astype(jnp.float32), tile_shape)

    def line(ref, index):
        return jnp.broadcast_to(ref[index : index + 1], tile_shape)

    def tile_of(ref, index):
        return ref[index * ROWS : (index + 1) * ROWS]

    side_bottom = jnp.where(
        first_lane,
        spread(west_ref, EDGE_MASKED + 2 * levels),
        spread(east_ref, EDGE_MASKED + 2 * levels),
    )

    def factors(at, level):
        begin = at * FIELDS * levels
        zonal = tile_of(state_ref, begin + 2 * levels + level)
        merid = tile_of(state_ref, begin + 3 * levels + level)
        zonal_west = jnp.where(
            first_lane,
            spread(west_ref, EDGE_STATE[at] + 2 * levels + level),
            shift(zonal, 1, 1),
        )
        merid_south = jnp.where(
            bottom_row, line(south_ref, layout.merid[at] + level), shift(merid, 1, 0)
        )
        merid_net = merid - jnp.where(top_row, line(north_ref, layout.merid[at] + level), 0.0)
        return (
            ADVECT_HALF * zonal,
            ADVECT_HALF * zonal_west,
            ADVECT_HALF * merid_net + DIFFUSE,
            ADVECT_HALF * merid_south - open_south,
        )

    def gradients(at, level, tracer, east, north):
        field = tile_of(state_ref, (at * FIELDS + tracer) * levels + level)
        field_east = jnp.where(
            last_lane,
            spread(east_ref, EDGE_STATE[at] + tracer * levels + level),
            shift(field, -1, 1),
        )
        field_north = jnp.where(
            top_row, line(north_ref, layout.tracer[at] + tracer * levels + level), shift(field, -1, 0)
        )
        return (field + field_east) * east, (field + field_north) * north

    level_of = rows_of((levels, LANES))
    for tracer in range(2):
        start = tracer * levels * ROWS
        at_masked = slice(layout.masked + tracer * levels, layout.masked + (tracer + 1) * levels)
        at_part = slice(layout.part + tracer * levels, layout.part + (tracer + 1) * levels)
        at_merid = slice(layout.merid[0], layout.merid[0] + levels)
        merid = strided(state_ref, 3 * levels * ROWS + ROWS - 1, levels)
        masked = strided(masked_ref, start + ROWS - 1, levels)
        face = (ADVECT_HALF * (north_ref[at_merid] - merid) + DIFFUSE) * (
            masked - north_ref[at_masked]
        )
        wet = level_of.astype(jnp.float32) < north_ref[layout.bottom : layout.bottom + 1]
        ring_ref[tracer * levels : (tracer + 1) * levels] = jnp.where(
            wet, north_ref[at_part] + face, 0.0
        )
        masked = strided(masked_ref, start, levels)
        face = (ADVECT_HALF * south_ref[at_merid] + DIFFUSE) * (masked - south_ref[at_masked])
        wet = level_of.astype(jnp.float32) < south_ref[layout.bottom : layout.bottom + 1]
        ring_ref[(2 + tracer) * levels : (3 + tracer) * levels] = jnp.where(
            wet, south_ref[at_part] + face, 0.0
        )

    for level in range(levels):
        zonal, zonal_west, north_factor, south_factor = factors(0, level)
        side_merid = jnp.where(
            first_lane,
            spread(west_ref, EDGE_STATE[0] + 3 * levels + level),
            spread(east_ref, EDGE_STATE[0] + 3 * levels + level),
        )
        side_north = side_merid - jnp.where(top_row, line(corner_ref, 2 * levels + level), 0.0)
        side_south = jnp.where(bottom_row, line(corner_ref, 5 * levels + level), shift(side_merid, 1, 0))
        side_north = ADVECT_HALF * side_north + DIFFUSE
        side_south = ADVECT_HALF * side_south - open_south
        zonal_total = jnp.zeros(tile_shape, jnp.float32)
        merid_total = jnp.zeros(tile_shape, jnp.float32)
        for tracer in range(2):
            index = tracer * levels + level
            masked = tile_of(masked_ref, index)
            west = spread(west_ref, EDGE_MASKED + index)
            east = spread(east_ref, EDGE_MASKED + index)
            side = jnp.where(first_lane, west, east)
            to_east = jnp.where(last_lane, east, shift(masked, -1, 1)) - masked
            to_west = masked - jnp.where(first_lane, west, shift(masked, 1, 1))
            to_north = (
                jnp.where(top_row, line(north_ref, layout.masked + index), shift(masked, -1, 0))
                - masked
            )
            to_south = masked - jnp.where(
                bottom_row, line(south_ref, layout.masked + index), shift(masked, 1, 0)
            )
            result = (
                tile_of(base_ref, index)
                + (zonal + DIFFUSE) * to_east
                + (zonal_west - DIFFUSE) * to_west
                + north_factor * to_north
                + south_factor * to_south
            )
            next_ref[index * ROWS : (index + 1) * ROWS] = jnp.where(level < bottom, result, 0.0)
            zonal_grad, merid_grad = gradients(0, level, tracer, to_east, to_north)
            zonal_total = zonal_total + zonal_grad
            merid_total = merid_total + merid_grad
            face = jnp.where(
                first_lane,
                (zonal_west + DIFFUSE) * (masked - side),
                (zonal - DIFFUSE) * (side - masked),
            )
            part = jnp.where(
                first_lane, spread(west_ref, EDGE_PART + index), spread(east_ref, EDGE_PART + index)
            )
            upper = jnp.where(top_row, line(corner_ref, index), shift(side, -1, 0)) - side
            lower = side - jnp.where(
                bottom_row, line(corner_ref, 3 * levels + index), shift(side, 1, 0)
            )
            result = part + face + side_north * upper + side_south * lower
            side_ref[index * ROWS : (index + 1) * ROWS] = jnp.where(
                side_bottom > level, result, 0.0
            )
        velocity_ref[level * ROWS : (level + 1) * ROWS] = ADVECT_HALF * zonal_total
        velocity_ref[(levels + level) * ROWS : (levels + level + 1) * ROWS] = (
            ADVECT_HALF * merid_total
        )

    for level in range(levels):
        zonal, zonal_west, north_factor, south_factor = factors(1, level)
        zonal_total = jnp.zeros(tile_shape, jnp.float32)
        merid_total = jnp.zeros(tile_shape, jnp.float32)
        for tracer in range(2):
            index = tracer * levels + level
            masked = tile_of(next_ref, index)
            side = tile_of(side_ref, index)
            to_east = jnp.where(last_lane, side, shift(masked, -1, 1)) - masked
            to_west = masked - jnp.where(first_lane, side, shift(masked, 1, 1))
            to_north = jnp.where(top_row, line(ring_ref, index), shift(masked, -1, 0)) - masked
            to_south = masked - jnp.where(
                bottom_row, line(ring_ref, 2 * levels + index), shift(masked, 1, 0)
            )
            adjoint_ref[index * ROWS : (index + 1) * ROWS] = (
                mixed(next_ref, kappa_ref, tracer * levels * ROWS, level, levels)
                + (zonal + DIFFUSE) * to_east
                + (zonal_west - DIFFUSE) * to_west
                + north_factor * to_north
                + south_factor * to_south
            )
            zonal_grad, merid_grad = gradients(1, level, tracer, to_east, to_north)
            zonal_total = zonal_total + zonal_grad
            merid_total = merid_total + merid_grad
        for total, begin in ((zonal_total, 0), (merid_total, levels)):
            here = slice((begin + level) * ROWS, (begin + level + 1) * ROWS)
            velocity_ref[here] = velocity_ref[here] + ADVECT_HALF * total


def line_routes(tiles, bands):
    def at(tile, band):
        return tile * bands + band

    upward = []
    for tile in range(tiles // 2):
        mirror = tiles - 1 - tile
        for band in range(bands - 1):
            upward.append((at(tile, band), at(tile, band + 1)))
            upward.append((at(mirror, band + 1), at(mirror, band)))
        upward.append((at(tile, bands - 1), at(mirror, bands - 1)))
    return upward, [(target, source) for source, target in upward]


def call(kernel, outputs, scratch, scalars, arrays):
    vmem = pl.BlockSpec(memory_space=pltpu.VMEM)
    smem = pl.BlockSpec(memory_space=pltpu.SMEM)
    return pl.pallas_call(
        kernel,
        out_shape=[jax.ShapeDtypeStruct(shape, dtype) for shape, dtype in outputs],
        in_specs=[smem] * len(scalars) + [vmem] * len(arrays),
        out_specs=[vmem] * len(outputs),
        scratch_shapes=[pltpu.VMEM(shape, jnp.float32) for shape in scratch],
        compiler_params=pltpu.CompilerParams(vmem_limit_bytes=32 * 1024 * 1024),
    )(*scalars, *arrays)


def shards(final_adjoint, store, holder_offset, holder_slot, bottom_level, mix_class, mix_table):
    bands = lax.axis_size("lat")
    tiles = lax.axis_size("lon")
    levels = final_adjoint.shape[1]
    slots = store.shape[2]
    steps = len(STEP_ORDER)
    pieces = FIELDS * levels
    full = levels * ROWS
    layout = Layout(levels)
    narrow, wide = jnp.bfloat16, jnp.float32
    (request,) = call(
        request_kernel,
        [((bands, steps, pieces, LANES), narrow)],
        [(pieces * slots, LANES)],
        [holder_slot],
        [store.reshape(pieces * slots, LANES)],
    )
    received = lax.all_to_all(request, "lat", split_axis=0, concat_axis=0, tiled=True)
    masked, base, kappa = call(
        prepare_kernel,
        [((2 * full, LANES), wide), ((2 * full, LANES), wide), ((full + ROWS, LANES), wide)],
        [],
        [mix_table],
        [
            final_adjoint.reshape(2 * full, LANES),
            bottom_level,
            mix_class.reshape((levels - 1) * ROWS, LANES),
        ],
    )
    state, to_west, to_east, top, bot = call(
        edges_kernel,
        [
            ((steps * FIELDS * full, LANES), wide),
            ((ROWS, EDGE_LANES), narrow),
            ((ROWS, EDGE_LANES), narrow),
            ((layout.rows, LANES), wide),
            ((layout.rows, LANES), wide),
        ],
        [(2 * full, LANES), (EDGE_LANES, LANES)],
        [holder_offset],
        [received, masked, base, bottom_level],
    )
    eastward = [(tile, (tile + 1) % tiles) for tile in range(tiles)]
    westward = [(target, source) for source, target in eastward]
    west = lax.ppermute(to_east, "lon", eastward)
    east = lax.ppermute(to_west, "lon", westward)
    first, second = call(
        functools.partial(complete_kernel, levels),
        [((layout.rows, LANES), narrow), ((layout.rows, LANES), narrow)],
        [(LANES, EDGE_LANES), (EDGE_LANES, LANES), (layout.rows, LANES), (layout.rows, LANES)],
        [],
        [west, east, top, bot],
    )
    upward, downward = line_routes(tiles, bands)
    first = lax.ppermute(first, ("lon", "lat"), upward)
    second = lax.ppermute(second, ("lon", "lat"), downward)
    adjoint, velocity = call(
        steps_kernel,
        [((2 * full, LANES), wide), ((2 * full, LANES), wide)],
        [
            (layout.rows, LANES),
            (layout.rows, LANES),
            (6 * levels, LANES),
            (2 * full, LANES),
            (2 * full, LANES),
            (4 * levels, LANES),
        ],
        [],
        [first, second, west, east, state, masked, base, kappa, bottom_level],
    )
    shape = (2, levels, ROWS, LANES)
    return adjoint.reshape(shape), velocity.reshape(shape)


def solution(mesh):
    return jax.shard_map(
        shards,
        mesh=mesh,
        in_specs=(
            P(None, None, "lat", "lon"),
            P(None, None, None, "lat", "lon"),
            P(),
            P(),
            P("lat", "lon"),
            P(None, "lat", "lon"),
            P(),
        ),
        out_specs=(P(None, None, "lat", "lon"), P(None, None, "lat", "lon")),
        check_vma=False,
    )
```

```python
import functools

import jax
import jax.numpy as jnp
from jax import lax
from jax.experimental import pallas as pl
from jax.experimental.pallas import tpu as pltpu
from jax.sharding import PartitionSpec as P

STEP_ORDER = (1, 0)
FIELDS = 4
ADVECT_HALF = 0.125
DIFFUSE = 0.1

ROWS = 8
LANES = 128

EDGE_STATE = (0, 256)
EDGE_MASKED = 512
EDGE_PART = 640
EDGE_LANES = 768


class Layout:
    def __init__(self, levels):
        self.tracer = (0, 3 * levels)
        self.merid = (2 * levels, 5 * levels)
        self.masked = 6 * levels
        self.part = 8 * levels
        self.corner = 10 * levels
        self.bottom = 11 * levels
        self.rows = (11 * levels + 1 + 15) // 16 * 16


def shift(block, amount, axis):
    return pltpu.roll(block, amount % block.shape[axis], axis)


def lanes_of(shape):
    return lax.broadcasted_iota(jnp.int32, shape, 1)


def rows_of(shape):
    return lax.broadcasted_iota(jnp.int32, shape, 0)


def strided(ref, start, count):
    return ref[pl.ds(start, count, stride=ROWS), :]


def request_kernel(slot_ref, store_ref, out_ref, wide_ref):
    tile = lax.axis_index("lon")
    bands, steps, pieces, lanes = out_ref.shape
    slots = store_ref.shape[0] // pieces
    wide_ref[...] = store_ref[...].astype(jnp.float32)
    for band in range(bands):
        for at, step in enumerate(STEP_ORDER):
            slot = slot_ref[step, band, tile]
            rows = wide_ref[pl.ds(slot, pieces, stride=slots), :]
            out_ref[band, at] = rows.astype(jnp.bfloat16)


def prepare_kernel(table_ref, adjoint_ref, bottom_ref, mix_ref, masked_ref, base_ref, kappa_ref):
    levels = adjoint_ref.shape[0] // (2 * ROWS)
    bottom = bottom_ref[...]
    edge = jnp.zeros((ROWS, LANES), jnp.float32)
    kappa_ref[0:ROWS] = edge
    kappa_ref[levels * ROWS : (levels + 1) * ROWS] = edge
    for level in range(levels - 1):
        classes = mix_ref[level * ROWS : (level + 1) * ROWS]
        kappa = jnp.full((ROWS, LANES), table_ref[0], jnp.float32)
        for index in range(1, table_ref.shape[0]):
            kappa = jnp.where(classes == index, table_ref[index], kappa)
        kappa_ref[(level + 1) * ROWS : (level + 2) * ROWS] = kappa
    for tracer in range(2):
        start = tracer * levels * ROWS
        for level in range(levels):
            here = slice(start + level * ROWS, start + (level + 1) * ROWS)
            masked_ref[here] = jnp.where(level < bottom, adjoint_ref[here], 0.0)
        for level in range(levels):
            base_ref[start + level * ROWS : start + (level + 1) * ROWS] = mixed(
                masked_ref, kappa_ref, start, level, levels
            )


def mixed(masked_ref, kappa_ref, start, level, levels):
    def at(index):
        return masked_ref[start + index * ROWS : start + (index + 1) * ROWS]

    masked = at(level)
    below = at(level + 1) if level + 1 < levels else jnp.zeros_like(masked)
    above = at(level - 1) if level > 0 else jnp.zeros_like(masked)
    kappa_above = kappa_ref[level * ROWS : (level + 1) * ROWS]
    kappa_below = kappa_ref[(level + 1) * ROWS : (level + 2) * ROWS]
    return masked + kappa_below * (below - masked) + kappa_above * (above - masked)


def edges_kernel(
    offset_ref,
    piece_ref,
    masked_ref,
    base_ref,
    bottom_ref,
    state_ref,
    inner_ref,
    outer_ref,
    top_ref,
    bot_ref,
    part_ref,
    column_ref,
):
    tile = lax.axis_index("lon")
    band = lax.axis_index("lat")
    levels = masked_ref.shape[0] // (2 * ROWS)
    pieces = FIELDS * levels
    holders = piece_ref.shape[0]
    lane = lanes_of((ROWS, LANES))
    sources = []
    for at, step in enumerate(STEP_ORDER):
        offset = offset_ref[step, band, tile]
        chunks = []
        for row in range(ROWS):
            chunk = piece_ref[lax.rem(row + offset, holders), at]
            state_ref[pl.ds(at * pieces * ROWS + row, pieces, stride=ROWS), :] = chunk.astype(
                jnp.float32
            )
            chunks.append(chunk)
        sources.append((EDGE_STATE[at], jnp.concatenate(chunks, axis=1)))
    for level in range(levels):
        zonal = state_ref[(2 * levels + level) * ROWS : (2 * levels + level + 1) * ROWS]
        east_factor = ADVECT_HALF * zonal + DIFFUSE
        west_factor = ADVECT_HALF * shift(zonal, 1, 1) - DIFFUSE
        for tracer in range(2):
            here = slice((tracer * levels + level) * ROWS, (tracer * levels + level + 1) * ROWS)
            masked = masked_ref[here]
            face = jnp.where(
                lane < LANES // 2,
                east_factor * (shift(masked, -1, 1) - masked),
                west_factor * (masked - shift(masked, 1, 1)),
            )
            part_ref[here] = base_ref[here] + face
    for start, ref in ((EDGE_MASKED, masked_ref), (EDGE_PART, part_ref)):
        columns = [strided(ref, row, 2 * levels).astype(jnp.bfloat16) for row in range(ROWS)]
        sources.append((start, jnp.concatenate(columns, axis=1)))
    place = (ROWS * LANES, LANES)
    from_row, from_lane = rows_of(place) // LANES, rows_of(place) % LANES
    chosen = ((from_lane == 0) & (lanes_of(place) == from_row)) | (
        (from_lane == LANES - 1) & (lanes_of(place) == from_row + ROWS)
    )
    pick = jnp.where(chosen, 1.0, 0.0).astype(jnp.bfloat16)
    column_ref[...] = jnp.zeros_like(column_ref)
    for start, source in sources:
        column_ref[start : start + source.shape[0]] = jnp.dot(
            source, pick, preferred_element_type=jnp.float32
        )
    edge = jnp.transpose(column_ref[...])
    bottom = bottom_ref[...].astype(jnp.float32)
    spot = lanes_of((ROWS, EDGE_LANES)) == EDGE_MASKED + 2 * levels
    to_west = jnp.where(spot, bottom[:, 0:1], edge[0:ROWS]).astype(jnp.bfloat16)
    to_east = jnp.where(spot, bottom[:, LANES - 1 :], edge[ROWS : 2 * ROWS]).astype(jnp.bfloat16)

    @pl.when(lax.rem(tile, 2) == 0)
    def _():
        inner_ref[...] = to_east
        outer_ref[...] = to_west

    @pl.when(lax.rem(tile, 2) == 1)
    def _():
        inner_ref[...] = to_west
        outer_ref[...] = to_east

    layout = Layout(levels)
    wide = lanes_of((levels, LANES))
    for row, inner, draft_ref in ((ROWS - 1, ROWS - 2, top_ref), (0, 1, bot_ref)):
        for at in range(2):
            begin = at * pieces * ROWS
            draft_ref[layout.tracer[at] : layout.tracer[at] + 2 * levels] = strided(
                state_ref, begin + row, 2 * levels
            )
            draft_ref[layout.merid[at] : layout.merid[at] + levels] = strided(
                state_ref, begin + 3 * levels * ROWS + row, levels
            )
        zonal = strided(state_ref, 2 * levels * ROWS + row, levels)
        merid = strided(state_ref, 3 * levels * ROWS + min(row, inner), levels)
        east_factor = ADVECT_HALF * zonal + DIFFUSE
        west_factor = ADVECT_HALF * shift(zonal, 1, 1) - DIFFUSE
        for tracer in range(2):
            begin = tracer * levels * ROWS
            masked = strided(masked_ref, begin + row, levels)
            next_row = strided(masked_ref, begin + inner, levels)
            if row > inner:
                along = (ADVECT_HALF * merid - DIFFUSE) * (masked - next_row)
            else:
                along = (ADVECT_HALF * merid + DIFFUSE) * (next_row - masked)
            east = east_factor * (shift(masked, -1, 1) - masked)
            west = west_factor * (masked - shift(masked, 1, 1))
            part = strided(base_ref, begin + row, levels) + along
            part = part + jnp.where(wide < LANES - 1, east, 0.0) + jnp.where(wide > 0, west, 0.0)
            at_masked = layout.masked + tracer * levels
            at_part = layout.part + tracer * levels
            draft_ref[at_masked : at_masked + levels] = masked
            draft_ref[at_part : at_part + levels] = part
        draft_ref[layout.corner : layout.corner + levels] = zonal
        draft_ref[layout.bottom : layout.rows] = jnp.broadcast_to(
            bottom[row : row + 1], (layout.rows - layout.bottom, LANES)
        )


def complete_kernel(
    levels,
    inner_ref,
    outer_ref,
    top_draft_ref,
    bot_draft_ref,
    near_ref,
    far_ref,
    west_ref,
    east_ref,
    edge_ref,
    column_ref,
    top_ref,
    bot_ref,
):
    layout = Layout(levels)
    odd_tile = lax.rem(lax.axis_index("lon"), 2) == 1
    odd_band = lax.rem(lax.axis_index("lat"), 2) == 1

    @pl.when(odd_tile)
    def _():
        west_ref[...] = inner_ref[...]
        east_ref[...] = outer_ref[...]

    @pl.when(jnp.logical_not(odd_tile))
    def _():
        west_ref[...] = outer_ref[...]
        east_ref[...] = inner_ref[...]

    top_ref[...] = top_draft_ref[...]
    bot_ref[...] = bot_draft_ref[...]
    edge_ref[...] = jnp.zeros_like(edge_ref)
    edge_ref[0:ROWS] = west_ref[...].astype(jnp.float32)
    edge_ref[ROWS : 2 * ROWS] = east_ref[...].astype(jnp.float32)
    column_ref[...] = jnp.transpose(edge_ref[...])
    lane = lanes_of((levels, LANES))

    def pair(start, row):
        block = column_ref[start : start + levels]
        return block[:, row : row + 1], block[:, ROWS + row : ROWS + row + 1]

    for row, draft_ref in ((ROWS - 1, top_ref), (0, bot_ref)):
        zonal = draft_ref[layout.corner : layout.corner + levels]
        zonal_west, _ = pair(EDGE_STATE[0] + 2 * levels, row)
        merid_west, merid_east = pair(EDGE_STATE[0] + 3 * levels, row)
        east_factor = ADVECT_HALF * zonal + DIFFUSE
        west_factor = ADVECT_HALF * zonal_west - DIFFUSE
        corner = jnp.where((lane == 32) | (lane == 96), merid_west, 0.0)
        corner = jnp.where((lane == 31) | (lane == 95), merid_east, corner)
        for tracer in range(2):
            west, east = pair(EDGE_MASKED + tracer * levels, row)
            at_masked = layout.masked + tracer * levels
            at_part = layout.part + tracer * levels
            masked = draft_ref[at_masked : at_masked + levels]
            face = jnp.where(lane == LANES - 1, east_factor * (east - masked), 0.0)
            face = jnp.where(lane == 0, west_factor * (masked - west), face)
            draft_ref[at_part : at_part + levels] = draft_ref[at_part : at_part + levels] + face
            corner = jnp.where(lane == (0, LANES // 2)[tracer], west, corner)
            corner = jnp.where(lane == (LANES - 1, LANES // 2 - 1)[tracer], east, corner)
        draft_ref[layout.corner : layout.corner + levels] = corner

    @pl.when(odd_band)
    def _():
        near_ref[...] = bot_ref[...].astype(jnp.bfloat16)
        far_ref[...] = top_ref[...].astype(jnp.bfloat16)

    @pl.when(jnp.logical_not(odd_band))
    def _():
        near_ref[...] = top_ref[...].astype(jnp.bfloat16)
        far_ref[...] = bot_ref[...].astype(jnp.bfloat16)


def steps_kernel(
    near_ref,
    far_ref,
    west_ref,
    east_ref,
    state_ref,
    masked_ref,
    base_ref,
    kappa_ref,
    bottom_ref,
    adjoint_ref,
    velocity_ref,
    north_ref,
    south_ref,
    corner_ref,
    next_ref,
    side_ref,
    ring_ref,
):
    levels = masked_ref.shape[0] // (2 * ROWS)
    layout = Layout(levels)
    band = lax.axis_index("lat")
    odd_band = lax.rem(band, 2) == 1
    top_band = (band == lax.axis_size("lat") - 1).astype(jnp.int32)
    folded = top_band.astype(jnp.float32)
    square = (LANES, LANES)
    from_lane = rows_of(square)
    turned = from_lane + top_band * (LANES - 1 - 2 * from_lane)
    turn = jnp.where(lanes_of(square) == turned, 1.0, 0.0).astype(jnp.bfloat16)

    @pl.when(odd_band)
    def _():
        north_ref[...] = jnp.dot(far_ref[...], turn, preferred_element_type=jnp.float32)
        south_ref[...] = near_ref[...].astype(jnp.float32)

    @pl.when(jnp.logical_not(odd_band))
    def _():
        north_ref[...] = jnp.dot(near_ref[...], turn, preferred_element_type=jnp.float32)
        south_ref[...] = far_ref[...].astype(jnp.float32)

    for at in range(2):
        here = slice(layout.merid[at], layout.merid[at] + levels)
        north_ref[here] = north_ref[here] * folded
    for side, (ref, scale) in enumerate(((north_ref, folded), (south_ref, None))):
        packed = ref[layout.corner : layout.corner + levels]
        merid = shift(packed, 96, 1)
        merid = merid if scale is None else merid * scale
        for item, block in enumerate((packed, shift(packed, LANES // 2, 1), merid)):
            begin = (side * 3 + item) * levels
            corner_ref[begin : begin + levels] = block

    tile_shape = (ROWS, LANES)
    lane = lanes_of(tile_shape)
    row = rows_of(tile_shape)
    first_lane, last_lane = lane == 0, lane == LANES - 1
    bottom_row, top_row = row == 0, row == ROWS - 1
    closed = (band == 0).astype(jnp.int32)
    open_south = jnp.where(row >= closed, DIFFUSE, 0.0)
    bottom = bottom_ref[...]

    def spread(ref, index):
        return jnp.broadcast_to(ref[:, index : index + 1].astype(jnp.float32), tile_shape)

    def line(ref, index):
        return jnp.broadcast_to(ref[index : index + 1], tile_shape)

    def tile_of(ref, index):
        return ref[index * ROWS : (index + 1) * ROWS]

    side_bottom = jnp.where(
        first_lane,
        spread(west_ref, EDGE_MASKED + 2 * levels),
        spread(east_ref, EDGE_MASKED + 2 * levels),
    )

    def factors(at, level):
        begin = at * FIELDS * levels
        zonal = tile_of(state_ref, begin + 2 * levels + level)
        merid = tile_of(state_ref, begin + 3 * levels + level)
        zonal_west = jnp.where(
            first_lane,
            spread(west_ref, EDGE_STATE[at] + 2 * levels + level),
            shift(zonal, 1, 1),
        )
        merid_south = jnp.where(
            bottom_row, line(south_ref, layout.merid[at] + level), shift(merid, 1, 0)
        )
        merid_net = merid - jnp.where(top_row, line(north_ref, layout.merid[at] + level), 0.0)
        return (
            ADVECT_HALF * zonal,
            ADVECT_HALF * zonal_west,
            ADVECT_HALF * merid_net + DIFFUSE,
            ADVECT_HALF * merid_south - open_south,
        )

    def gradients(at, level, tracer, east, north):
        field = tile_of(state_ref, (at * FIELDS + tracer) * levels + level)
        field_east = jnp.where(
            last_lane,
            spread(east_ref, EDGE_STATE[at] + tracer * levels + level),
            shift(field, -1, 1),
        )
        field_north = jnp.where(
            top_row, line(north_ref, layout.tracer[at] + tracer * levels + level), shift(field, -1, 0)
        )
        return (field + field_east) * east, (field + field_north) * north

    level_of = rows_of((levels, LANES))
    for tracer in range(2):
        start = tracer * levels * ROWS
        at_masked = slice(layout.masked + tracer * levels, layout.masked + (tracer + 1) * levels)
        at_part = slice(layout.part + tracer * levels, layout.part + (tracer + 1) * levels)
        at_merid = slice(layout.merid[0], layout.merid[0] + levels)
        merid = strided(state_ref, 3 * levels * ROWS + ROWS - 1, levels)
        masked = strided(masked_ref, start + ROWS - 1, levels)
        face = (ADVECT_HALF * (north_ref[at_merid] - merid) + DIFFUSE) * (
            masked - north_ref[at_masked]
        )
        wet = level_of.astype(jnp.float32) < north_ref[layout.bottom : layout.bottom + 1]
        ring_ref[tracer * levels : (tracer + 1) * levels] = jnp.where(
            wet, north_ref[at_part] + face, 0.0
        )
        masked = strided(masked_ref, start, levels)
        face = (ADVECT_HALF * south_ref[at_merid] + DIFFUSE) * (masked - south_ref[at_masked])
        wet = level_of.astype(jnp.float32) < south_ref[layout.bottom : layout.bottom + 1]
        ring_ref[(2 + tracer) * levels : (3 + tracer) * levels] = jnp.where(
            wet, south_ref[at_part] + face, 0.0
        )

    for level in range(levels):
        zonal, zonal_west, north_factor, south_factor = factors(0, level)
        side_merid = jnp.where(
            first_lane,
            spread(west_ref, EDGE_STATE[0] + 3 * levels + level),
            spread(east_ref, EDGE_STATE[0] + 3 * levels + level),
        )
        side_north = side_merid - jnp.where(top_row, line(corner_ref, 2 * levels + level), 0.0)
        side_south = jnp.where(bottom_row, line(corner_ref, 5 * levels + level), shift(side_merid, 1, 0))
        side_north = ADVECT_HALF * side_north + DIFFUSE
        side_south = ADVECT_HALF * side_south - open_south
        zonal_total = jnp.zeros(tile_shape, jnp.float32)
        merid_total = jnp.zeros(tile_shape, jnp.float32)
        for tracer in range(2):
            index = tracer * levels + level
            masked = tile_of(masked_ref, index)
            west = spread(west_ref, EDGE_MASKED + index)
            east = spread(east_ref, EDGE_MASKED + index)
            side = jnp.where(first_lane, west, east)
            to_east = jnp.where(last_lane, east, shift(masked, -1, 1)) - masked
            to_west = masked - jnp.where(first_lane, west, shift(masked, 1, 1))
            to_north = (
                jnp.where(top_row, line(north_ref, layout.masked + index), shift(masked, -1, 0))
                - masked
            )
            to_south = masked - jnp.where(
                bottom_row, line(south_ref, layout.masked + index), shift(masked, 1, 0)
            )
            result = (
                tile_of(base_ref, index)
                + (zonal + DIFFUSE) * to_east
                + (zonal_west - DIFFUSE) * to_west
                + north_factor * to_north
                + south_factor * to_south
            )
            next_ref[index * ROWS : (index + 1) * ROWS] = jnp.where(level < bottom, result, 0.0)
            zonal_grad, merid_grad = gradients(0, level, tracer, to_east, to_north)
            zonal_total = zonal_total + zonal_grad
            merid_total = merid_total + merid_grad
            face = jnp.where(
                first_lane,
                (zonal_west + DIFFUSE) * (masked - side),
                (zonal - DIFFUSE) * (side - masked),
            )
            part = jnp.where(
                first_lane, spread(west_ref, EDGE_PART + index), spread(east_ref, EDGE_PART + index)
            )
            upper = jnp.where(top_row, line(corner_ref, index), shift(side, -1, 0)) - side
            lower = side - jnp.where(
                bottom_row, line(corner_ref, 3 * levels + index), shift(side, 1, 0)
            )
            result = part + face + side_north * upper + side_south * lower
            side_ref[index * ROWS : (index + 1) * ROWS] = jnp.where(
                side_bottom > level, result, 0.0
            )
        velocity_ref[level * ROWS : (level + 1) * ROWS] = ADVECT_HALF * zonal_total
        velocity_ref[(levels + level) * ROWS : (levels + level + 1) * ROWS] = (
            ADVECT_HALF * merid_total
        )

    for level in range(levels):
        zonal, zonal_west, north_factor, south_factor = factors(1, level)
        zonal_total = jnp.zeros(tile_shape, jnp.float32)
        merid_total = jnp.zeros(tile_shape, jnp.float32)
        for tracer in range(2):
            index = tracer * levels + level
            masked = tile_of(next_ref, index)
            side = tile_of(side_ref, index)
            to_east = jnp.where(last_lane, side, shift(masked, -1, 1)) - masked
            to_west = masked - jnp.where(first_lane, side, shift(masked, 1, 1))
            to_north = jnp.where(top_row, line(ring_ref, index), shift(masked, -1, 0)) - masked
            to_south = masked - jnp.where(
                bottom_row, line(ring_ref, 2 * levels + index), shift(masked, 1, 0)
            )
            adjoint_ref[index * ROWS : (index + 1) * ROWS] = (
                mixed(next_ref, kappa_ref, tracer * levels * ROWS, level, levels)
                + (zonal + DIFFUSE) * to_east
                + (zonal_west - DIFFUSE) * to_west
                + north_factor * to_north
                + south_factor * to_south
            )
            zonal_grad, merid_grad = gradients(1, level, tracer, to_east, to_north)
            zonal_total = zonal_total + zonal_grad
            merid_total = merid_total + merid_grad
        for total, begin in ((zonal_total, 0), (merid_total, levels)):
            here = slice((begin + level) * ROWS, (begin + level + 1) * ROWS)
            velocity_ref[here] = velocity_ref[here] + ADVECT_HALF * total


def swaps(pairs):
    return [pair for low, high in pairs for pair in ((low, high), (high, low))]


def ring_routes(tiles):
    inner = swaps((tile, tile + 1) for tile in range(0, tiles, 2))
    outer = swaps((tile, (tile + 1) % tiles) for tile in range(1, tiles, 2))
    return inner, outer


def line_routes(tiles, bands):
    near, far = [], []
    for tile in range(tiles):
        start = tile * bands
        near += [(start + band, start + band + 1) for band in range(0, bands, 2)]
        far += [(start + band, start + band + 1) for band in range(1, bands - 1, 2)]
        if tile < tiles // 2:
            far.append((start + bands - 1, (tiles - tile) * bands - 1))
    return swaps(near), swaps(far)


def call(kernel, outputs, scratch, scalars, arrays):
    vmem = pl.BlockSpec(memory_space=pltpu.VMEM)
    smem = pl.BlockSpec(memory_space=pltpu.SMEM)
    return pl.pallas_call(
        kernel,
        out_shape=[jax.ShapeDtypeStruct(shape, dtype) for shape, dtype in outputs],
        in_specs=[smem] * len(scalars) + [vmem] * len(arrays),
        out_specs=[vmem] * len(outputs),
        scratch_shapes=[pltpu.VMEM(shape, jnp.float32) for shape in scratch],
        compiler_params=pltpu.CompilerParams(vmem_limit_bytes=32 * 1024 * 1024),
    )(*scalars, *arrays)


def shards(final_adjoint, store, holder_offset, holder_slot, bottom_level, mix_class, mix_table):
    bands = lax.axis_size("lat")
    tiles = lax.axis_size("lon")
    levels = final_adjoint.shape[1]
    slots = store.shape[2]
    steps = len(STEP_ORDER)
    pieces = FIELDS * levels
    full = levels * ROWS
    layout = Layout(levels)
    narrow, wide = jnp.bfloat16, jnp.float32
    (request,) = call(
        request_kernel,
        [((bands, steps, pieces, LANES), narrow)],
        [(pieces * slots, LANES)],
        [holder_slot],
        [store.reshape(pieces * slots, LANES)],
    )
    received = lax.all_to_all(request, "lat", split_axis=0, concat_axis=0, tiled=True)
    masked, base, kappa = call(
        prepare_kernel,
        [((2 * full, LANES), wide), ((2 * full, LANES), wide), ((full + ROWS, LANES), wide)],
        [],
        [mix_table],
        [
            final_adjoint.reshape(2 * full, LANES),
            bottom_level,
            mix_class.reshape((levels - 1) * ROWS, LANES),
        ],
    )
    state, inner, outer, top, bot = call(
        edges_kernel,
        [
            ((steps * FIELDS * full, LANES), wide),
            ((ROWS, EDGE_LANES), narrow),
            ((ROWS, EDGE_LANES), narrow),
            ((layout.rows, LANES), wide),
            ((layout.rows, LANES), wide),
        ],
        [(2 * full, LANES), (EDGE_LANES, LANES)],
        [holder_offset],
        [received, masked, base, bottom_level],
    )
    inner_routes, outer_routes = ring_routes(tiles)
    near_routes, far_routes = line_routes(tiles, bands)
    inner = lax.ppermute(inner, "lon", inner_routes)
    outer = lax.ppermute(outer, "lon", outer_routes)
    near, far, west, east = call(
        functools.partial(complete_kernel, levels),
        [
            ((layout.rows, LANES), narrow),
            ((layout.rows, LANES), narrow),
            ((ROWS, EDGE_LANES), narrow),
            ((ROWS, EDGE_LANES), narrow),
        ],
        [(LANES, EDGE_LANES), (EDGE_LANES, LANES), (layout.rows, LANES), (layout.rows, LANES)],
        [],
        [inner, outer, top, bot],
    )
    near = lax.ppermute(near, ("lon", "lat"), near_routes)
    far = lax.ppermute(far, ("lon", "lat"), far_routes)
    adjoint, velocity = call(
        steps_kernel,
        [((2 * full, LANES), wide), ((2 * full, LANES), wide)],
        [
            (layout.rows, LANES),
            (layout.rows, LANES),
            (6 * levels, LANES),
            (2 * full, LANES),
            (2 * full, LANES),
            (4 * levels, LANES),
        ],
        [],
        [near, far, west, east, state, masked, base, kappa, bottom_level],
    )
    shape = (2, levels, ROWS, LANES)
    return adjoint.reshape(shape), velocity.reshape(shape)


def solution(mesh):
    return jax.shard_map(
        shards,
        mesh=mesh,
        in_specs=(
            P(None, None, "lat", "lon"),
            P(None, None, None, "lat", "lon"),
            P(),
            P(),
            P("lat", "lon"),
            P(None, "lat", "lon"),
            P(),
        ),
        out_specs=(P(None, None, "lat", "lon"), P(None, None, "lat", "lon")),
        check_vma=False,
    )
```

```python
import functools

import jax
import jax.numpy as jnp
from jax import lax
from jax.experimental import pallas as pl
from jax.experimental.pallas import tpu as pltpu
from jax.sharding import PartitionSpec as P

STEP_ORDER = (1, 0)
FIELDS = 4
ADVECT_HALF = 0.125
DIFFUSE = 0.1

ROWS = 8
LANES = 128

EDGE_STATE = (0, 256)
EDGE_MASKED = 512
EDGE_PART = 640
EDGE_LANES = 768


class Layout:
    def __init__(self, levels):
        self.tracer = (0, 3 * levels)
        self.merid = (2 * levels, 5 * levels)
        self.masked = 6 * levels
        self.part = 8 * levels
        self.corner = 10 * levels
        self.bottom = 11 * levels
        self.rows = (11 * levels + 1 + 15) // 16 * 16


def shift(block, amount, axis):
    return pltpu.roll(block, amount % block.shape[axis], axis)


def lanes_of(shape):
    return lax.broadcasted_iota(jnp.int32, shape, 1)


def rows_of(shape):
    return lax.broadcasted_iota(jnp.int32, shape, 0)


def strided(ref, start, count):
    return ref[pl.ds(start, count, stride=ROWS), :]


def request_kernel(slot_ref, store_ref, out_ref, wide_ref):
    tile = lax.axis_index("lon")
    bands, steps, pieces, lanes = out_ref.shape
    slots = store_ref.shape[0] // pieces
    wide_ref[...] = store_ref[...].astype(jnp.float32)
    for band in range(bands):
        for at, step in enumerate(STEP_ORDER):
            slot = slot_ref[step, band, tile]
            rows = wide_ref[pl.ds(slot, pieces, stride=slots), :]
            out_ref[band, at] = rows.astype(jnp.bfloat16)


def columns_kernel(
    slot_ref, store_ref, masked_ref, base_ref, bottom_ref, mail_ref, wide_ref, column_ref, row_ref
):
    tile = lax.axis_index("lon")
    odd = lax.rem(tile, 2)
    half, height, _ = mail_ref.shape
    half = half // 2
    slots = store_ref.shape[0] // (masked_ref.shape[0] // ROWS * 2)
    pieces = store_ref.shape[0] // slots
    rows = masked_ref.shape[0] // ROWS
    edge_lane = odd * (LANES - 1)
    next_lane = edge_lane + 1 - 2 * odd

    def picks(count):
        place = (count * LANES, LANES)
        source, lane = rows_of(place) // LANES, rows_of(place) % LANES
        chosen = ((lane == edge_lane) & (lanes_of(place) == source)) | (
            (lane == next_lane) & (lanes_of(place) == source + count)
        )
        return jnp.where(chosen, 1.0, 0.0).astype(jnp.bfloat16)

    wide_ref[...] = store_ref[...].astype(jnp.float32)
    column_ref[...] = jnp.zeros_like(column_ref)
    stored = [
        wide_ref[pl.ds(slot, pieces, stride=slots), :].astype(jnp.bfloat16) for slot in range(slots)
    ]
    column_ref[0:pieces] = jnp.dot(
        jnp.concatenate(stored, axis=1), picks(slots), preferred_element_type=jnp.float32
    )
    row_ref[...] = jnp.transpose(column_ref[...])
    column_ref[...] = jnp.zeros_like(column_ref)
    pick = picks(ROWS)
    for start, ref in ((0, masked_ref), (LANES, base_ref)):
        blocks = [strided(ref, row, rows).astype(jnp.bfloat16) for row in range(ROWS)]
        column_ref[start : start + rows] = jnp.dot(
            jnp.concatenate(blocks, axis=1), pick, preferred_element_type=jnp.float32
        )
    level_rows = jnp.transpose(column_ref[...])[0 : 2 * ROWS]
    bottom = bottom_ref[...].astype(jnp.float32)
    bottom = jnp.where(odd == 1, bottom[:, LANES - 1 :], bottom[:, 0:1])
    spot = (lanes_of(level_rows.shape) == rows) & (rows_of(level_rows.shape) < ROWS)
    bottom = jnp.concatenate([bottom, bottom], axis=0)
    level_rows = jnp.where(spot, bottom, level_rows)
    mail_ref[...] = jnp.zeros_like(mail_ref)
    blank = jnp.zeros((ROWS - 3, level_rows.shape[1]), jnp.float32)
    for band in range(half):
        state = []
        for step in STEP_ORDER:
            state.append(row_ref[pl.ds(slot_ref[step, band, tile], 1), :])
        state.append(row_ref[pl.ds(slots + slot_ref[STEP_ORDER[0], band, tile], 1), :])
        letter = jnp.concatenate(state + [blank, level_rows], axis=0)
        mail_ref[odd * half + band] = letter.astype(jnp.bfloat16)


def prepare_kernel(table_ref, adjoint_ref, bottom_ref, mix_ref, masked_ref, base_ref, kappa_ref):
    levels = adjoint_ref.shape[0] // (2 * ROWS)
    bottom = bottom_ref[...]
    edge = jnp.zeros((ROWS, LANES), jnp.float32)
    kappa_ref[0:ROWS] = edge
    kappa_ref[levels * ROWS : (levels + 1) * ROWS] = edge
    for level in range(levels - 1):
        classes = mix_ref[level * ROWS : (level + 1) * ROWS]
        kappa = jnp.full((ROWS, LANES), table_ref[0], jnp.float32)
        for index in range(1, table_ref.shape[0]):
            kappa = jnp.where(classes == index, table_ref[index], kappa)
        kappa_ref[(level + 1) * ROWS : (level + 2) * ROWS] = kappa
    for tracer in range(2):
        start = tracer * levels * ROWS
        for level in range(levels):
            here = slice(start + level * ROWS, start + (level + 1) * ROWS)
            masked_ref[here] = jnp.where(level < bottom, adjoint_ref[here], 0.0)
        for level in range(levels):
            base_ref[start + level * ROWS : start + (level + 1) * ROWS] = mixed(
                masked_ref, kappa_ref, start, level, levels
            )


def mixed(masked_ref, kappa_ref, start, level, levels):
    def at(index):
        return masked_ref[start + index * ROWS : start + (index + 1) * ROWS]

    masked = at(level)
    below = at(level + 1) if level + 1 < levels else jnp.zeros_like(masked)
    above = at(level - 1) if level > 0 else jnp.zeros_like(masked)
    kappa_above = kappa_ref[level * ROWS : (level + 1) * ROWS]
    kappa_below = kappa_ref[(level + 1) * ROWS : (level + 2) * ROWS]
    return masked + kappa_below * (below - masked) + kappa_above * (above - masked)


def edges_kernel(
    offset_ref,
    piece_ref,
    mail_ref,
    masked_ref,
    base_ref,
    bottom_ref,
    state_ref,
    inner_ref,
    outer_ref,
    top_ref,
    bot_ref,
    part_ref,
    column_ref,
    letter_ref,
):
    tile = lax.axis_index("lon")
    band = lax.axis_index("lat")
    levels = masked_ref.shape[0] // (2 * ROWS)
    pieces = FIELDS * levels
    holders = piece_ref.shape[0]
    lane = lanes_of((ROWS, LANES))
    sources = []
    for at, step in enumerate(STEP_ORDER):
        offset = offset_ref[step, band, tile]
        chunks = []
        for row in range(ROWS):
            chunk = piece_ref[lax.rem(row + offset, holders), at]
            state_ref[pl.ds(at * pieces * ROWS + row, pieces, stride=ROWS), :] = chunk.astype(
                jnp.float32
            )
            chunks.append(chunk)
        sources.append((EDGE_STATE[at], jnp.concatenate(chunks, axis=1)))
    for level in range(levels):
        zonal = state_ref[(2 * levels + level) * ROWS : (2 * levels + level + 1) * ROWS]
        east_factor = ADVECT_HALF * zonal + DIFFUSE
        west_factor = ADVECT_HALF * shift(zonal, 1, 1) - DIFFUSE
        for tracer in range(2):
            here = slice((tracer * levels + level) * ROWS, (tracer * levels + level + 1) * ROWS)
            masked = masked_ref[here]
            face = jnp.where(
                lane < LANES // 2,
                east_factor * (shift(masked, -1, 1) - masked),
                west_factor * (masked - shift(masked, 1, 1)),
            )
            part_ref[here] = base_ref[here] + face
    for start, ref in ((EDGE_MASKED, masked_ref), (EDGE_PART, part_ref)):
        columns = [strided(ref, row, 2 * levels).astype(jnp.bfloat16) for row in range(ROWS)]
        sources.append((start, jnp.concatenate(columns, axis=1)))
    place = (ROWS * LANES, LANES)
    from_row, from_lane = rows_of(place) // LANES, rows_of(place) % LANES
    chosen = ((from_lane == 0) & (lanes_of(place) == from_row)) | (
        (from_lane == LANES - 1) & (lanes_of(place) == from_row + ROWS)
    )
    pick = jnp.where(chosen, 1.0, 0.0).astype(jnp.bfloat16)
    column_ref[...] = jnp.zeros_like(column_ref)
    for start, source in sources:
        column_ref[start : start + source.shape[0]] = jnp.dot(
            source, pick, preferred_element_type=jnp.float32
        )
    edge = jnp.transpose(column_ref[...])
    bottom = bottom_ref[...].astype(jnp.float32)
    spot = lanes_of((ROWS, EDGE_LANES)) == EDGE_MASKED + 2 * levels
    to_west = jnp.where(spot, bottom[:, 0:1], edge[0:ROWS]).astype(jnp.bfloat16)
    to_east = jnp.where(spot, bottom[:, LANES - 1 :], edge[ROWS : 2 * ROWS]).astype(jnp.bfloat16)

    odd = lax.rem(tile, 2)

    @pl.when(odd == 0)
    def _():
        inner_ref[...] = to_east

    @pl.when(odd == 1)
    def _():
        inner_ref[...] = to_west

    tiles = offset_ref.shape[2]
    neighbour = lax.rem(tile + 2 * odd - 1 + tiles, tiles)
    half = odd * holders
    for at, step in enumerate(STEP_ORDER):
        offset = offset_ref[step, band, neighbour]
        for row in range(ROWS):
            letter = mail_ref[half + lax.rem(row + offset, holders)].astype(jnp.float32)
            letter_ref[at * ROWS + row : at * ROWS + row + 1] = letter[at : at + 1]
            if at == 0:
                letter_ref[2 * ROWS + row : 2 * ROWS + row + 1] = letter[2:3]
    own = mail_ref[half + band].astype(jnp.float32)
    edge_row, next_row = own[ROWS : 2 * ROWS], own[2 * ROWS : 3 * ROWS]
    chosen = jnp.where(odd == 1, letter_ref[0:ROWS], letter_ref[2 * ROWS : 3 * ROWS])
    lanes = lanes_of(chosen.shape)
    zonal = jnp.where(lanes < levels, shift(chosen, -2 * levels, 1), shift(chosen, -levels, 1))
    sign = (2 * odd - 1).astype(jnp.float32)
    face = (ADVECT_HALF * zonal + sign * DIFFUSE) * (sign * (next_row - edge_row))
    part = edge_row[:, LANES:] + face[:, 0:LANES]
    outer = (letter_ref[0:ROWS], letter_ref[ROWS : 2 * ROWS], edge_row[:, 0:LANES], part)
    outer_ref[...] = jnp.concatenate(outer, axis=1).astype(jnp.bfloat16)
    layout = Layout(levels)
    wide = lanes_of((levels, LANES))
    for row, inner, draft_ref in ((ROWS - 1, ROWS - 2, top_ref), (0, 1, bot_ref)):
        for at in range(2):
            begin = at * pieces * ROWS
            draft_ref[layout.tracer[at] : layout.tracer[at] + 2 * levels] = strided(
                state_ref, begin + row, 2 * levels
            )
            draft_ref[layout.merid[at] : layout.merid[at] + levels] = strided(
                state_ref, begin + 3 * levels * ROWS + row, levels
            )
        zonal = strided(state_ref, 2 * levels * ROWS + row, levels)
        merid = strided(state_ref, 3 * levels * ROWS + min(row, inner), levels)
        east_factor = ADVECT_HALF * zonal + DIFFUSE
        west_factor = ADVECT_HALF * shift(zonal, 1, 1) - DIFFUSE
        for tracer in range(2):
            begin = tracer * levels * ROWS
            masked = strided(masked_ref, begin + row, levels)
            next_row = strided(masked_ref, begin + inner, levels)
            if row > inner:
                along = (ADVECT_HALF * merid - DIFFUSE) * (masked - next_row)
            else:
                along = (ADVECT_HALF * merid + DIFFUSE) * (next_row - masked)
            east = east_factor * (shift(masked, -1, 1) - masked)
            west = west_factor * (masked - shift(masked, 1, 1))
            part = strided(base_ref, begin + row, levels) + along
            part = part + jnp.where(wide < LANES - 1, east, 0.0) + jnp.where(wide > 0, west, 0.0)
            at_masked = layout.masked + tracer * levels
            at_part = layout.part + tracer * levels
            draft_ref[at_masked : at_masked + levels] = masked
            draft_ref[at_part : at_part + levels] = part
        draft_ref[layout.corner : layout.corner + levels] = zonal
        draft_ref[layout.bottom : layout.rows] = jnp.broadcast_to(
            bottom[row : row + 1], (layout.rows - layout.bottom, LANES)
        )


def complete_kernel(
    levels,
    inner_ref,
    outer_ref,
    top_draft_ref,
    bot_draft_ref,
    near_ref,
    far_ref,
    west_ref,
    east_ref,
    edge_ref,
    column_ref,
    top_ref,
    bot_ref,
):
    layout = Layout(levels)
    odd_tile = lax.rem(lax.axis_index("lon"), 2) == 1
    odd_band = lax.rem(lax.axis_index("lat"), 2) == 1

    @pl.when(odd_tile)
    def _():
        west_ref[...] = inner_ref[...]
        east_ref[...] = outer_ref[...]

    @pl.when(jnp.logical_not(odd_tile))
    def _():
        west_ref[...] = outer_ref[...]
        east_ref[...] = inner_ref[...]

    top_ref[...] = top_draft_ref[...]
    bot_ref[...] = bot_draft_ref[...]
    edge_ref[...] = jnp.zeros_like(edge_ref)
    edge_ref[0:ROWS] = west_ref[...].astype(jnp.float32)
    edge_ref[ROWS : 2 * ROWS] = east_ref[...].astype(jnp.float32)
    column_ref[...] = jnp.transpose(edge_ref[...])
    lane = lanes_of((levels, LANES))

    def pair(start, row):
        block = column_ref[start : start + levels]
        return block[:, row : row + 1], block[:, ROWS + row : ROWS + row + 1]

    for row, draft_ref in ((ROWS - 1, top_ref), (0, bot_ref)):
        zonal = draft_ref[layout.corner : layout.corner + levels]
        zonal_west, _ = pair(EDGE_STATE[0] + 2 * levels, row)
        merid_west, merid_east = pair(EDGE_STATE[0] + 3 * levels, row)
        east_factor = ADVECT_HALF * zonal + DIFFUSE
        west_factor = ADVECT_HALF * zonal_west - DIFFUSE
        corner = jnp.where((lane == 32) | (lane == 96), merid_west, 0.0)
        corner = jnp.where((lane == 31) | (lane == 95), merid_east, corner)
        for tracer in range(2):
            west, east = pair(EDGE_MASKED + tracer * levels, row)
            at_masked = layout.masked + tracer * levels
            at_part = layout.part + tracer * levels
            masked = draft_ref[at_masked : at_masked + levels]
            face = jnp.where(lane == LANES - 1, east_factor * (east - masked), 0.0)
            face = jnp.where(lane == 0, west_factor * (masked - west), face)
            draft_ref[at_part : at_part + levels] = draft_ref[at_part : at_part + levels] + face
            corner = jnp.where(lane == (0, LANES // 2)[tracer], west, corner)
            corner = jnp.where(lane == (LANES - 1, LANES // 2 - 1)[tracer], east, corner)
        draft_ref[layout.corner : layout.corner + levels] = corner

    @pl.when(odd_band)
    def _():
        near_ref[...] = bot_ref[...].astype(jnp.bfloat16)
        far_ref[...] = top_ref[...].astype(jnp.bfloat16)

    @pl.when(jnp.logical_not(odd_band))
    def _():
        near_ref[...] = top_ref[...].astype(jnp.bfloat16)
        far_ref[...] = bot_ref[...].astype(jnp.bfloat16)


def steps_kernel(
    near_ref,
    far_ref,
    west_ref,
    east_ref,
    state_ref,
    masked_ref,
    base_ref,
    kappa_ref,
    bottom_ref,
    adjoint_ref,
    velocity_ref,
    north_ref,
    south_ref,
    corner_ref,
    next_ref,
    side_ref,
    ring_ref,
):
    levels = masked_ref.shape[0] // (2 * ROWS)
    layout = Layout(levels)
    band = lax.axis_index("lat")
    odd_band = lax.rem(band, 2) == 1
    top_band = (band == lax.axis_size("lat") - 1).astype(jnp.int32)
    folded = top_band.astype(jnp.float32)
    square = (LANES, LANES)
    from_lane = rows_of(square)
    turned = from_lane + top_band * (LANES - 1 - 2 * from_lane)
    turn = jnp.where(lanes_of(square) == turned, 1.0, 0.0).astype(jnp.bfloat16)

    @pl.when(odd_band)
    def _():
        north_ref[...] = jnp.dot(far_ref[...], turn, preferred_element_type=jnp.float32)
        south_ref[...] = near_ref[...].astype(jnp.float32)

    @pl.when(jnp.logical_not(odd_band))
    def _():
        north_ref[...] = jnp.dot(near_ref[...], turn, preferred_element_type=jnp.float32)
        south_ref[...] = far_ref[...].astype(jnp.float32)

    for at in range(2):
        here = slice(layout.merid[at], layout.merid[at] + levels)
        north_ref[here] = north_ref[here] * folded
    for side, (ref, scale) in enumerate(((north_ref, folded), (south_ref, None))):
        packed = ref[layout.corner : layout.corner + levels]
        merid = shift(packed, 96, 1)
        merid = merid if scale is None else merid * scale
        for item, block in enumerate((packed, shift(packed, LANES // 2, 1), merid)):
            begin = (side * 3 + item) * levels
            corner_ref[begin : begin + levels] = block

    tile_shape = (ROWS, LANES)
    lane = lanes_of(tile_shape)
    row = rows_of(tile_shape)
    first_lane, last_lane = lane == 0, lane == LANES - 1
    bottom_row, top_row = row == 0, row == ROWS - 1
    closed = (band == 0).astype(jnp.int32)
    open_south = jnp.where(row >= closed, DIFFUSE, 0.0)
    bottom = bottom_ref[...]

    def spread(ref, index):
        return jnp.broadcast_to(ref[:, index : index + 1].astype(jnp.float32), tile_shape)

    def line(ref, index):
        return jnp.broadcast_to(ref[index : index + 1], tile_shape)

    def tile_of(ref, index):
        return ref[index * ROWS : (index + 1) * ROWS]

    side_bottom = jnp.where(
        first_lane,
        spread(west_ref, EDGE_MASKED + 2 * levels),
        spread(east_ref, EDGE_MASKED + 2 * levels),
    )

    def factors(at, level):
        begin = at * FIELDS * levels
        zonal = tile_of(state_ref, begin + 2 * levels + level)
        merid = tile_of(state_ref, begin + 3 * levels + level)
        zonal_west = jnp.where(
            first_lane,
            spread(west_ref, EDGE_STATE[at] + 2 * levels + level),
            shift(zonal, 1, 1),
        )
        merid_south = jnp.where(
            bottom_row, line(south_ref, layout.merid[at] + level), shift(merid, 1, 0)
        )
        merid_net = merid - jnp.where(top_row, line(north_ref, layout.merid[at] + level), 0.0)
        return (
            ADVECT_HALF * zonal,
            ADVECT_HALF * zonal_west,
            ADVECT_HALF * merid_net + DIFFUSE,
            ADVECT_HALF * merid_south - open_south,
        )

    def gradients(at, level, tracer, east, north):
        field = tile_of(state_ref, (at * FIELDS + tracer) * levels + level)
        field_east = jnp.where(
            last_lane,
            spread(east_ref, EDGE_STATE[at] + tracer * levels + level),
            shift(field, -1, 1),
        )
        field_north = jnp.where(
            top_row, line(north_ref, layout.tracer[at] + tracer * levels + level), shift(field, -1, 0)
        )
        return (field + field_east) * east, (field + field_north) * north

    level_of = rows_of((levels, LANES))
    for tracer in range(2):
        start = tracer * levels * ROWS
        at_masked = slice(layout.masked + tracer * levels, layout.masked + (tracer + 1) * levels)
        at_part = slice(layout.part + tracer * levels, layout.part + (tracer + 1) * levels)
        at_merid = slice(layout.merid[0], layout.merid[0] + levels)
        merid = strided(state_ref, 3 * levels * ROWS + ROWS - 1, levels)
        masked = strided(masked_ref, start + ROWS - 1, levels)
        face = (ADVECT_HALF * (north_ref[at_merid] - merid) + DIFFUSE) * (
            masked - north_ref[at_masked]
        )
        wet = level_of.astype(jnp.float32) < north_ref[layout.bottom : layout.bottom + 1]
        ring_ref[tracer * levels : (tracer + 1) * levels] = jnp.where(
            wet, north_ref[at_part] + face, 0.0
        )
        masked = strided(masked_ref, start, levels)
        face = (ADVECT_HALF * south_ref[at_merid] + DIFFUSE) * (masked - south_ref[at_masked])
        wet = level_of.astype(jnp.float32) < south_ref[layout.bottom : layout.bottom + 1]
        ring_ref[(2 + tracer) * levels : (3 + tracer) * levels] = jnp.where(
            wet, south_ref[at_part] + face, 0.0
        )

    for level in range(levels):
        zonal, zonal_west, north_factor, south_factor = factors(0, level)
        side_merid = jnp.where(
            first_lane,
            spread(west_ref, EDGE_STATE[0] + 3 * levels + level),
            spread(east_ref, EDGE_STATE[0] + 3 * levels + level),
        )
        side_north = side_merid - jnp.where(top_row, line(corner_ref, 2 * levels + level), 0.0)
        side_south = jnp.where(bottom_row, line(corner_ref, 5 * levels + level), shift(side_merid, 1, 0))
        side_north = ADVECT_HALF * side_north + DIFFUSE
        side_south = ADVECT_HALF * side_south - open_south
        zonal_total = jnp.zeros(tile_shape, jnp.float32)
        merid_total = jnp.zeros(tile_shape, jnp.float32)
        for tracer in range(2):
            index = tracer * levels + level
            masked = tile_of(masked_ref, index)
            west = spread(west_ref, EDGE_MASKED + index)
            east = spread(east_ref, EDGE_MASKED + index)
            side = jnp.where(first_lane, west, east)
            to_east = jnp.where(last_lane, east, shift(masked, -1, 1)) - masked
            to_west = masked - jnp.where(first_lane, west, shift(masked, 1, 1))
            to_north = (
                jnp.where(top_row, line(north_ref, layout.masked + index), shift(masked, -1, 0))
                - masked
            )
            to_south = masked - jnp.where(
                bottom_row, line(south_ref, layout.masked + index), shift(masked, 1, 0)
            )
            result = (
                tile_of(base_ref, index)
                + (zonal + DIFFUSE) * to_east
                + (zonal_west - DIFFUSE) * to_west
                + north_factor * to_north
                + south_factor * to_south
            )
            next_ref[index * ROWS : (index + 1) * ROWS] = jnp.where(level < bottom, result, 0.0)
            zonal_grad, merid_grad = gradients(0, level, tracer, to_east, to_north)
            zonal_total = zonal_total + zonal_grad
            merid_total = merid_total + merid_grad
            face = jnp.where(
                first_lane,
                (zonal_west + DIFFUSE) * (masked - side),
                (zonal - DIFFUSE) * (side - masked),
            )
            part = jnp.where(
                first_lane, spread(west_ref, EDGE_PART + index), spread(east_ref, EDGE_PART + index)
            )
            upper = jnp.where(top_row, line(corner_ref, index), shift(side, -1, 0)) - side
            lower = side - jnp.where(
                bottom_row, line(corner_ref, 3 * levels + index), shift(side, 1, 0)
            )
            result = part + face + side_north * upper + side_south * lower
            side_ref[index * ROWS : (index + 1) * ROWS] = jnp.where(
                side_bottom > level, result, 0.0
            )
        velocity_ref[level * ROWS : (level + 1) * ROWS] = ADVECT_HALF * zonal_total
        velocity_ref[(levels + level) * ROWS : (levels + level + 1) * ROWS] = (
            ADVECT_HALF * merid_total
        )

    for level in range(levels):
        zonal, zonal_west, north_factor, south_factor = factors(1, level)
        zonal_total = jnp.zeros(tile_shape, jnp.float32)
        merid_total = jnp.zeros(tile_shape, jnp.float32)
        for tracer in range(2):
            index = tracer * levels + level
            masked = tile_of(next_ref, index)
            side = tile_of(side_ref, index)
            to_east = jnp.where(last_lane, side, shift(masked, -1, 1)) - masked
            to_west = masked - jnp.where(first_lane, side, shift(masked, 1, 1))
            to_north = jnp.where(top_row, line(ring_ref, index), shift(masked, -1, 0)) - masked
            to_south = masked - jnp.where(
                bottom_row, line(ring_ref, 2 * levels + index), shift(masked, 1, 0)
            )
            adjoint_ref[index * ROWS : (index + 1) * ROWS] = (
                mixed(next_ref, kappa_ref, tracer * levels * ROWS, level, levels)
                + (zonal + DIFFUSE) * to_east
                + (zonal_west - DIFFUSE) * to_west
                + north_factor * to_north
                + south_factor * to_south
            )
            zonal_grad, merid_grad = gradients(1, level, tracer, to_east, to_north)
            zonal_total = zonal_total + zonal_grad
            merid_total = merid_total + merid_grad
        for total, begin in ((zonal_total, 0), (merid_total, levels)):
            here = slice((begin + level) * ROWS, (begin + level + 1) * ROWS)
            velocity_ref[here] = velocity_ref[here] + ADVECT_HALF * total


def swaps(pairs):
    return [pair for low, high in pairs for pair in ((low, high), (high, low))]


def line_routes(tiles, bands):
    near, far = [], []
    for tile in range(tiles):
        start = tile * bands
        near += [(start + band, start + band + 1) for band in range(0, bands, 2)]
        far += [(start + band, start + band + 1) for band in range(1, bands - 1, 2)]
        if tile < tiles // 2:
            far.append((start + bands - 1, (tiles - tile) * bands - 1))
    return swaps(near), swaps(far)


def call(kernel, outputs, scratch, scalars, arrays):
    vmem = pl.BlockSpec(memory_space=pltpu.VMEM)
    smem = pl.BlockSpec(memory_space=pltpu.SMEM)
    return pl.pallas_call(
        kernel,
        out_shape=[jax.ShapeDtypeStruct(shape, dtype) for shape, dtype in outputs],
        in_specs=[smem] * len(scalars) + [vmem] * len(arrays),
        out_specs=[vmem] * len(outputs),
        scratch_shapes=[pltpu.VMEM(shape, jnp.float32) for shape in scratch],
        compiler_params=pltpu.CompilerParams(vmem_limit_bytes=32 * 1024 * 1024),
    )(*scalars, *arrays)


def shards(final_adjoint, store, holder_offset, holder_slot, bottom_level, mix_class, mix_table):
    bands = lax.axis_size("lat")
    tiles = lax.axis_size("lon")
    levels = final_adjoint.shape[1]
    slots = store.shape[2]
    steps = len(STEP_ORDER)
    pieces = FIELDS * levels
    full = levels * ROWS
    layout = Layout(levels)
    narrow, wide = jnp.bfloat16, jnp.float32
    (request,) = call(
        request_kernel,
        [((bands, steps, pieces, LANES), narrow)],
        [(pieces * slots, LANES)],
        [holder_slot],
        [store.reshape(pieces * slots, LANES)],
    )
    received = lax.all_to_all(request, "lat", split_axis=0, concat_axis=0, tiled=True)
    masked, base, kappa = call(
        prepare_kernel,
        [((2 * full, LANES), wide), ((2 * full, LANES), wide), ((full + ROWS, LANES), wide)],
        [],
        [mix_table],
        [
            final_adjoint.reshape(2 * full, LANES),
            bottom_level,
            mix_class.reshape((levels - 1) * ROWS, LANES),
        ],
    )
    (mail,) = call(
        columns_kernel,
        [((2 * bands, 3 * ROWS, 2 * LANES), narrow)],
        [(pieces * slots, LANES), (2 * LANES, LANES), (LANES, 2 * LANES)],
        [holder_slot],
        [store.reshape(pieces * slots, LANES), masked, base, bottom_level],
    )
    groups = [
        [tile * bands + band for tile in (low, (low + 1) % tiles) for band in range(bands)]
        for low in range(1, tiles, 2)
    ]
    mail = lax.all_to_all(
        mail, ("lon", "lat"), split_axis=0, concat_axis=0, tiled=True, axis_index_groups=groups
    )
    state, inner, outer, top, bot = call(
        edges_kernel,
        [
            ((steps * FIELDS * full, LANES), wide),
            ((ROWS, EDGE_LANES), narrow),
            ((ROWS, EDGE_LANES), narrow),
            ((layout.rows, LANES), wide),
            ((layout.rows, LANES), wide),
        ],
        [(2 * full, LANES), (EDGE_LANES, LANES), (3 * ROWS, 2 * LANES)],
        [holder_offset],
        [received, mail, masked, base, bottom_level],
    )
    near_routes, far_routes = line_routes(tiles, bands)
    inner = lax.ppermute(inner, "lon", swaps((tile, tile + 1) for tile in range(0, tiles, 2)))
    near, far, west, east = call(
        functools.partial(complete_kernel, levels),
        [
            ((layout.rows, LANES), narrow),
            ((layout.rows, LANES), narrow),
            ((ROWS, EDGE_LANES), narrow),
            ((ROWS, EDGE_LANES), narrow),
        ],
        [(LANES, EDGE_LANES), (EDGE_LANES, LANES), (layout.rows, LANES), (layout.rows, LANES)],
        [],
        [inner, outer, top, bot],
    )
    near = lax.ppermute(near, ("lon", "lat"), near_routes)
    far = lax.ppermute(far, ("lon", "lat"), far_routes)
    adjoint, velocity = call(
        steps_kernel,
        [((2 * full, LANES), wide), ((2 * full, LANES), wide)],
        [
            (layout.rows, LANES),
            (layout.rows, LANES),
            (6 * levels, LANES),
            (2 * full, LANES),
            (2 * full, LANES),
            (4 * levels, LANES),
        ],
        [],
        [near, far, west, east, state, masked, base, kappa, bottom_level],
    )
    shape = (2, levels, ROWS, LANES)
    return adjoint.reshape(shape), velocity.reshape(shape)


def solution(mesh):
    return jax.shard_map(
        shards,
        mesh=mesh,
        in_specs=(
            P(None, None, "lat", "lon"),
            P(None, None, None, "lat", "lon"),
            P(),
            P(),
            P("lat", "lon"),
            P(None, "lat", "lon"),
            P(),
        ),
        out_specs=(P(None, None, "lat", "lon"), P(None, None, "lat", "lon")),
        check_vma=False,
    )
```

```python
import functools

import jax
import jax.numpy as jnp
from jax import lax
from jax.experimental import pallas as pl
from jax.experimental.pallas import tpu as pltpu
from jax.sharding import PartitionSpec as P

STEP_ORDER = (1, 0)
FIELDS = 4
ADVECT_HALF = 0.125
DIFFUSE = 0.1

ROWS = 8
LANES = 128

EDGE_STATE = (0, 256)
EDGE_MASKED = 512
EDGE_PART = 640
EDGE_LANES = 768


class Layout:
    def __init__(self, levels):
        self.tracer = (0, 3 * levels)
        self.merid = (2 * levels, 5 * levels)
        self.masked = 6 * levels
        self.part = 8 * levels
        self.corner = 10 * levels
        self.bottom = 11 * levels
        self.rows = (11 * levels + 1 + 15) // 16 * 16


def shift(block, amount, axis):
    return pltpu.roll(block, amount % block.shape[axis], axis)


def lanes_of(shape):
    return lax.broadcasted_iota(jnp.int32, shape, 1)


def rows_of(shape):
    return lax.broadcasted_iota(jnp.int32, shape, 0)


def strided(ref, start, count):
    return ref[pl.ds(start, count, stride=ROWS), :]


def request_kernel(
    slot_hbm, store_hbm, out_hbm, slot_ref, store_ref, wide_ref, pack_ref, slot_sem, in_sem, out_sem
):
    tile = lax.axis_index("lon")
    bands, steps, pieces, lanes = pack_ref.shape
    slots = store_ref.shape[0] // pieces
    length = store_ref.shape[0] // FIELDS
    table = pltpu.make_async_copy(slot_hbm, slot_ref, slot_sem)
    table.start()
    loads = []
    for field in range(FIELDS):
        here = pl.ds(field * length, length)
        load = pltpu.make_async_copy(store_hbm.at[here], store_ref.at[here], in_sem.at[field])
        load.start()
        loads.append(load)
    for field, load in enumerate(loads):
        load.wait()
        here = slice(field * length, (field + 1) * length)
        wide_ref[here] = store_ref[here].astype(jnp.float32)
    table.wait()
    stores = []
    for band in range(bands):
        for at, step in enumerate(STEP_ORDER):
            slot = slot_ref[step, band, tile]
            rows = wide_ref[pl.ds(slot, pieces, stride=slots), :]
            pack_ref[band, at] = rows.astype(jnp.bfloat16)
        store = pltpu.make_async_copy(pack_ref.at[band], out_hbm.at[band], out_sem.at[band])
        store.start()
        stores.append(store)
    for store in stores:
        store.wait()


def pick_columns():
    place = (ROWS * LANES, LANES)
    row, source = rows_of(place) // LANES, rows_of(place) % LANES
    order = lanes_of(place) - row
    chosen = (
        ((source == 0) & (order == 0))
        | ((source == LANES - 1) & (order == ROWS))
        | ((source == 1) & (order == 2 * ROWS))
        | ((source == LANES - 2) & (order == 3 * ROWS))
    )
    return jnp.where(chosen, 1.0, 0.0).astype(jnp.bfloat16)


def prepare_kernel(
    table_ref,
    adjoint_ref,
    bottom_ref,
    mix_ref,
    masked_ref,
    base_ref,
    kappa_ref,
    side_ref,
    pick_ref,
    column_ref,
):
    levels = adjoint_ref.shape[0] // (2 * ROWS)
    bottom = bottom_ref[...]
    edge = jnp.zeros((ROWS, LANES), jnp.float32)
    kappa_ref[0:ROWS] = edge
    kappa_ref[levels * ROWS : (levels + 1) * ROWS] = edge
    for level in range(levels - 1):
        classes = mix_ref[level * ROWS : (level + 1) * ROWS]
        kappa = jnp.full((ROWS, LANES), table_ref[0], jnp.float32)
        for index in range(1, table_ref.shape[0]):
            kappa = jnp.where(classes == index, table_ref[index], kappa)
        kappa_ref[(level + 1) * ROWS : (level + 2) * ROWS] = kappa
    for tracer in range(2):
        start = tracer * levels * ROWS
        for level in range(levels):
            here = slice(start + level * ROWS, start + (level + 1) * ROWS)
            masked_ref[here] = jnp.where(level < bottom, adjoint_ref[here], 0.0)
        for level in range(levels):
            base_ref[start + level * ROWS : start + (level + 1) * ROWS] = mixed(
                masked_ref, kappa_ref, start, level, levels
            )
    pick = pick_columns()
    pick_ref[...] = pick
    column_ref[...] = jnp.zeros_like(column_ref)
    rows = 2 * levels
    for start, ref in ((0, masked_ref), (LANES, base_ref)):
        blocks = [strided(ref, row, rows).astype(jnp.bfloat16) for row in range(ROWS)]
        column_ref[start : start + rows] = jnp.dot(
            jnp.concatenate(blocks, axis=1), pick, preferred_element_type=jnp.float32
        )
    side = jnp.transpose(column_ref[...])[0 : 4 * ROWS]
    spot = lanes_of((ROWS, 2 * LANES)) == rows
    depth = bottom.astype(jnp.float32)
    side_ref[...] = side
    side_ref[0:ROWS] = jnp.where(spot, depth[:, 0:1], side[0:ROWS])
    side_ref[ROWS : 2 * ROWS] = jnp.where(spot, depth[:, LANES - 1 :], side[ROWS : 2 * ROWS])


def mixed(masked_ref, kappa_ref, start, level, levels):
    def at(index):
        return masked_ref[start + index * ROWS : start + (index + 1) * ROWS]

    masked = at(level)
    below = at(level + 1) if level + 1 < levels else jnp.zeros_like(masked)
    above = at(level - 1) if level > 0 else jnp.zeros_like(masked)
    kappa_above = kappa_ref[level * ROWS : (level + 1) * ROWS]
    kappa_below = kappa_ref[(level + 1) * ROWS : (level + 2) * ROWS]
    return masked + kappa_below * (below - masked) + kappa_above * (above - masked)


def edges_kernel(
    offset_ref, piece_ref, side_ref, pick_ref, outer_ref, inner_ref, column_ref
):
    tile = lax.axis_index("lon")
    band = lax.axis_index("lat")
    holders, _, pieces, _ = piece_ref.shape
    levels = pieces // FIELDS
    column_ref[...] = jnp.zeros_like(column_ref)
    for at, step in enumerate(STEP_ORDER):
        offset = offset_ref[step, band, tile]
        chunks = [piece_ref[lax.rem(row + offset, holders), at] for row in range(ROWS)]
        column_ref[EDGE_STATE[at] : EDGE_STATE[at] + pieces] = jnp.dot(
            jnp.concatenate(chunks, axis=1), pick_ref[...], preferred_element_type=jnp.float32
        )
    state = jnp.transpose(column_ref[...])
    lane = lanes_of((ROWS, 2 * LANES))
    sides = []
    for at, sign in ((0, 1.0), (1, -1.0)):
        edge = state[at * ROWS : (at + 1) * ROWS]
        zonal = edge if at == 0 else state[3 * ROWS : 4 * ROWS]
        zonal = zonal[:, 0 : 2 * LANES]
        zonal = jnp.where(lane < levels, shift(zonal, -2 * levels, 1), shift(zonal, -levels, 1))
        masked = side_ref[at * ROWS : (at + 1) * ROWS]
        beside = side_ref[(at + 2) * ROWS : (at + 3) * ROWS]
        face = (ADVECT_HALF * zonal + sign * DIFFUSE) * (sign * (beside - masked))
        part = masked[:, LANES:] + face[:, 0:LANES]
        side = jnp.concatenate([edge, masked[:, 0:LANES], part], axis=1)
        sides.append(side.astype(jnp.bfloat16))
    to_west, to_east = sides

    @pl.when(lax.rem(tile, 2) == 0)
    def _():
        inner_ref[...] = to_east
        outer_ref[...] = to_west

    @pl.when(lax.rem(tile, 2) == 1)
    def _():
        inner_ref[...] = to_west
        outer_ref[...] = to_east


def drafts_kernel(
    offset_ref, piece_ref, masked_ref, base_ref, bottom_ref, state_ref, top_ref, bot_ref
):
    tile = lax.axis_index("lon")
    band = lax.axis_index("lat")
    levels = masked_ref.shape[0] // (2 * ROWS)
    pieces = FIELDS * levels
    holders = piece_ref.shape[0]
    for at, step in enumerate(STEP_ORDER):
        offset = offset_ref[step, band, tile]
        for row in range(ROWS):
            chunk = piece_ref[lax.rem(row + offset, holders), at]
            state_ref[pl.ds(at * pieces * ROWS + row, pieces, stride=ROWS), :] = chunk.astype(
                jnp.float32
            )
    bottom = bottom_ref[...].astype(jnp.float32)
    layout = Layout(levels)
    wide = lanes_of((levels, LANES))
    for row, inner, draft_ref in ((ROWS - 1, ROWS - 2, top_ref), (0, 1, bot_ref)):
        for at in range(2):
            begin = at * pieces * ROWS
            draft_ref[layout.tracer[at] : layout.tracer[at] + 2 * levels] = strided(
                state_ref, begin + row, 2 * levels
            )
            draft_ref[layout.merid[at] : layout.merid[at] + levels] = strided(
                state_ref, begin + 3 * levels * ROWS + row, levels
            )
        zonal = strided(state_ref, 2 * levels * ROWS + row, levels)
        merid = strided(state_ref, 3 * levels * ROWS + min(row, inner), levels)
        east_factor = ADVECT_HALF * zonal + DIFFUSE
        west_factor = ADVECT_HALF * shift(zonal, 1, 1) - DIFFUSE
        for tracer in range(2):
            begin = tracer * levels * ROWS
            masked = strided(masked_ref, begin + row, levels)
            next_row = strided(masked_ref, begin + inner, levels)
            if row > inner:
                along = (ADVECT_HALF * merid - DIFFUSE) * (masked - next_row)
            else:
                along = (ADVECT_HALF * merid + DIFFUSE) * (next_row - masked)
            east = east_factor * (shift(masked, -1, 1) - masked)
            west = west_factor * (masked - shift(masked, 1, 1))
            part = strided(base_ref, begin + row, levels) + along
            part = part + jnp.where(wide < LANES - 1, east, 0.0) + jnp.where(wide > 0, west, 0.0)
            at_masked = layout.masked + tracer * levels
            at_part = layout.part + tracer * levels
            draft_ref[at_masked : at_masked + levels] = masked
            draft_ref[at_part : at_part + levels] = part
        draft_ref[layout.corner : layout.corner + levels] = zonal
        draft_ref[layout.bottom : layout.rows] = jnp.broadcast_to(
            bottom[row : row + 1], (layout.rows - layout.bottom, LANES)
        )


def complete_kernel(
    levels,
    outer_ref,
    inner_ref,
    top_draft_ref,
    bot_draft_ref,
    far_ref,
    near_ref,
    west_ref,
    east_ref,
    pack_ref,
    edge_ref,
    column_ref,
    top_ref,
    bot_ref,
):
    layout = Layout(levels)
    odd_tile = lax.rem(lax.axis_index("lon"), 2) == 1
    odd_band = lax.rem(lax.axis_index("lat"), 2) == 1

    @pl.when(odd_tile)
    def _():
        west_ref[...] = inner_ref[...]
        east_ref[...] = outer_ref[...]

    @pl.when(jnp.logical_not(odd_tile))
    def _():
        west_ref[...] = outer_ref[...]
        east_ref[...] = inner_ref[...]

    top_ref[...] = top_draft_ref[...]
    bot_ref[...] = bot_draft_ref[...]
    edge_ref[...] = jnp.zeros_like(edge_ref)
    edge_ref[0:ROWS] = west_ref[...].astype(jnp.float32)
    edge_ref[ROWS : 2 * ROWS] = east_ref[...].astype(jnp.float32)
    column_ref[...] = jnp.transpose(edge_ref[...])
    lane = lanes_of((levels, LANES))

    def pair(start, row):
        block = column_ref[start : start + levels]
        return block[:, row : row + 1], block[:, ROWS + row : ROWS + row + 1]

    for row, draft_ref in ((ROWS - 1, top_ref), (0, bot_ref)):
        zonal = draft_ref[layout.corner : layout.corner + levels]
        zonal_west, _ = pair(EDGE_STATE[0] + 2 * levels, row)
        merid_west, merid_east = pair(EDGE_STATE[0] + 3 * levels, row)
        east_factor = ADVECT_HALF * zonal + DIFFUSE
        west_factor = ADVECT_HALF * zonal_west - DIFFUSE
        corner = jnp.where((lane == 32) | (lane == 96), merid_west, 0.0)
        corner = jnp.where((lane == 31) | (lane == 95), merid_east, corner)
        for tracer in range(2):
            west, east = pair(EDGE_MASKED + tracer * levels, row)
            at_masked = layout.masked + tracer * levels
            at_part = layout.part + tracer * levels
            masked = draft_ref[at_masked : at_masked + levels]
            face = jnp.where(lane == LANES - 1, east_factor * (east - masked), 0.0)
            face = jnp.where(lane == 0, west_factor * (masked - west), face)
            draft_ref[at_part : at_part + levels] = draft_ref[at_part : at_part + levels] + face
            corner = jnp.where(lane == (0, LANES // 2)[tracer], west, corner)
            corner = jnp.where(lane == (LANES - 1, LANES // 2 - 1)[tracer], east, corner)
        draft_ref[layout.corner : layout.corner + levels] = corner
        begin = 0 if row else levels
        pack_ref[begin : begin + levels] = corner

    @pl.when(odd_band)
    def _():
        near_ref[...] = bot_ref[...].astype(jnp.bfloat16)
        far_ref[...] = top_ref[...].astype(jnp.bfloat16)

    @pl.when(jnp.logical_not(odd_band))
    def _():
        near_ref[...] = top_ref[...].astype(jnp.bfloat16)
        far_ref[...] = bot_ref[...].astype(jnp.bfloat16)


class Tile:
    def __init__(self, levels, west_ref, east_ref, state_ref):
        self.levels = levels
        self.west_ref, self.east_ref, self.state_ref = west_ref, east_ref, state_ref
        self.shape = (ROWS, LANES)
        lane, row = lanes_of(self.shape), rows_of(self.shape)
        self.first_lane, self.last_lane = lane == 0, lane == LANES - 1
        self.bottom_row, self.top_row = row == 0, row == ROWS - 1

    def spread(self, ref, index):
        return jnp.broadcast_to(ref[:, index : index + 1].astype(jnp.float32), self.shape)

    def line(self, ref, index):
        return jnp.broadcast_to(ref[index : index + 1], self.shape)

    def side(self, index):
        return jnp.where(
            self.first_lane, self.spread(self.west_ref, index), self.spread(self.east_ref, index)
        )

    def velocities(self, at, level):
        begin = at * FIELDS * self.levels
        zonal = tile_of(self.state_ref, begin + 2 * self.levels + level)
        merid = tile_of(self.state_ref, begin + 3 * self.levels + level)
        zonal_west = jnp.where(
            self.first_lane,
            self.spread(self.west_ref, EDGE_STATE[at] + 2 * self.levels + level),
            shift(zonal, 1, 1),
        )
        return ADVECT_HALF * zonal, ADVECT_HALF * zonal_west, merid

    def tracer(self, at, level, tracer):
        field = tile_of(self.state_ref, (at * FIELDS + tracer) * self.levels + level)
        east = jnp.where(
            self.last_lane,
            self.spread(self.east_ref, EDGE_STATE[at] + tracer * self.levels + level),
            shift(field, -1, 1),
        )
        return field, east


def tile_of(ref, index):
    return ref[index * ROWS : (index + 1) * ROWS]


def first_step_kernel(
    west_ref,
    east_ref,
    state_ref,
    masked_ref,
    base_ref,
    bottom_ref,
    next_ref,
    side_ref,
    velocity_ref,
):
    levels = masked_ref.shape[0] // (2 * ROWS)
    tile = Tile(levels, west_ref, east_ref, state_ref)
    first_lane, last_lane = tile.first_lane, tile.last_lane
    top_row, bottom_row = tile.top_row, tile.bottom_row
    bottom = bottom_ref[...]
    side_bottom = tile.side(EDGE_MASKED + 2 * levels)
    for level in range(levels):
        zonal, zonal_west, merid = tile.velocities(0, level)
        north_factor = ADVECT_HALF * merid + DIFFUSE
        south_factor = ADVECT_HALF * shift(merid, 1, 0) - DIFFUSE
        side_merid = tile.side(EDGE_STATE[0] + 3 * levels + level)
        side_north = ADVECT_HALF * side_merid + DIFFUSE
        side_south = ADVECT_HALF * shift(side_merid, 1, 0) - DIFFUSE
        zonal_total = jnp.zeros(tile.shape, jnp.float32)
        merid_total = jnp.zeros(tile.shape, jnp.float32)
        for tracer in range(2):
            index = tracer * levels + level
            masked = tile_of(masked_ref, index)
            west = tile.spread(west_ref, EDGE_MASKED + index)
            east = tile.spread(east_ref, EDGE_MASKED + index)
            side = jnp.where(first_lane, west, east)
            to_east = jnp.where(last_lane, east, shift(masked, -1, 1)) - masked
            to_west = masked - jnp.where(first_lane, west, shift(masked, 1, 1))
            to_north = jnp.where(top_row, 0.0, shift(masked, -1, 0) - masked)
            to_south = jnp.where(bottom_row, 0.0, masked - shift(masked, 1, 0))
            result = (
                tile_of(base_ref, index)
                + (zonal + DIFFUSE) * to_east
                + (zonal_west - DIFFUSE) * to_west
                + north_factor * to_north
                + south_factor * to_south
            )
            next_ref[index * ROWS : (index + 1) * ROWS] = jnp.where(level < bottom, result, 0.0)
            field, field_east = tile.tracer(0, level, tracer)
            zonal_total = zonal_total + (field + field_east) * to_east
            merid_total = merid_total + (field + shift(field, -1, 0)) * to_north
            face = jnp.where(
                first_lane,
                (zonal_west + DIFFUSE) * (masked - side),
                (zonal - DIFFUSE) * (side - masked),
            )
            upper = jnp.where(top_row, 0.0, shift(side, -1, 0) - side)
            lower = jnp.where(bottom_row, 0.0, side - shift(side, 1, 0))
            result = (
                tile.side(EDGE_PART + index) + face + side_north * upper + side_south * lower
            )
            side_ref[index * ROWS : (index + 1) * ROWS] = jnp.where(
                side_bottom > level, result, 0.0
            )
        velocity_ref[level * ROWS : (level + 1) * ROWS] = ADVECT_HALF * zonal_total
        velocity_ref[(levels + level) * ROWS : (levels + level + 1) * ROWS] = (
            ADVECT_HALF * merid_total
        )


def second_step_kernel(
    far_ref,
    near_ref,
    pack_ref,
    west_ref,
    east_ref,
    state_ref,
    masked_ref,
    kappa_ref,
    bottom_ref,
    next_in_ref,
    side_in_ref,
    velocity_in_ref,
    adjoint_ref,
    velocity_ref,
    north_ref,
    south_ref,
    next_ref,
    side_ref,
    ring_ref,
):
    levels = masked_ref.shape[0] // (2 * ROWS)
    layout = Layout(levels)
    band = lax.axis_index("lat")
    odd_band = lax.rem(band, 2) == 1
    top_band = (band == lax.axis_size("lat") - 1).astype(jnp.int32)
    folded = top_band.astype(jnp.float32)
    open_south = jnp.where(band > 0, DIFFUSE, 0.0)
    square = (LANES, LANES)
    from_lane = rows_of(square)
    turned = from_lane + top_band * (LANES - 1 - 2 * from_lane)
    turn = jnp.where(lanes_of(square) == turned, 1.0, 0.0).astype(jnp.bfloat16)

    @pl.when(odd_band)
    def _():
        north_ref[...] = jnp.dot(far_ref[...], turn, preferred_element_type=jnp.float32)
        south_ref[...] = near_ref[...].astype(jnp.float32)

    @pl.when(jnp.logical_not(odd_band))
    def _():
        north_ref[...] = jnp.dot(near_ref[...], turn, preferred_element_type=jnp.float32)
        south_ref[...] = far_ref[...].astype(jnp.float32)

    next_ref[...] = next_in_ref[...]
    side_ref[...] = side_in_ref[...]
    velocity_ref[...] = velocity_in_ref[...]
    for at in range(2):
        here = slice(layout.merid[at], layout.merid[at] + levels)
        north_ref[here] = north_ref[here] * folded

    def rows_at(ref, begin):
        return ref[begin : begin + levels]

    def unpacked(packed):
        return packed, shift(packed, LANES // 2, 1), shift(packed, 96, 1)

    level_of = rows_of((levels, LANES)).astype(jnp.float32)
    left = lanes_of((levels, LANES)) < LANES // 2

    def side_depth(row):
        spot = slice(EDGE_MASKED + 2 * levels, EDGE_MASKED + 2 * levels + 1)
        west = west_ref[...].astype(jnp.float32)[row : row + 1, spot]
        east = east_ref[...].astype(jnp.float32)[row : row + 1, spot]
        return jnp.where(left, west, east)

    def add_rows(ref, begin, value):
        here = pl.ds(begin, levels, stride=ROWS)
        ref[here, :] = ref[here, :] + value

    top = ROWS - 1
    depth = bottom_ref[...].astype(jnp.float32)
    top_merid = strided(state_ref, 3 * levels * ROWS + top, levels)
    north_merid = rows_at(north_ref, layout.merid[0])
    south_merid = rows_at(south_ref, layout.merid[0])
    top_factor = ADVECT_HALF * (top_merid - north_merid) + DIFFUSE
    bottom_factor = ADVECT_HALF * south_merid - open_south
    own_top = unpacked(rows_at(pack_ref, 0))
    own_bottom = unpacked(rows_at(pack_ref, levels))
    north_corner = unpacked(rows_at(north_ref, layout.corner))
    south_corner = unpacked(rows_at(south_ref, layout.corner))
    side_top_factor = ADVECT_HALF * (own_top[2] - folded * north_corner[2]) + DIFFUSE
    side_bottom_factor = ADVECT_HALF * south_corner[2] - open_south
    merid_total = jnp.zeros((levels, LANES), jnp.float32)
    for tracer in range(2):
        start = tracer * levels * ROWS
        masked = strided(masked_ref, start + top, levels)
        beyond = rows_at(north_ref, layout.masked + tracer * levels)
        part = rows_at(north_ref, layout.part + tracer * levels)
        step = beyond - masked
        add_rows(
            next_ref, start + top, jnp.where(level_of < depth[top:], top_factor * step, 0.0)
        )
        ring = part - (ADVECT_HALF * (north_merid - top_merid) + DIFFUSE) * step
        wet = level_of < north_ref[layout.bottom : layout.bottom + 1]
        ring_ref[tracer * levels : (tracer + 1) * levels] = jnp.where(wet, ring, 0.0)
        field = strided(state_ref, start + top, levels)
        field_north = rows_at(north_ref, layout.tracer[0] + tracer * levels)
        merid_total = merid_total + (field + field_north) * step
        masked = strided(masked_ref, start, levels)
        beyond = rows_at(south_ref, layout.masked + tracer * levels)
        part = rows_at(south_ref, layout.part + tracer * levels)
        step = masked - beyond
        add_rows(
            next_ref, start, jnp.where(level_of < depth[0:1], bottom_factor * step, 0.0)
        )
        ring = part + (ADVECT_HALF * south_merid + DIFFUSE) * step
        wet = level_of < south_ref[layout.bottom : layout.bottom + 1]
        ring_ref[(2 + tracer) * levels : (3 + tracer) * levels] = jnp.where(wet, ring, 0.0)
        face = side_top_factor * (north_corner[tracer] - own_top[tracer])
        add_rows(side_ref, start + top, jnp.where(level_of < side_depth(top), face, 0.0))
        face = side_bottom_factor * (own_bottom[tracer] - south_corner[tracer])
        add_rows(side_ref, start, jnp.where(level_of < side_depth(0), face, 0.0))
    add_rows(velocity_ref, levels * ROWS + top, ADVECT_HALF * merid_total)

    tile = Tile(levels, west_ref, east_ref, state_ref)
    first_lane, last_lane = tile.first_lane, tile.last_lane
    top_row, bottom_row = tile.top_row, tile.bottom_row
    closed = (band == 0).astype(jnp.int32)
    spread_south = jnp.where(rows_of(tile.shape) >= closed, DIFFUSE, 0.0)
    for level in range(levels):
        zonal, zonal_west, merid = tile.velocities(1, level)
        merid_south = jnp.where(
            bottom_row, tile.line(south_ref, layout.merid[1] + level), shift(merid, 1, 0)
        )
        merid_net = merid - jnp.where(top_row, tile.line(north_ref, layout.merid[1] + level), 0.0)
        north_factor = ADVECT_HALF * merid_net + DIFFUSE
        south_factor = ADVECT_HALF * merid_south - spread_south
        zonal_total = jnp.zeros(tile.shape, jnp.float32)
        merid_total = jnp.zeros(tile.shape, jnp.float32)
        for tracer in range(2):
            index = tracer * levels + level
            masked = tile_of(next_ref, index)
            side = tile_of(side_ref, index)
            to_east = jnp.where(last_lane, side, shift(masked, -1, 1)) - masked
            to_west = masked - jnp.where(first_lane, side, shift(masked, 1, 1))
            to_north = jnp.where(top_row, tile.line(ring_ref, index), shift(masked, -1, 0)) - masked
            to_south = masked - jnp.where(
                bottom_row, tile.line(ring_ref, 2 * levels + index), shift(masked, 1, 0)
            )
            adjoint_ref[index * ROWS : (index + 1) * ROWS] = (
                mixed(next_ref, kappa_ref, tracer * levels * ROWS, level, levels)
                + (zonal + DIFFUSE) * to_east
                + (zonal_west - DIFFUSE) * to_west
                + north_factor * to_north
                + south_factor * to_south
            )
            field, field_east = tile.tracer(1, level, tracer)
            field_north = jnp.where(
                top_row,
                tile.line(north_ref, layout.tracer[1] + tracer * levels + level),
                shift(field, -1, 0),
            )
            zonal_total = zonal_total + (field + field_east) * to_east
            merid_total = merid_total + (field + field_north) * to_north
        for total, begin in ((zonal_total, 0), (merid_total, levels)):
            here = slice((begin + level) * ROWS, (begin + level + 1) * ROWS)
            velocity_ref[here] = velocity_ref[here] + ADVECT_HALF * total


def swaps(pairs):
    return [pair for low, high in pairs for pair in ((low, high), (high, low))]


def ring_routes(tiles):
    inner = swaps((tile, tile + 1) for tile in range(0, tiles, 2))
    outer = swaps((tile, (tile + 1) % tiles) for tile in range(1, tiles, 2))
    return inner, outer


def line_routes(tiles, bands):
    near, far = [], []
    for tile in range(tiles):
        start = tile * bands
        near += [(start + band, start + band + 1) for band in range(0, bands, 2)]
        far += [(start + band, start + band + 1) for band in range(1, bands - 1, 2)]
        if tile < tiles // 2:
            far.append((start + bands - 1, (tiles - tile) * bands - 1))
    return swaps(near), swaps(far)


def call(kernel, outputs, scratch, scalars, arrays):
    vmem = pl.BlockSpec(memory_space=pltpu.VMEM)
    smem = pl.BlockSpec(memory_space=pltpu.SMEM)
    return pl.pallas_call(
        kernel,
        out_shape=[jax.ShapeDtypeStruct(shape, dtype) for shape, dtype in outputs],
        in_specs=[smem] * len(scalars) + [vmem] * len(arrays),
        out_specs=[vmem] * len(outputs),
        scratch_shapes=[pltpu.VMEM(shape, jnp.float32) for shape in scratch],
        compiler_params=pltpu.CompilerParams(vmem_limit_bytes=32 * 1024 * 1024),
    )(*scalars, *arrays)


def shards(final_adjoint, store, holder_offset, holder_slot, bottom_level, mix_class, mix_table):
    bands = lax.axis_size("lat")
    tiles = lax.axis_size("lon")
    levels = final_adjoint.shape[1]
    slots = store.shape[2]
    steps = len(STEP_ORDER)
    pieces = FIELDS * levels
    full = levels * ROWS
    layout = Layout(levels)
    narrow, wide = jnp.bfloat16, jnp.float32
    hbm = pl.BlockSpec(memory_space=pltpu.HBM)
    request = pl.pallas_call(
        request_kernel,
        out_shape=jax.ShapeDtypeStruct((bands, steps, pieces, LANES), narrow),
        in_specs=[hbm, hbm],
        out_specs=hbm,
        scratch_shapes=[
            pltpu.SMEM(holder_slot.shape, jnp.int32),
            pltpu.VMEM((pieces * slots, LANES), narrow),
            pltpu.VMEM((pieces * slots, LANES), wide),
            pltpu.VMEM((bands, steps, pieces, LANES), narrow),
            pltpu.SemaphoreType.DMA,
            pltpu.SemaphoreType.DMA((FIELDS,)),
            pltpu.SemaphoreType.DMA((bands,)),
        ],
        compiler_params=pltpu.CompilerParams(vmem_limit_bytes=32 * 1024 * 1024),
    )(
        pltpu.with_memory_space_constraint(holder_slot, pltpu.HBM),
        pltpu.with_memory_space_constraint(store.reshape(pieces * slots, LANES), pltpu.HBM),
    )
    received = lax.all_to_all(request, "lat", split_axis=0, concat_axis=0, tiled=True)
    masked, base, kappa, side, pick = call(
        prepare_kernel,
        [
            ((2 * full, LANES), wide),
            ((2 * full, LANES), wide),
            ((full + ROWS, LANES), wide),
            ((4 * ROWS, 2 * LANES), wide),
            ((ROWS * LANES, LANES), narrow),
        ],
        [(2 * LANES, LANES)],
        [mix_table],
        [
            final_adjoint.reshape(2 * full, LANES),
            bottom_level,
            mix_class.reshape((levels - 1) * ROWS, LANES),
        ],
    )
    outer, inner = call(
        edges_kernel,
        [((ROWS, EDGE_LANES), narrow), ((ROWS, EDGE_LANES), narrow)],
        [(EDGE_MASKED, LANES)],
        [holder_offset],
        [received, side, pick],
    )
    inner_routes, outer_routes = ring_routes(tiles)
    near_routes, far_routes = line_routes(tiles, bands)
    outer = lax.ppermute(outer, "lon", outer_routes)
    inner = lax.ppermute(inner, "lon", inner_routes)
    state, top, bot = call(
        drafts_kernel,
        [
            ((steps * FIELDS * full, LANES), wide),
            ((layout.rows, LANES), wide),
            ((layout.rows, LANES), wide),
        ],
        [],
        [holder_offset],
        [received, masked, base, bottom_level],
    )
    far, near, west, east, pack = call(
        functools.partial(complete_kernel, levels),
        [
            ((layout.rows, LANES), narrow),
            ((layout.rows, LANES), narrow),
            ((ROWS, EDGE_LANES), narrow),
            ((ROWS, EDGE_LANES), narrow),
            ((2 * levels, LANES), wide),
        ],
        [(LANES, EDGE_LANES), (EDGE_LANES, LANES), (layout.rows, LANES), (layout.rows, LANES)],
        [],
        [outer, inner, top, bot],
    )
    far = lax.ppermute(far, ("lon", "lat"), far_routes)
    near = lax.ppermute(near, ("lon", "lat"), near_routes)
    following, beside, velocity = call(
        first_step_kernel,
        [((2 * full, LANES), wide)] * 3,
        [],
        [],
        [west, east, state, masked, base, bottom_level],
    )
    adjoint, velocity = call(
        second_step_kernel,
        [((2 * full, LANES), wide)] * 2,
        [
            (layout.rows, LANES),
            (layout.rows, LANES),
            (2 * full, LANES),
            (2 * full, LANES),
            (4 * levels, LANES),
        ],
        [],
        [
            far,
            near,
            pack,
            west,
            east,
            state,
            masked,
            kappa,
            bottom_level,
            following,
            beside,
            velocity,
        ],
    )
    shape = (2, levels, ROWS, LANES)
    return adjoint.reshape(shape), velocity.reshape(shape)


def solution(mesh):
    return jax.shard_map(
        shards,
        mesh=mesh,
        in_specs=(
            P(None, None, "lat", "lon"),
            P(None, None, None, "lat", "lon"),
            P(),
            P(),
            P("lat", "lon"),
            P(None, "lat", "lon"),
            P(),
        ),
        out_specs=(P(None, None, "lat", "lon"), P(None, None, "lat", "lon")),
        check_vma=False,
    )
```

```python
import functools

import jax
import jax.numpy as jnp
from jax import lax
from jax.experimental import pallas as pl
from jax.experimental.pallas import tpu as pltpu
from jax.sharding import PartitionSpec as P

STEP_ORDER = (1, 0)
FIELDS = 4
ADVECT_HALF = 0.125
DIFFUSE = 0.1

ROWS = 8
LANES = 128

EDGE_STATE = (0, 256)
EDGE_MASKED = 512
EDGE_PART = 640
EDGE_LANES = 768


class Layout:
    def __init__(self, levels):
        self.tracer = (0, 3 * levels)
        self.merid = (2 * levels, 5 * levels)
        self.masked = 6 * levels
        self.part = 8 * levels
        self.corner = 10 * levels
        self.bottom = 11 * levels
        self.rows = (11 * levels + 1 + 15) // 16 * 16


def shift(block, amount, axis):
    return pltpu.roll(block, amount % block.shape[axis], axis)


def lanes_of(shape):
    return lax.broadcasted_iota(jnp.int32, shape, 1)


def rows_of(shape):
    return lax.broadcasted_iota(jnp.int32, shape, 0)


def strided(ref, start, count):
    return ref[pl.ds(start, count, stride=ROWS), :]


def request_kernel(
    slot_hbm, store_hbm, out_hbm, slot_ref, store_ref, wide_ref, pack_ref, slot_sem, in_sem, out_sem
):
    tile = lax.axis_index("lon")
    bands, steps, pieces, lanes = pack_ref.shape
    slots = store_ref.shape[0] // pieces
    length = store_ref.shape[0] // FIELDS
    table = pltpu.make_async_copy(slot_hbm, slot_ref, slot_sem)
    table.start()
    loads = []
    for field in range(FIELDS):
        here = pl.ds(field * length, length)
        load = pltpu.make_async_copy(store_hbm.at[here], store_ref.at[here], in_sem.at[field])
        load.start()
        loads.append(load)
    for field, load in enumerate(loads):
        load.wait()
        here = slice(field * length, (field + 1) * length)
        wide_ref[here] = store_ref[here].astype(jnp.float32)
    table.wait()
    stores = []
    for band in range(bands):
        for at, step in enumerate(STEP_ORDER):
            slot = slot_ref[step, band, tile]
            rows = wide_ref[pl.ds(slot, pieces, stride=slots), :]
            pack_ref[band, at] = rows.astype(jnp.bfloat16)
        store = pltpu.make_async_copy(pack_ref.at[band], out_hbm.at[band], out_sem.at[band])
        store.start()
        stores.append(store)
    for store in stores:
        store.wait()


def pick_columns():
    place = (ROWS * LANES, LANES)
    row, source = rows_of(place) // LANES, rows_of(place) % LANES
    order = lanes_of(place) - row
    chosen = (
        ((source == 0) & (order == 0))
        | ((source == LANES - 1) & (order == ROWS))
        | ((source == 1) & (order == 2 * ROWS))
        | ((source == LANES - 2) & (order == 3 * ROWS))
    )
    return jnp.where(chosen, 1.0, 0.0).astype(jnp.bfloat16)


def prepare_kernel(
    table_ref,
    adjoint_ref,
    bottom_ref,
    mix_ref,
    masked_ref,
    base_ref,
    kappa_ref,
    side_ref,
    pick_ref,
    column_ref,
):
    levels = adjoint_ref.shape[0] // (2 * ROWS)
    bottom = bottom_ref[...]
    edge = jnp.zeros((ROWS, LANES), jnp.float32)
    kappa_ref[0:ROWS] = edge
    kappa_ref[levels * ROWS : (levels + 1) * ROWS] = edge
    for level in range(levels - 1):
        classes = mix_ref[level * ROWS : (level + 1) * ROWS]
        kappa = jnp.full((ROWS, LANES), table_ref[0], jnp.float32)
        for index in range(1, table_ref.shape[0]):
            kappa = jnp.where(classes == index, table_ref[index], kappa)
        kappa_ref[(level + 1) * ROWS : (level + 2) * ROWS] = kappa
    for tracer in range(2):
        start = tracer * levels * ROWS
        for level in range(levels):
            here = slice(start + level * ROWS, start + (level + 1) * ROWS)
            masked_ref[here] = jnp.where(level < bottom, adjoint_ref[here], 0.0)
        for level in range(levels):
            base_ref[start + level * ROWS : start + (level + 1) * ROWS] = mixed(
                masked_ref, kappa_ref, start, level, levels
            )
    pick = pick_columns()
    pick_ref[...] = pick
    column_ref[...] = jnp.zeros_like(column_ref)
    rows = 2 * levels
    for start, ref in ((0, masked_ref), (LANES, base_ref)):
        blocks = [strided(ref, row, rows).astype(jnp.bfloat16) for row in range(ROWS)]
        column_ref[start : start + rows] = jnp.dot(
            jnp.concatenate(blocks, axis=1), pick, preferred_element_type=jnp.float32
        )
    side = jnp.transpose(column_ref[...])[0 : 4 * ROWS]
    spot = lanes_of((ROWS, 2 * LANES)) == rows
    depth = bottom.astype(jnp.float32)
    side_ref[...] = side
    side_ref[0:ROWS] = jnp.where(spot, depth[:, 0:1], side[0:ROWS])
    side_ref[ROWS : 2 * ROWS] = jnp.where(spot, depth[:, LANES - 1 :], side[ROWS : 2 * ROWS])


def mixed(masked_ref, kappa_ref, start, level, levels):
    def at(index):
        return masked_ref[start + index * ROWS : start + (index + 1) * ROWS]

    masked = at(level)
    below = at(level + 1) if level + 1 < levels else jnp.zeros_like(masked)
    above = at(level - 1) if level > 0 else jnp.zeros_like(masked)
    kappa_above = kappa_ref[level * ROWS : (level + 1) * ROWS]
    kappa_below = kappa_ref[(level + 1) * ROWS : (level + 2) * ROWS]
    return masked + kappa_below * (below - masked) + kappa_above * (above - masked)


def edges_kernel(
    offset_ref, piece_ref, side_ref, pick_ref, outer_ref, inner_ref, column_ref
):
    tile = lax.axis_index("lon")
    band = lax.axis_index("lat")
    holders, _, pieces, _ = piece_ref.shape
    levels = pieces // FIELDS
    column_ref[...] = jnp.zeros_like(column_ref)
    for at, step in enumerate(STEP_ORDER):
        offset = offset_ref[step, band, tile]
        chunks = [piece_ref[lax.rem(row + offset, holders), at] for row in range(ROWS)]
        column_ref[EDGE_STATE[at] : EDGE_STATE[at] + pieces] = jnp.dot(
            jnp.concatenate(chunks, axis=1), pick_ref[...], preferred_element_type=jnp.float32
        )
    state = jnp.transpose(column_ref[...])
    lane = lanes_of((ROWS, 2 * LANES))
    sides = []
    for at, sign in ((0, 1.0), (1, -1.0)):
        edge = state[at * ROWS : (at + 1) * ROWS]
        zonal = edge if at == 0 else state[3 * ROWS : 4 * ROWS]
        zonal = zonal[:, 0 : 2 * LANES]
        zonal = jnp.where(lane < levels, shift(zonal, -2 * levels, 1), shift(zonal, -levels, 1))
        masked = side_ref[at * ROWS : (at + 1) * ROWS]
        beside = side_ref[(at + 2) * ROWS : (at + 3) * ROWS]
        face = (ADVECT_HALF * zonal + sign * DIFFUSE) * (sign * (beside - masked))
        part = masked[:, LANES:] + face[:, 0:LANES]
        side = jnp.concatenate([edge, masked[:, 0:LANES], part], axis=1)
        sides.append(side.astype(jnp.bfloat16))
    to_west, to_east = sides

    @pl.when(lax.rem(tile, 2) == 0)
    def _():
        inner_ref[...] = to_east
        outer_ref[...] = to_west

    @pl.when(lax.rem(tile, 2) == 1)
    def _():
        inner_ref[...] = to_west
        outer_ref[...] = to_east


def tiles_kernel(offset_ref, piece_ref, west_ref, state_ref):
    tile = lax.axis_index("lon")
    band = lax.axis_index("lat")
    holders, _, pieces, _ = piece_ref.shape
    for at, step in enumerate(STEP_ORDER):
        offset = offset_ref[step, band, tile]
        for row in range(ROWS):
            chunk = piece_ref[lax.rem(row + offset, holders), at]
            state_ref[pl.ds(at * pieces * ROWS + row, pieces, stride=ROWS), :] = chunk.astype(
                jnp.float32
            )


def drafts_kernel(
    offset_ref, piece_ref, masked_ref, base_ref, bottom_ref, top_ref, bot_ref, line_ref
):
    tile = lax.axis_index("lon")
    band = lax.axis_index("lat")
    levels = masked_ref.shape[0] // (2 * ROWS)
    pieces = FIELDS * levels
    holders = piece_ref.shape[0]
    for slot, (row, at) in enumerate(((ROWS - 1, 0), (ROWS - 1, 1), (0, 0), (0, 1), (ROWS - 2, 0))):
        offset = offset_ref[STEP_ORDER[at], band, tile]
        chunk = piece_ref[lax.rem(row + offset, holders), at]
        line_ref[slot * pieces : (slot + 1) * pieces] = chunk.astype(jnp.float32)
    bottom = bottom_ref[...].astype(jnp.float32)
    layout = Layout(levels)
    wide = lanes_of((levels, LANES))
    for row, inner, first, facing, draft_ref in (
        (ROWS - 1, ROWS - 2, 0, 4, top_ref),
        (0, 1, 2, 2, bot_ref),
    ):
        for at in range(2):
            begin = (first + at) * pieces
            draft_ref[layout.tracer[at] : layout.tracer[at] + 2 * levels] = line_ref[
                begin : begin + 2 * levels
            ]
            draft_ref[layout.merid[at] : layout.merid[at] + levels] = line_ref[
                begin + 3 * levels : begin + 4 * levels
            ]
        zonal = line_ref[first * pieces + 2 * levels : first * pieces + 3 * levels]
        merid = line_ref[facing * pieces + 3 * levels : facing * pieces + 4 * levels]
        east_factor = ADVECT_HALF * zonal + DIFFUSE
        west_factor = ADVECT_HALF * shift(zonal, 1, 1) - DIFFUSE
        for tracer in range(2):
            begin = tracer * levels * ROWS
            masked = strided(masked_ref, begin + row, levels)
            next_row = strided(masked_ref, begin + inner, levels)
            if row > inner:
                along = (ADVECT_HALF * merid - DIFFUSE) * (masked - next_row)
            else:
                along = (ADVECT_HALF * merid + DIFFUSE) * (next_row - masked)
            east = east_factor * (shift(masked, -1, 1) - masked)
            west = west_factor * (masked - shift(masked, 1, 1))
            part = strided(base_ref, begin + row, levels) + along
            part = part + jnp.where(wide < LANES - 1, east, 0.0) + jnp.where(wide > 0, west, 0.0)
            at_masked = layout.masked + tracer * levels
            at_part = layout.part + tracer * levels
            draft_ref[at_masked : at_masked + levels] = masked
            draft_ref[at_part : at_part + levels] = part
        draft_ref[layout.corner : layout.corner + levels] = zonal
        draft_ref[layout.bottom : layout.rows] = jnp.broadcast_to(
            bottom[row : row + 1], (layout.rows - layout.bottom, LANES)
        )


def complete_kernel(
    levels,
    outer_ref,
    inner_ref,
    top_draft_ref,
    bot_draft_ref,
    far_ref,
    near_ref,
    west_ref,
    east_ref,
    pack_ref,
    edge_ref,
    column_ref,
    top_ref,
    bot_ref,
):
    layout = Layout(levels)
    odd_tile = lax.rem(lax.axis_index("lon"), 2) == 1
    odd_band = lax.rem(lax.axis_index("lat"), 2) == 1

    @pl.when(odd_tile)
    def _():
        west_ref[...] = inner_ref[...]
        east_ref[...] = outer_ref[...]

    @pl.when(jnp.logical_not(odd_tile))
    def _():
        west_ref[...] = outer_ref[...]
        east_ref[...] = inner_ref[...]

    top_ref[...] = top_draft_ref[...]
    bot_ref[...] = bot_draft_ref[...]
    edge_ref[...] = jnp.zeros_like(edge_ref)
    edge_ref[0:ROWS] = west_ref[...].astype(jnp.float32)
    edge_ref[ROWS : 2 * ROWS] = east_ref[...].astype(jnp.float32)
    column_ref[...] = jnp.transpose(edge_ref[...])
    lane = lanes_of((levels, LANES))

    def pair(start, row):
        block = column_ref[start : start + levels]
        return block[:, row : row + 1], block[:, ROWS + row : ROWS + row + 1]

    for row, draft_ref in ((ROWS - 1, top_ref), (0, bot_ref)):
        zonal = draft_ref[layout.corner : layout.corner + levels]
        zonal_west, _ = pair(EDGE_STATE[0] + 2 * levels, row)
        merid_west, merid_east = pair(EDGE_STATE[0] + 3 * levels, row)
        east_factor = ADVECT_HALF * zonal + DIFFUSE
        west_factor = ADVECT_HALF * zonal_west - DIFFUSE
        corner = jnp.where((lane == 32) | (lane == 96), merid_west, 0.0)
        corner = jnp.where((lane == 31) | (lane == 95), merid_east, corner)
        for tracer in range(2):
            west, east = pair(EDGE_MASKED + tracer * levels, row)
            at_masked = layout.masked + tracer * levels
            at_part = layout.part + tracer * levels
            masked = draft_ref[at_masked : at_masked + levels]
            face = jnp.where(lane == LANES - 1, east_factor * (east - masked), 0.0)
            face = jnp.where(lane == 0, west_factor * (masked - west), face)
            draft_ref[at_part : at_part + levels] = draft_ref[at_part : at_part + levels] + face
            corner = jnp.where(lane == (0, LANES // 2)[tracer], west, corner)
            corner = jnp.where(lane == (LANES - 1, LANES // 2 - 1)[tracer], east, corner)
        draft_ref[layout.corner : layout.corner + levels] = corner
        begin = 0 if row else levels
        pack_ref[begin : begin + levels] = corner

    @pl.when(odd_band)
    def _():
        near_ref[...] = bot_ref[...].astype(jnp.bfloat16)
        far_ref[...] = top_ref[...].astype(jnp.bfloat16)

    @pl.when(jnp.logical_not(odd_band))
    def _():
        near_ref[...] = top_ref[...].astype(jnp.bfloat16)
        far_ref[...] = bot_ref[...].astype(jnp.bfloat16)


class Tile:
    def __init__(self, levels, west_ref, east_ref, state_ref):
        self.levels = levels
        self.west_ref, self.east_ref, self.state_ref = west_ref, east_ref, state_ref
        self.shape = (ROWS, LANES)
        lane, row = lanes_of(self.shape), rows_of(self.shape)
        self.first_lane, self.last_lane = lane == 0, lane == LANES - 1
        self.bottom_row, self.top_row = row == 0, row == ROWS - 1

    def spread(self, ref, index):
        return jnp.broadcast_to(ref[:, index : index + 1].astype(jnp.float32), self.shape)

    def line(self, ref, index):
        return jnp.broadcast_to(ref[index : index + 1], self.shape)

    def side(self, index):
        return jnp.where(
            self.first_lane, self.spread(self.west_ref, index), self.spread(self.east_ref, index)
        )

    def velocities(self, at, level):
        begin = at * FIELDS * self.levels
        zonal = tile_of(self.state_ref, begin + 2 * self.levels + level)
        merid = tile_of(self.state_ref, begin + 3 * self.levels + level)
        zonal_west = jnp.where(
            self.first_lane,
            self.spread(self.west_ref, EDGE_STATE[at] + 2 * self.levels + level),
            shift(zonal, 1, 1),
        )
        return ADVECT_HALF * zonal, ADVECT_HALF * zonal_west, merid

    def tracer(self, at, level, tracer):
        field = tile_of(self.state_ref, (at * FIELDS + tracer) * self.levels + level)
        east = jnp.where(
            self.last_lane,
            self.spread(self.east_ref, EDGE_STATE[at] + tracer * self.levels + level),
            shift(field, -1, 1),
        )
        return field, east


def tile_of(ref, index):
    return ref[index * ROWS : (index + 1) * ROWS]


def first_step_kernel(
    west_ref,
    east_ref,
    state_ref,
    masked_ref,
    base_ref,
    bottom_ref,
    next_ref,
    side_ref,
    velocity_ref,
):
    levels = masked_ref.shape[0] // (2 * ROWS)
    tile = Tile(levels, west_ref, east_ref, state_ref)
    first_lane, last_lane = tile.first_lane, tile.last_lane
    top_row, bottom_row = tile.top_row, tile.bottom_row
    bottom = bottom_ref[...]
    side_bottom = tile.side(EDGE_MASKED + 2 * levels)
    for level in range(levels):
        zonal, zonal_west, merid = tile.velocities(0, level)
        north_factor = ADVECT_HALF * merid + DIFFUSE
        south_factor = ADVECT_HALF * shift(merid, 1, 0) - DIFFUSE
        side_merid = tile.side(EDGE_STATE[0] + 3 * levels + level)
        side_north = ADVECT_HALF * side_merid + DIFFUSE
        side_south = ADVECT_HALF * shift(side_merid, 1, 0) - DIFFUSE
        zonal_total = jnp.zeros(tile.shape, jnp.float32)
        merid_total = jnp.zeros(tile.shape, jnp.float32)
        for tracer in range(2):
            index = tracer * levels + level
            masked = tile_of(masked_ref, index)
            west = tile.spread(west_ref, EDGE_MASKED + index)
            east = tile.spread(east_ref, EDGE_MASKED + index)
            side = jnp.where(first_lane, west, east)
            to_east = jnp.where(last_lane, east, shift(masked, -1, 1)) - masked
            to_west = masked - jnp.where(first_lane, west, shift(masked, 1, 1))
            to_north = jnp.where(top_row, 0.0, shift(masked, -1, 0) - masked)
            to_south = jnp.where(bottom_row, 0.0, masked - shift(masked, 1, 0))
            result = (
                tile_of(base_ref, index)
                + (zonal + DIFFUSE) * to_east
                + (zonal_west - DIFFUSE) * to_west
                + north_factor * to_north
                + south_factor * to_south
            )
            next_ref[index * ROWS : (index + 1) * ROWS] = jnp.where(level < bottom, result, 0.0)
            field, field_east = tile.tracer(0, level, tracer)
            zonal_total = zonal_total + (field + field_east) * to_east
            merid_total = merid_total + (field + shift(field, -1, 0)) * to_north
            face = jnp.where(
                first_lane,
                (zonal_west + DIFFUSE) * (masked - side),
                (zonal - DIFFUSE) * (side - masked),
            )
            upper = jnp.where(top_row, 0.0, shift(side, -1, 0) - side)
            lower = jnp.where(bottom_row, 0.0, side - shift(side, 1, 0))
            result = (
                tile.side(EDGE_PART + index) + face + side_north * upper + side_south * lower
            )
            side_ref[index * ROWS : (index + 1) * ROWS] = jnp.where(
                side_bottom > level, result, 0.0
            )
        velocity_ref[level * ROWS : (level + 1) * ROWS] = ADVECT_HALF * zonal_total
        velocity_ref[(levels + level) * ROWS : (levels + level + 1) * ROWS] = (
            ADVECT_HALF * merid_total
        )


def second_step_kernel(
    far_ref,
    near_ref,
    pack_ref,
    west_ref,
    east_ref,
    state_ref,
    masked_ref,
    kappa_ref,
    bottom_ref,
    next_in_ref,
    side_in_ref,
    velocity_in_ref,
    adjoint_ref,
    velocity_ref,
    next_ref,
    side_ref,
    north_ref,
    south_ref,
    ring_ref,
    total_ref,
):
    levels = masked_ref.shape[0] // (2 * ROWS)
    layout = Layout(levels)
    band = lax.axis_index("lat")
    odd_band = lax.rem(band, 2) == 1
    top_band = (band == lax.axis_size("lat") - 1).astype(jnp.int32)
    folded = top_band.astype(jnp.float32)
    open_south = jnp.where(band > 0, DIFFUSE, 0.0)
    square = (LANES, LANES)
    from_lane = rows_of(square)
    turned = from_lane + top_band * (LANES - 1 - 2 * from_lane)
    turn = jnp.where(lanes_of(square) == turned, 1.0, 0.0).astype(jnp.bfloat16)

    @pl.when(odd_band)
    def _():
        north_ref[...] = jnp.dot(far_ref[...], turn, preferred_element_type=jnp.float32)
        south_ref[...] = near_ref[...].astype(jnp.float32)

    @pl.when(jnp.logical_not(odd_band))
    def _():
        north_ref[...] = jnp.dot(near_ref[...], turn, preferred_element_type=jnp.float32)
        south_ref[...] = far_ref[...].astype(jnp.float32)

    for at in range(2):
        here = slice(layout.merid[at], layout.merid[at] + levels)
        north_ref[here] = north_ref[here] * folded

    def rows_at(ref, begin):
        return ref[begin : begin + levels]

    def unpacked(packed):
        return packed, shift(packed, LANES // 2, 1), shift(packed, 96, 1)

    level_of = rows_of((levels, LANES)).astype(jnp.float32)
    left = lanes_of((levels, LANES)) < LANES // 2

    def side_depth(row):
        spot = slice(EDGE_MASKED + 2 * levels, EDGE_MASKED + 2 * levels + 1)
        west = west_ref[...].astype(jnp.float32)[row : row + 1, spot]
        east = east_ref[...].astype(jnp.float32)[row : row + 1, spot]
        return jnp.where(left, west, east)

    def add_rows(ref, begin, value):
        here = pl.ds(begin, levels, stride=ROWS)
        ref[here, :] = ref[here, :] + value

    top = ROWS - 1
    depth = bottom_ref[...].astype(jnp.float32)
    top_merid = strided(state_ref, 3 * levels * ROWS + top, levels)
    north_merid = rows_at(north_ref, layout.merid[0])
    south_merid = rows_at(south_ref, layout.merid[0])
    top_factor = ADVECT_HALF * (top_merid - north_merid) + DIFFUSE
    bottom_factor = ADVECT_HALF * south_merid - open_south
    own_top = unpacked(rows_at(pack_ref, 0))
    own_bottom = unpacked(rows_at(pack_ref, levels))
    north_corner = unpacked(rows_at(north_ref, layout.corner))
    south_corner = unpacked(rows_at(south_ref, layout.corner))
    side_top_factor = ADVECT_HALF * (own_top[2] - folded * north_corner[2]) + DIFFUSE
    side_bottom_factor = ADVECT_HALF * south_corner[2] - open_south
    merid_total = jnp.zeros((levels, LANES), jnp.float32)
    for tracer in range(2):
        start = tracer * levels * ROWS
        masked = strided(masked_ref, start + top, levels)
        beyond = rows_at(north_ref, layout.masked + tracer * levels)
        part = rows_at(north_ref, layout.part + tracer * levels)
        step = beyond - masked
        add_rows(
            next_ref, start + top, jnp.where(level_of < depth[top:], top_factor * step, 0.0)
        )
        ring = part - (ADVECT_HALF * (north_merid - top_merid) + DIFFUSE) * step
        wet = level_of < north_ref[layout.bottom : layout.bottom + 1]
        ring_ref[tracer * levels : (tracer + 1) * levels] = jnp.where(wet, ring, 0.0)
        field = strided(state_ref, start + top, levels)
        field_north = rows_at(north_ref, layout.tracer[0] + tracer * levels)
        merid_total = merid_total + (field + field_north) * step
        masked = strided(masked_ref, start, levels)
        beyond = rows_at(south_ref, layout.masked + tracer * levels)
        part = rows_at(south_ref, layout.part + tracer * levels)
        step = masked - beyond
        add_rows(
            next_ref, start, jnp.where(level_of < depth[0:1], bottom_factor * step, 0.0)
        )
        ring = part + (ADVECT_HALF * south_merid + DIFFUSE) * step
        wet = level_of < south_ref[layout.bottom : layout.bottom + 1]
        ring_ref[(2 + tracer) * levels : (3 + tracer) * levels] = jnp.where(wet, ring, 0.0)
        face = side_top_factor * (north_corner[tracer] - own_top[tracer])
        add_rows(side_ref, start + top, jnp.where(level_of < side_depth(top), face, 0.0))
        face = side_bottom_factor * (own_bottom[tracer] - south_corner[tracer])
        add_rows(side_ref, start, jnp.where(level_of < side_depth(0), face, 0.0))
    total_ref[...] = merid_total

    tile = Tile(levels, west_ref, east_ref, state_ref)
    first_lane, last_lane = tile.first_lane, tile.last_lane
    top_row, bottom_row = tile.top_row, tile.bottom_row
    closed = (band == 0).astype(jnp.int32)
    spread_south = jnp.where(rows_of(tile.shape) >= closed, DIFFUSE, 0.0)
    for level in range(levels):
        zonal, zonal_west, merid = tile.velocities(1, level)
        merid_south = jnp.where(
            bottom_row, tile.line(south_ref, layout.merid[1] + level), shift(merid, 1, 0)
        )
        merid_net = merid - jnp.where(top_row, tile.line(north_ref, layout.merid[1] + level), 0.0)
        north_factor = ADVECT_HALF * merid_net + DIFFUSE
        south_factor = ADVECT_HALF * merid_south - spread_south
        zonal_total = jnp.zeros(tile.shape, jnp.float32)
        merid_total = jnp.zeros(tile.shape, jnp.float32)
        for tracer in range(2):
            index = tracer * levels + level
            masked = tile_of(next_ref, index)
            side = tile_of(side_ref, index)
            to_east = jnp.where(last_lane, side, shift(masked, -1, 1)) - masked
            to_west = masked - jnp.where(first_lane, side, shift(masked, 1, 1))
            to_north = jnp.where(top_row, tile.line(ring_ref, index), shift(masked, -1, 0)) - masked
            to_south = masked - jnp.where(
                bottom_row, tile.line(ring_ref, 2 * levels + index), shift(masked, 1, 0)
            )
            adjoint_ref[index * ROWS : (index + 1) * ROWS] = (
                mixed(next_ref, kappa_ref, tracer * levels * ROWS, level, levels)
                + (zonal + DIFFUSE) * to_east
                + (zonal_west - DIFFUSE) * to_west
                + north_factor * to_north
                + south_factor * to_south
            )
            field, field_east = tile.tracer(1, level, tracer)
            field_north = jnp.where(
                top_row,
                tile.line(north_ref, layout.tracer[1] + tracer * levels + level),
                shift(field, -1, 0),
            )
            zonal_total = zonal_total + (field + field_east) * to_east
            merid_total = merid_total + (field + field_north) * to_north
        merid_total = merid_total + jnp.where(top_row, tile.line(total_ref, level), 0.0)
        for total, begin in ((zonal_total, 0), (merid_total, levels)):
            here = slice((begin + level) * ROWS, (begin + level + 1) * ROWS)
            velocity_ref[here] = velocity_in_ref[here] + ADVECT_HALF * total


def swaps(pairs):
    return [pair for low, high in pairs for pair in ((low, high), (high, low))]


def ring_routes(tiles):
    inner = swaps((tile, tile + 1) for tile in range(0, tiles, 2))
    outer = swaps((tile, (tile + 1) % tiles) for tile in range(1, tiles, 2))
    return inner, outer


def line_routes(tiles, bands):
    near, far = [], []
    for tile in range(tiles):
        start = tile * bands
        near += [(start + band, start + band + 1) for band in range(0, bands, 2)]
        far += [(start + band, start + band + 1) for band in range(1, bands - 1, 2)]
        if tile < tiles // 2:
            far.append((start + bands - 1, (tiles - tile) * bands - 1))
    return swaps(near), swaps(far)


def call(kernel, outputs, scratch, scalars, arrays, aliases=None):
    vmem = pl.BlockSpec(memory_space=pltpu.VMEM)
    smem = pl.BlockSpec(memory_space=pltpu.SMEM)
    return pl.pallas_call(
        kernel,
        out_shape=[jax.ShapeDtypeStruct(shape, dtype) for shape, dtype in outputs],
        in_specs=[smem] * len(scalars) + [vmem] * len(arrays),
        out_specs=[vmem] * len(outputs),
        scratch_shapes=[pltpu.VMEM(shape, jnp.float32) for shape in scratch],
        input_output_aliases=aliases or {},
        compiler_params=pltpu.CompilerParams(vmem_limit_bytes=32 * 1024 * 1024),
    )(*scalars, *arrays)


def shards(final_adjoint, store, holder_offset, holder_slot, bottom_level, mix_class, mix_table):
    bands = lax.axis_size("lat")
    tiles = lax.axis_size("lon")
    levels = final_adjoint.shape[1]
    slots = store.shape[2]
    steps = len(STEP_ORDER)
    pieces = FIELDS * levels
    full = levels * ROWS
    layout = Layout(levels)
    narrow, wide = jnp.bfloat16, jnp.float32
    hbm = pl.BlockSpec(memory_space=pltpu.HBM)
    request = pl.pallas_call(
        request_kernel,
        out_shape=jax.ShapeDtypeStruct((bands, steps, pieces, LANES), narrow),
        in_specs=[hbm, hbm],
        out_specs=hbm,
        scratch_shapes=[
            pltpu.SMEM(holder_slot.shape, jnp.int32),
            pltpu.VMEM((pieces * slots, LANES), narrow),
            pltpu.VMEM((pieces * slots, LANES), wide),
            pltpu.VMEM((bands, steps, pieces, LANES), narrow),
            pltpu.SemaphoreType.DMA,
            pltpu.SemaphoreType.DMA((FIELDS,)),
            pltpu.SemaphoreType.DMA((bands,)),
        ],
        compiler_params=pltpu.CompilerParams(vmem_limit_bytes=32 * 1024 * 1024),
    )(
        pltpu.with_memory_space_constraint(holder_slot, pltpu.HBM),
        pltpu.with_memory_space_constraint(store.reshape(pieces * slots, LANES), pltpu.HBM),
    )
    received = lax.all_to_all(request, "lat", split_axis=0, concat_axis=0, tiled=True)
    masked, base, kappa, side, pick = call(
        prepare_kernel,
        [
            ((2 * full, LANES), wide),
            ((2 * full, LANES), wide),
            ((full + ROWS, LANES), wide),
            ((4 * ROWS, 2 * LANES), wide),
            ((ROWS * LANES, LANES), narrow),
        ],
        [(2 * LANES, LANES)],
        [mix_table],
        [
            final_adjoint.reshape(2 * full, LANES),
            bottom_level,
            mix_class.reshape((levels - 1) * ROWS, LANES),
        ],
    )
    outer, inner = call(
        edges_kernel,
        [((ROWS, EDGE_LANES), narrow), ((ROWS, EDGE_LANES), narrow)],
        [(EDGE_MASKED, LANES)],
        [holder_offset],
        [received, side, pick],
    )
    inner_routes, outer_routes = ring_routes(tiles)
    near_routes, far_routes = line_routes(tiles, bands)
    outer = lax.ppermute(outer, "lon", outer_routes)
    inner = lax.ppermute(inner, "lon", inner_routes)
    top, bot = call(
        drafts_kernel,
        [((layout.rows, LANES), wide), ((layout.rows, LANES), wide)],
        [(5 * pieces, LANES)],
        [holder_offset],
        [received, masked, base, bottom_level],
    )
    far, near, west, east, pack = call(
        functools.partial(complete_kernel, levels),
        [
            ((layout.rows, LANES), narrow),
            ((layout.rows, LANES), narrow),
            ((ROWS, EDGE_LANES), narrow),
            ((ROWS, EDGE_LANES), narrow),
            ((2 * levels, LANES), wide),
        ],
        [(LANES, EDGE_LANES), (EDGE_LANES, LANES), (layout.rows, LANES), (layout.rows, LANES)],
        [],
        [outer, inner, top, bot],
    )
    far = lax.ppermute(far, ("lon", "lat"), far_routes)
    near = lax.ppermute(near, ("lon", "lat"), near_routes)
    (state,) = call(
        tiles_kernel,
        [((steps * FIELDS * full, LANES), wide)],
        [],
        [holder_offset],
        [received, west],
    )
    following, beside, velocity = call(
        first_step_kernel,
        [((2 * full, LANES), wide)] * 3,
        [],
        [],
        [west, east, state, masked, base, bottom_level],
    )
    adjoint, velocity, _, _ = call(
        second_step_kernel,
        [((2 * full, LANES), wide)] * 4,
        [
            (layout.rows, LANES),
            (layout.rows, LANES),
            (4 * levels, LANES),
            (levels, LANES),
        ],
        [],
        [
            far,
            near,
            pack,
            west,
            east,
            state,
            masked,
            kappa,
            bottom_level,
            following,
            beside,
            velocity,
        ],
        {9: 2, 10: 3},
    )
    shape = (2, levels, ROWS, LANES)
    return adjoint.reshape(shape), velocity.reshape(shape)


def solution(mesh):
    return jax.shard_map(
        shards,
        mesh=mesh,
        in_specs=(
            P(None, None, "lat", "lon"),
            P(None, None, None, "lat", "lon"),
            P(),
            P(),
            P("lat", "lon"),
            P(None, "lat", "lon"),
            P(),
        ),
        out_specs=(P(None, None, "lat", "lon"), P(None, None, "lat", "lon")),
        check_vma=False,
    )
```

```python
import functools

import jax
import jax.numpy as jnp
from jax import lax
from jax.experimental import pallas as pl
from jax.experimental.pallas import tpu as pltpu
from jax.sharding import PartitionSpec as P

STEP_ORDER = (1, 0)
FIELDS = 4
ADVECT_HALF = 0.125
DIFFUSE = 0.1

ROWS = 8
LANES = 128

EDGE_STATE = (0, 256)
EDGE_MASKED = 512
EDGE_PART = 640
EDGE_LANES = 768


class Layout:
    def __init__(self, levels):
        self.tracer = (0, 3 * levels)
        self.merid = (2 * levels, 5 * levels)
        self.masked = 6 * levels
        self.part = 8 * levels
        self.corner = 10 * levels
        self.bottom = 11 * levels
        self.rows = (11 * levels + 1 + 15) // 16 * 16


def shift(block, amount, axis):
    return pltpu.roll(block, amount % block.shape[axis], axis)


def lanes_of(shape):
    return lax.broadcasted_iota(jnp.int32, shape, 1)


def rows_of(shape):
    return lax.broadcasted_iota(jnp.int32, shape, 0)


def strided(ref, start, count):
    return ref[pl.ds(start, count, stride=ROWS), :]


def request_kernel(
    slot_hbm, store_hbm, out_hbm, slot_ref, store_ref, wide_ref, pack_ref, slot_sem, in_sem, out_sem
):
    tile = lax.axis_index("lon")
    bands, steps, pieces, lanes = pack_ref.shape
    slots = store_ref.shape[0] // pieces
    length = store_ref.shape[0] // FIELDS
    table = pltpu.make_async_copy(slot_hbm, slot_ref, slot_sem)
    table.start()
    loads = []
    for field in range(FIELDS):
        here = pl.ds(field * length, length)
        load = pltpu.make_async_copy(store_hbm.at[here], store_ref.at[here], in_sem.at[field])
        load.start()
        loads.append(load)
    for field, load in enumerate(loads):
        load.wait()
        here = slice(field * length, (field + 1) * length)
        wide_ref[here] = store_ref[here].astype(jnp.float32)
    table.wait()
    stores = []
    for band in range(bands):
        for at, step in enumerate(STEP_ORDER):
            slot = slot_ref[step, band, tile]
            rows = wide_ref[pl.ds(slot, pieces, stride=slots), :]
            pack_ref[band, at] = rows.astype(jnp.bfloat16)
        store = pltpu.make_async_copy(pack_ref.at[band], out_hbm.at[band], out_sem.at[band])
        store.start()
        stores.append(store)
    for store in stores:
        store.wait()


def pick_columns(offset=0):
    place = (ROWS * LANES, LANES)
    row, source = rows_of(place) // LANES, rows_of(place) % LANES
    order = lanes_of(place) - (row + ROWS - offset) % ROWS
    chosen = (
        ((source == 0) & (order == 0))
        | ((source == LANES - 1) & (order == ROWS))
        | ((source == 1) & (order == 2 * ROWS))
        | ((source == LANES - 2) & (order == 3 * ROWS))
    )
    return jnp.where(chosen, 1.0, 0.0).astype(jnp.bfloat16)


def prepare_kernel(
    table_ref,
    offset_ref,
    adjoint_ref,
    bottom_ref,
    mix_ref,
    masked_ref,
    base_ref,
    kappa_ref,
    side_ref,
    pick_ref,
    column_ref,
):
    levels = adjoint_ref.shape[0] // (2 * ROWS)
    bottom = bottom_ref[...]
    edge = jnp.zeros((ROWS, LANES), jnp.float32)
    kappa_ref[0:ROWS] = edge
    kappa_ref[levels * ROWS : (levels + 1) * ROWS] = edge
    for level in range(levels - 1):
        classes = mix_ref[level * ROWS : (level + 1) * ROWS]
        kappa = jnp.full((ROWS, LANES), table_ref[0], jnp.float32)
        for index in range(1, table_ref.shape[0]):
            kappa = jnp.where(classes == index, table_ref[index], kappa)
        kappa_ref[(level + 1) * ROWS : (level + 2) * ROWS] = kappa
    for tracer in range(2):
        start = tracer * levels * ROWS
        for level in range(levels):
            here = slice(start + level * ROWS, start + (level + 1) * ROWS)
            masked_ref[here] = jnp.where(level < bottom, adjoint_ref[here], 0.0)
        for level in range(levels):
            base_ref[start + level * ROWS : start + (level + 1) * ROWS] = mixed(
                masked_ref, kappa_ref, start, level, levels
            )
    pick = pick_columns()
    for at, step in enumerate(STEP_ORDER):
        pick_ref[at] = pick_columns(offset_ref[step, lax.axis_index("lat"), lax.axis_index("lon")])
    column_ref[...] = jnp.zeros_like(column_ref)
    rows = 2 * levels
    for start, ref in ((0, masked_ref), (LANES, base_ref)):
        blocks = [strided(ref, row, rows).astype(jnp.bfloat16) for row in range(ROWS)]
        column_ref[start : start + rows] = jnp.dot(
            jnp.concatenate(blocks, axis=1), pick, preferred_element_type=jnp.float32
        )
    side = jnp.transpose(column_ref[...])[0 : 4 * ROWS]
    spot = lanes_of((ROWS, 2 * LANES)) == rows
    depth = bottom.astype(jnp.float32)
    side_ref[...] = side
    side_ref[0:ROWS] = jnp.where(spot, depth[:, 0:1], side[0:ROWS])
    side_ref[ROWS : 2 * ROWS] = jnp.where(spot, depth[:, LANES - 1 :], side[ROWS : 2 * ROWS])


def mixed(masked_ref, kappa_ref, start, level, levels):
    def at(index):
        return masked_ref[start + index * ROWS : start + (index + 1) * ROWS]

    masked = at(level)
    below = at(level + 1) if level + 1 < levels else jnp.zeros_like(masked)
    above = at(level - 1) if level > 0 else jnp.zeros_like(masked)
    kappa_above = kappa_ref[level * ROWS : (level + 1) * ROWS]
    kappa_below = kappa_ref[(level + 1) * ROWS : (level + 2) * ROWS]
    return masked + kappa_below * (below - masked) + kappa_above * (above - masked)


def edges_kernel(piece_ref, side_ref, pick_ref, outer_ref, inner_ref, column_ref):
    tile = lax.axis_index("lon")
    holders, steps, pieces, _ = piece_ref.shape
    levels = pieces // FIELDS
    column_ref[...] = jnp.zeros_like(column_ref)
    for at in range(steps):
        chunks = [piece_ref[holder, at] for holder in range(holders)]
        column_ref[EDGE_STATE[at] : EDGE_STATE[at] + pieces] = jnp.dot(
            jnp.concatenate(chunks, axis=1), pick_ref[at], preferred_element_type=jnp.float32
        )
    state = jnp.transpose(column_ref[...])
    lane = lanes_of((ROWS, 2 * LANES))
    sides = []
    for at, sign in ((0, 1.0), (1, -1.0)):
        edge = state[at * ROWS : (at + 1) * ROWS]
        zonal = edge if at == 0 else state[3 * ROWS : 4 * ROWS]
        zonal = zonal[:, 0 : 2 * LANES]
        zonal = jnp.where(lane < levels, shift(zonal, -2 * levels, 1), shift(zonal, -levels, 1))
        masked = side_ref[at * ROWS : (at + 1) * ROWS]
        beside = side_ref[(at + 2) * ROWS : (at + 3) * ROWS]
        face = (ADVECT_HALF * zonal + sign * DIFFUSE) * (sign * (beside - masked))
        part = masked[:, LANES:] + face[:, 0:LANES]
        side = jnp.concatenate([edge, masked[:, 0:LANES], part], axis=1)
        sides.append(side.astype(jnp.bfloat16))
    to_west, to_east = sides

    @pl.when(lax.rem(tile, 2) == 0)
    def _():
        inner_ref[...] = to_east
        outer_ref[...] = to_west

    @pl.when(lax.rem(tile, 2) == 1)
    def _():
        inner_ref[...] = to_west
        outer_ref[...] = to_east


def tiles_kernel(offset_ref, piece_ref, west_ref, state_ref):
    tile = lax.axis_index("lon")
    band = lax.axis_index("lat")
    holders, _, pieces, _ = piece_ref.shape
    for at, step in enumerate(STEP_ORDER):
        offset = offset_ref[step, band, tile]
        for row in range(ROWS):
            chunk = piece_ref[lax.rem(row + offset, holders), at]
            state_ref[pl.ds(at * pieces * ROWS + row, pieces, stride=ROWS), :] = chunk.astype(
                jnp.float32
            )


def drafts_kernel(
    offset_ref, piece_ref, masked_ref, base_ref, bottom_ref, top_ref, bot_ref, line_ref
):
    tile = lax.axis_index("lon")
    band = lax.axis_index("lat")
    levels = masked_ref.shape[0] // (2 * ROWS)
    pieces = FIELDS * levels
    holders = piece_ref.shape[0]
    for slot, (row, at) in enumerate(((ROWS - 1, 0), (ROWS - 1, 1), (0, 0), (0, 1), (ROWS - 2, 0))):
        offset = offset_ref[STEP_ORDER[at], band, tile]
        chunk = piece_ref[lax.rem(row + offset, holders), at]
        line_ref[slot * pieces : (slot + 1) * pieces] = chunk.astype(jnp.float32)
    bottom = bottom_ref[...].astype(jnp.float32)
    layout = Layout(levels)
    wide = lanes_of((levels, LANES))
    for row, inner, first, facing, draft_ref in (
        (ROWS - 1, ROWS - 2, 0, 4, top_ref),
        (0, 1, 2, 2, bot_ref),
    ):
        for at in range(2):
            begin = (first + at) * pieces
            draft_ref[layout.tracer[at] : layout.tracer[at] + 2 * levels] = line_ref[
                begin : begin + 2 * levels
            ]
            draft_ref[layout.merid[at] : layout.merid[at] + levels] = line_ref[
                begin + 3 * levels : begin + 4 * levels
            ]
        zonal = line_ref[first * pieces + 2 * levels : first * pieces + 3 * levels]
        merid = line_ref[facing * pieces + 3 * levels : facing * pieces + 4 * levels]
        east_factor = ADVECT_HALF * zonal + DIFFUSE
        west_factor = ADVECT_HALF * shift(zonal, 1, 1) - DIFFUSE
        for tracer in range(2):
            begin = tracer * levels * ROWS
            masked = strided(masked_ref, begin + row, levels)
            next_row = strided(masked_ref, begin + inner, levels)
            if row > inner:
                along = (ADVECT_HALF * merid - DIFFUSE) * (masked - next_row)
            else:
                along = (ADVECT_HALF * merid + DIFFUSE) * (next_row - masked)
            east = east_factor * (shift(masked, -1, 1) - masked)
            west = west_factor * (masked - shift(masked, 1, 1))
            part = strided(base_ref, begin + row, levels) + along
            part = part + jnp.where(wide < LANES - 1, east, 0.0) + jnp.where(wide > 0, west, 0.0)
            at_masked = layout.masked + tracer * levels
            at_part = layout.part + tracer * levels
            draft_ref[at_masked : at_masked + levels] = masked
            draft_ref[at_part : at_part + levels] = part
        draft_ref[layout.corner : layout.corner + levels] = zonal
        draft_ref[layout.bottom : layout.rows] = jnp.broadcast_to(
            bottom[row : row + 1], (layout.rows - layout.bottom, LANES)
        )


def complete_kernel(
    levels,
    outer_ref,
    inner_ref,
    top_draft_ref,
    bot_draft_ref,
    far_ref,
    near_ref,
    west_ref,
    east_ref,
    pack_ref,
    edge_ref,
    column_ref,
    top_ref,
    bot_ref,
):
    layout = Layout(levels)
    odd_tile = lax.rem(lax.axis_index("lon"), 2) == 1
    odd_band = lax.rem(lax.axis_index("lat"), 2) == 1

    @pl.when(odd_tile)
    def _():
        west_ref[...] = inner_ref[...]
        east_ref[...] = outer_ref[...]

    @pl.when(jnp.logical_not(odd_tile))
    def _():
        west_ref[...] = outer_ref[...]
        east_ref[...] = inner_ref[...]

    top_ref[...] = top_draft_ref[...]
    bot_ref[...] = bot_draft_ref[...]
    edge_ref[...] = jnp.zeros_like(edge_ref)
    edge_ref[0:ROWS] = west_ref[...].astype(jnp.float32)
    edge_ref[ROWS : 2 * ROWS] = east_ref[...].astype(jnp.float32)
    column_ref[...] = jnp.transpose(edge_ref[...])
    lane = lanes_of((levels, LANES))

    def pair(start, row):
        block = column_ref[start : start + levels]
        return block[:, row : row + 1], block[:, ROWS + row : ROWS + row + 1]

    for row, draft_ref in ((ROWS - 1, top_ref), (0, bot_ref)):
        zonal = draft_ref[layout.corner : layout.corner + levels]
        zonal_west, _ = pair(EDGE_STATE[0] + 2 * levels, row)
        merid_west, merid_east = pair(EDGE_STATE[0] + 3 * levels, row)
        east_factor = ADVECT_HALF * zonal + DIFFUSE
        west_factor = ADVECT_HALF * zonal_west - DIFFUSE
        corner = jnp.where((lane == 32) | (lane == 96), merid_west, 0.0)
        corner = jnp.where((lane == 31) | (lane == 95), merid_east, corner)
        for tracer in range(2):
            west, east = pair(EDGE_MASKED + tracer * levels, row)
            at_masked = layout.masked + tracer * levels
            at_part = layout.part + tracer * levels
            masked = draft_ref[at_masked : at_masked + levels]
            face = jnp.where(lane == LANES - 1, east_factor * (east - masked), 0.0)
            face = jnp.where(lane == 0, west_factor * (masked - west), face)
            draft_ref[at_part : at_part + levels] = draft_ref[at_part : at_part + levels] + face
            corner = jnp.where(lane == (0, LANES // 2)[tracer], west, corner)
            corner = jnp.where(lane == (LANES - 1, LANES // 2 - 1)[tracer], east, corner)
        draft_ref[layout.corner : layout.corner + levels] = corner
        begin = 0 if row else 4 * levels
        pack_ref[begin : begin + levels] = corner
        zonal_west, _ = pair(EDGE_STATE[1] + 2 * levels, row)
        pack_ref[begin + levels : begin + 2 * levels] = jnp.broadcast_to(
            zonal_west, (levels, LANES)
        )
        for tracer in range(2):
            _, east = pair(EDGE_STATE[1] + tracer * levels, row)
            here = begin + (2 + tracer) * levels
            pack_ref[here : here + levels] = jnp.broadcast_to(east, (levels, LANES))

    @pl.when(odd_band)
    def _():
        near_ref[...] = bot_ref[...].astype(jnp.bfloat16)
        far_ref[...] = top_ref[...].astype(jnp.bfloat16)

    @pl.when(jnp.logical_not(odd_band))
    def _():
        near_ref[...] = top_ref[...].astype(jnp.bfloat16)
        far_ref[...] = bot_ref[...].astype(jnp.bfloat16)


class Tile:
    def __init__(self, levels, west_ref, east_ref, state_ref):
        self.levels = levels
        self.west_ref, self.east_ref, self.state_ref = west_ref, east_ref, state_ref
        self.shape = (ROWS, LANES)
        lane, row = lanes_of(self.shape), rows_of(self.shape)
        self.first_lane, self.last_lane = lane == 0, lane == LANES - 1
        self.bottom_row, self.top_row = row == 0, row == ROWS - 1

    def spread(self, ref, index):
        return jnp.broadcast_to(ref[:, index : index + 1].astype(jnp.float32), self.shape)

    def line(self, ref, index):
        return jnp.broadcast_to(ref[index : index + 1], self.shape)

    def side(self, index):
        return jnp.where(
            self.first_lane, self.spread(self.west_ref, index), self.spread(self.east_ref, index)
        )

    def velocities(self, at, level):
        begin = at * FIELDS * self.levels
        zonal = tile_of(self.state_ref, begin + 2 * self.levels + level)
        merid = tile_of(self.state_ref, begin + 3 * self.levels + level)
        zonal_west = jnp.where(
            self.first_lane,
            self.spread(self.west_ref, EDGE_STATE[at] + 2 * self.levels + level),
            shift(zonal, 1, 1),
        )
        return ADVECT_HALF * zonal, ADVECT_HALF * zonal_west, merid

    def tracer(self, at, level, tracer):
        field = tile_of(self.state_ref, (at * FIELDS + tracer) * self.levels + level)
        east = jnp.where(
            self.last_lane,
            self.spread(self.east_ref, EDGE_STATE[at] + tracer * self.levels + level),
            shift(field, -1, 1),
        )
        return field, east


def tile_of(ref, index):
    return ref[index * ROWS : (index + 1) * ROWS]


def steps_kernel(
    west_ref,
    east_ref,
    state_ref,
    masked_ref,
    base_ref,
    kappa_ref,
    bottom_ref,
    adjoint_ref,
    velocity_ref,
    next_ref,
    side_ref,
):
    levels = masked_ref.shape[0] // (2 * ROWS)
    tile = Tile(levels, west_ref, east_ref, state_ref)
    first_lane, last_lane = tile.first_lane, tile.last_lane
    top_row, bottom_row = tile.top_row, tile.bottom_row
    bottom = bottom_ref[...]
    side_bottom = tile.side(EDGE_MASKED + 2 * levels)
    for level in range(levels):
        zonal, zonal_west, merid = tile.velocities(0, level)
        north_factor = ADVECT_HALF * merid + DIFFUSE
        south_factor = ADVECT_HALF * shift(merid, 1, 0) - DIFFUSE
        side_merid = tile.side(EDGE_STATE[0] + 3 * levels + level)
        side_north = ADVECT_HALF * side_merid + DIFFUSE
        side_south = ADVECT_HALF * shift(side_merid, 1, 0) - DIFFUSE
        zonal_total = jnp.zeros(tile.shape, jnp.float32)
        merid_total = jnp.zeros(tile.shape, jnp.float32)
        for tracer in range(2):
            index = tracer * levels + level
            masked = tile_of(masked_ref, index)
            west = tile.spread(west_ref, EDGE_MASKED + index)
            east = tile.spread(east_ref, EDGE_MASKED + index)
            side = jnp.where(first_lane, west, east)
            to_east = jnp.where(last_lane, east, shift(masked, -1, 1)) - masked
            to_west = masked - jnp.where(first_lane, west, shift(masked, 1, 1))
            to_north = jnp.where(top_row, 0.0, shift(masked, -1, 0) - masked)
            to_south = jnp.where(bottom_row, 0.0, masked - shift(masked, 1, 0))
            result = (
                tile_of(base_ref, index)
                + (zonal + DIFFUSE) * to_east
                + (zonal_west - DIFFUSE) * to_west
                + north_factor * to_north
                + south_factor * to_south
            )
            next_ref[index * ROWS : (index + 1) * ROWS] = jnp.where(level < bottom, result, 0.0)
            field, field_east = tile.tracer(0, level, tracer)
            zonal_total = zonal_total + (field + field_east) * to_east
            merid_total = merid_total + (field + shift(field, -1, 0)) * to_north
            face = jnp.where(
                first_lane,
                (zonal_west + DIFFUSE) * (masked - side),
                (zonal - DIFFUSE) * (side - masked),
            )
            upper = jnp.where(top_row, 0.0, shift(side, -1, 0) - side)
            lower = jnp.where(bottom_row, 0.0, side - shift(side, 1, 0))
            result = (
                tile.side(EDGE_PART + index) + face + side_north * upper + side_south * lower
            )
            side_ref[index * ROWS : (index + 1) * ROWS] = jnp.where(
                side_bottom > level, result, 0.0
            )
        velocity_ref[level * ROWS : (level + 1) * ROWS] = ADVECT_HALF * zonal_total
        velocity_ref[(levels + level) * ROWS : (levels + level + 1) * ROWS] = (
            ADVECT_HALF * merid_total
        )

    for level in range(levels):
        zonal, zonal_west, merid = tile.velocities(1, level)
        north_factor = ADVECT_HALF * merid + DIFFUSE
        south_factor = ADVECT_HALF * shift(merid, 1, 0) - DIFFUSE
        zonal_total = jnp.zeros(tile.shape, jnp.float32)
        merid_total = jnp.zeros(tile.shape, jnp.float32)
        for tracer in range(2):
            index = tracer * levels + level
            masked = tile_of(next_ref, index)
            side = tile_of(side_ref, index)
            to_east = jnp.where(last_lane, side, shift(masked, -1, 1)) - masked
            to_west = masked - jnp.where(first_lane, side, shift(masked, 1, 1))
            to_north = jnp.where(top_row, 0.0, shift(masked, -1, 0) - masked)
            to_south = jnp.where(bottom_row, 0.0, masked - shift(masked, 1, 0))
            adjoint_ref[index * ROWS : (index + 1) * ROWS] = (
                mixed(next_ref, kappa_ref, tracer * levels * ROWS, level, levels)
                + (zonal + DIFFUSE) * to_east
                + (zonal_west - DIFFUSE) * to_west
                + north_factor * to_north
                + south_factor * to_south
            )
            field, field_east = tile.tracer(1, level, tracer)
            zonal_total = zonal_total + (field + field_east) * to_east
            merid_total = merid_total + (field + shift(field, -1, 0)) * to_north
        for total, begin in ((zonal_total, 0), (merid_total, levels)):
            here = slice((begin + level) * ROWS, (begin + level + 1) * ROWS)
            velocity_ref[here] = velocity_ref[here] + ADVECT_HALF * total


def finish_kernel(
    far_ref,
    near_ref,
    pack_ref,
    west_ref,
    east_ref,
    state_ref,
    masked_ref,
    kappa_ref,
    bottom_ref,
    next_ref,
    adjoint_in_ref,
    velocity_in_ref,
    adjoint_ref,
    velocity_ref,
    north_ref,
    south_ref,
    guard_ref,
):
    levels = masked_ref.shape[0] // (2 * ROWS)
    layout = Layout(levels)
    top = ROWS - 1
    band = lax.axis_index("lat")
    odd_band = lax.rem(band, 2) == 1
    top_band = (band == lax.axis_size("lat") - 1).astype(jnp.int32)
    folded = top_band.astype(jnp.float32)
    open_south = jnp.where(band > 0, DIFFUSE, 0.0)
    square = (LANES, LANES)
    from_lane = rows_of(square)
    turned = from_lane + top_band * (LANES - 1 - 2 * from_lane)
    turn = jnp.where(lanes_of(square) == turned, 1.0, 0.0).astype(jnp.bfloat16)

    @pl.when(odd_band)
    def _():
        north_ref[...] = jnp.dot(far_ref[...], turn, preferred_element_type=jnp.float32)
        south_ref[...] = near_ref[...].astype(jnp.float32)

    @pl.when(jnp.logical_not(odd_band))
    def _():
        north_ref[...] = jnp.dot(near_ref[...], turn, preferred_element_type=jnp.float32)
        south_ref[...] = far_ref[...].astype(jnp.float32)

    adjoint_ref[...] = adjoint_in_ref[...]
    velocity_ref[...] = velocity_in_ref[...]
    guard_ref[...] = jnp.zeros_like(guard_ref)

    def rows_at(ref, begin):
        return ref[begin : begin + levels]

    def unpacked(packed):
        return packed, shift(packed, LANES // 2, 1), shift(packed, 96, 1)

    def state_row(at, field, row):
        return strided(state_ref, (at * FIELDS + field) * levels * ROWS + row, levels)

    def add_rows(ref, begin, value):
        here = pl.ds(begin, levels, stride=ROWS)
        ref[here, :] = ref[here, :] + value

    level_of = rows_of((levels, LANES)).astype(jnp.float32)
    lane = lanes_of((levels, LANES))
    first_lane, last_lane = lane == 0, lane == LANES - 1

    def side_depth(row):
        spot = slice(EDGE_MASKED + 2 * levels, EDGE_MASKED + 2 * levels + 1)
        west = west_ref[...].astype(jnp.float32)[row : row + 1, spot]
        east = east_ref[...].astype(jnp.float32)[row : row + 1, spot]
        return jnp.where(lane < LANES // 2, west, east)

    depth = bottom_ref[...].astype(jnp.float32)
    merid_top = state_row(0, 3, top)
    north_merid = rows_at(north_ref, layout.merid[0]) * folded
    south_merid = rows_at(south_ref, layout.merid[0])
    top_factor = ADVECT_HALF * (merid_top - north_merid) + DIFFUSE
    bottom_factor = ADVECT_HALF * south_merid - open_south
    own_corner = (unpacked(rows_at(pack_ref, 4 * levels)), unpacked(rows_at(pack_ref, 0)))
    north_corner = unpacked(rows_at(north_ref, layout.corner))
    south_corner = unpacked(rows_at(south_ref, layout.corner))
    side_top = ADVECT_HALF * (own_corner[1][2] - folded * north_corner[2]) + DIFFUSE
    side_bottom = ADVECT_HALF * south_corner[2] - open_south

    merids = {row: state_row(1, 3, row) for row in (0, top - 1, top)}
    next_north = ADVECT_HALF * (merids[top] - folded * rows_at(north_ref, layout.merid[1])) + DIFFUSE
    next_south = ADVECT_HALF * rows_at(south_ref, layout.merid[1]) - open_south
    east_factors, west_factors, kappas = [], [], []
    for row, begin in ((0, 4 * levels), (top, 0)):
        zonal = state_row(1, 2, row)
        zonal_west = jnp.where(first_lane, rows_at(pack_ref, begin + levels), shift(zonal, 1, 1))
        east_factors.append(ADVECT_HALF * zonal + DIFFUSE)
        west_factors.append(ADVECT_HALF * zonal_west - DIFFUSE)
        kappas.append(
            (strided(kappa_ref, row, levels), strided(kappa_ref, ROWS + row, levels))
        )

    zonal_totals = [jnp.zeros((levels, LANES), jnp.float32) for _ in range(2)]
    merid_totals = {row: jnp.zeros((levels, LANES), jnp.float32) for row in (0, top - 1, top)}
    for tracer in range(2):
        start = tracer * levels * ROWS
        own_top = strided(masked_ref, start + top, levels)
        own_bottom = strided(masked_ref, start, levels)
        north = rows_at(north_ref, layout.masked + tracer * levels)
        south = rows_at(south_ref, layout.masked + tracer * levels)
        north_step, south_step = north - own_top, own_bottom - south
        wet = level_of < north_ref[layout.bottom : layout.bottom + 1]
        ring_north = rows_at(north_ref, layout.part + tracer * levels)
        ring_north = ring_north - (ADVECT_HALF * (north_merid - merid_top) + DIFFUSE) * north_step
        ring_north = jnp.where(wet, ring_north, 0.0)
        wet = level_of < south_ref[layout.bottom : layout.bottom + 1]
        ring_south = rows_at(south_ref, layout.part + tracer * levels)
        ring_south = ring_south + (ADVECT_HALF * south_merid + DIFFUSE) * south_step
        ring_south = jnp.where(wet, ring_south, 0.0)
        first_field = state_row(0, tracer, top) + rows_at(
            north_ref, layout.tracer[0] + tracer * levels
        )
        merid_totals[top] = merid_totals[top] + first_field * north_step
        changes = (
            jnp.where(level_of < depth[0:1], bottom_factor * south_step, 0.0),
            jnp.where(level_of < depth[top:], top_factor * north_step, 0.0),
        )
        side_changes = (
            side_bottom * (own_corner[0][tracer] - south_corner[tracer]),
            side_top * (north_corner[tracer] - own_corner[1][tracer]),
        )
        fields = {row: state_row(1, tracer, row) for row in (0, 1, top - 1, top)}
        for at, row in enumerate((0, top)):
            change = changes[at]
            side = jnp.where(level_of < side_depth(row), side_changes[at], 0.0)
            guard_ref[ROWS : ROWS + levels] = change
            above = guard_ref[ROWS - 1 : ROWS - 1 + levels]
            below = guard_ref[ROWS + 1 : ROWS + 1 + levels]
            kappa_above, kappa_below = kappas[at]
            to_east = jnp.where(last_lane, side, shift(change, -1, 1)) - change
            to_west = change - jnp.where(first_lane, side, shift(change, 1, 1))
            value = (
                change
                + kappa_below * (below - change)
                + kappa_above * (above - change)
                + east_factors[at] * to_east
                + west_factors[at] * to_west
            )
            begin = (4 * levels if row == 0 else 0) + (2 + tracer) * levels
            field_east = jnp.where(
                last_lane, rows_at(pack_ref, begin), shift(fields[row], -1, 1)
            )
            zonal_totals[at] = zonal_totals[at] + (fields[row] + field_east) * to_east
            full = strided(next_ref, start + row, levels) + change
            if row == 0:
                value = value - (ADVECT_HALF * merids[0] + DIFFUSE) * change
                value = value + next_south * (full - ring_south)
                add_rows(adjoint_ref, start + 1, -(ADVECT_HALF * merids[0] - DIFFUSE) * change)
                merid_totals[0] = merid_totals[0] - (fields[0] + fields[1]) * change
            else:
                value = value + (ADVECT_HALF * merids[top - 1] - DIFFUSE) * change
                value = value + next_north * (ring_north - full)
                inner = (ADVECT_HALF * merids[top - 1] + DIFFUSE) * change
                add_rows(adjoint_ref, start + top - 1, inner)
                merid_totals[top - 1] = (
                    merid_totals[top - 1] + (fields[top - 1] + fields[top]) * change
                )
                field_north = rows_at(north_ref, layout.tracer[1] + tracer * levels)
                merid_totals[top] = merid_totals[top] + (fields[top] + field_north) * (
                    ring_north - full
                )
            add_rows(adjoint_ref, start + row, value)
    for at, row in enumerate((0, top)):
        add_rows(velocity_ref, row, ADVECT_HALF * zonal_totals[at])
    for row, total in merid_totals.items():
        add_rows(velocity_ref, levels * ROWS + row, ADVECT_HALF * total)


def swaps(pairs):
    return [pair for low, high in pairs for pair in ((low, high), (high, low))]


def ring_routes(tiles):
    inner = swaps((tile, tile + 1) for tile in range(0, tiles, 2))
    outer = swaps((tile, (tile + 1) % tiles) for tile in range(1, tiles, 2))
    return inner, outer


def line_routes(tiles, bands):
    near, far = [], []
    for tile in range(tiles):
        start = tile * bands
        near += [(start + band, start + band + 1) for band in range(0, bands, 2)]
        far += [(start + band, start + band + 1) for band in range(1, bands - 1, 2)]
        if tile < tiles // 2:
            far.append((start + bands - 1, (tiles - tile) * bands - 1))
    return swaps(near), swaps(far)


def call(kernel, outputs, scratch, scalars, arrays):
    vmem = pl.BlockSpec(memory_space=pltpu.VMEM)
    smem = pl.BlockSpec(memory_space=pltpu.SMEM)
    return pl.pallas_call(
        kernel,
        out_shape=[jax.ShapeDtypeStruct(shape, dtype) for shape, dtype in outputs],
        in_specs=[smem] * len(scalars) + [vmem] * len(arrays),
        out_specs=[vmem] * len(outputs),
        scratch_shapes=[pltpu.VMEM(shape, jnp.float32) for shape in scratch],
        compiler_params=pltpu.CompilerParams(vmem_limit_bytes=32 * 1024 * 1024),
    )(*scalars, *arrays)


def shards(final_adjoint, store, holder_offset, holder_slot, bottom_level, mix_class, mix_table):
    bands = lax.axis_size("lat")
    tiles = lax.axis_size("lon")
    levels = final_adjoint.shape[1]
    slots = store.shape[2]
    steps = len(STEP_ORDER)
    pieces = FIELDS * levels
    full = levels * ROWS
    layout = Layout(levels)
    narrow, wide = jnp.bfloat16, jnp.float32
    hbm = pl.BlockSpec(memory_space=pltpu.HBM)
    request = pl.pallas_call(
        request_kernel,
        out_shape=jax.ShapeDtypeStruct((bands, steps, pieces, LANES), narrow),
        in_specs=[hbm, hbm],
        out_specs=hbm,
        scratch_shapes=[
            pltpu.SMEM(holder_slot.shape, jnp.int32),
            pltpu.VMEM((pieces * slots, LANES), narrow),
            pltpu.VMEM((pieces * slots, LANES), wide),
            pltpu.VMEM((bands, steps, pieces, LANES), narrow),
            pltpu.SemaphoreType.DMA,
            pltpu.SemaphoreType.DMA((FIELDS,)),
            pltpu.SemaphoreType.DMA((bands,)),
        ],
        compiler_params=pltpu.CompilerParams(vmem_limit_bytes=32 * 1024 * 1024),
    )(
        pltpu.with_memory_space_constraint(holder_slot, pltpu.HBM),
        pltpu.with_memory_space_constraint(store.reshape(pieces * slots, LANES), pltpu.HBM),
    )
    received = lax.all_to_all(request, "lat", split_axis=0, concat_axis=0, tiled=True)
    masked, base, kappa, side, pick = call(
        prepare_kernel,
        [
            ((2 * full, LANES), wide),
            ((2 * full, LANES), wide),
            ((full + ROWS, LANES), wide),
            ((4 * ROWS, 2 * LANES), wide),
            ((steps, ROWS * LANES, LANES), narrow),
        ],
        [(2 * LANES, LANES)],
        [mix_table, holder_offset],
        [
            final_adjoint.reshape(2 * full, LANES),
            bottom_level,
            mix_class.reshape((levels - 1) * ROWS, LANES),
        ],
    )
    outer, inner = call(
        edges_kernel,
        [((ROWS, EDGE_LANES), narrow), ((ROWS, EDGE_LANES), narrow)],
        [(EDGE_MASKED, LANES)],
        [],
        [received, side, pick],
    )
    inner_routes, outer_routes = ring_routes(tiles)
    near_routes, far_routes = line_routes(tiles, bands)
    outer = lax.ppermute(outer, "lon", outer_routes)
    inner = lax.ppermute(inner, "lon", inner_routes)
    top, bot = call(
        drafts_kernel,
        [((layout.rows, LANES), wide), ((layout.rows, LANES), wide)],
        [(5 * pieces, LANES)],
        [holder_offset],
        [received, masked, base, bottom_level],
    )
    far, near, west, east, pack = call(
        functools.partial(complete_kernel, levels),
        [
            ((layout.rows, LANES), narrow),
            ((layout.rows, LANES), narrow),
            ((ROWS, EDGE_LANES), narrow),
            ((ROWS, EDGE_LANES), narrow),
            ((8 * levels, LANES), wide),
        ],
        [(LANES, EDGE_LANES), (EDGE_LANES, LANES), (layout.rows, LANES), (layout.rows, LANES)],
        [],
        [outer, inner, top, bot],
    )
    far = lax.ppermute(far, ("lon", "lat"), far_routes)
    near = lax.ppermute(near, ("lon", "lat"), near_routes)
    (state,) = call(
        tiles_kernel,
        [((steps * FIELDS * full, LANES), wide)],
        [],
        [holder_offset],
        [received, west],
    )
    adjoint, velocity, following = call(
        steps_kernel,
        [((2 * full, LANES), wide)] * 3,
        [(2 * full, LANES)],
        [],
        [west, east, state, masked, base, kappa, bottom_level],
    )
    adjoint, velocity = call(
        finish_kernel,
        [((2 * full, LANES), wide)] * 2,
        [
            (layout.rows, LANES),
            (layout.rows, LANES),
            ((levels + 2 * ROWS + ROWS - 1) // ROWS * ROWS, LANES),
        ],
        [],
        [
            far,
            near,
            pack,
            west,
            east,
            state,
            masked,
            kappa,
            bottom_level,
            following,
            adjoint,
            velocity,
        ],
    )
    shape = (2, levels, ROWS, LANES)
    return adjoint.reshape(shape), velocity.reshape(shape)


def solution(mesh):
    return jax.shard_map(
        shards,
        mesh=mesh,
        in_specs=(
            P(None, None, "lat", "lon"),
            P(None, None, None, "lat", "lon"),
            P(),
            P(),
            P("lat", "lon"),
            P(None, "lat", "lon"),
            P(),
        ),
        out_specs=(P(None, None, "lat", "lon"), P(None, None, "lat", "lon")),
        check_vma=False,
    )
```

```python
import functools

import jax
import jax.numpy as jnp
from jax import lax
from jax.experimental import pallas as pl
from jax.experimental.pallas import tpu as pltpu
from jax.sharding import PartitionSpec as P

STEP_ORDER = (1, 0)
FIELDS = 4
ADVECT_HALF = 0.125
DIFFUSE = 0.1

ROWS = 8
LANES = 128

EDGE_STATE = (0, 256)
EDGE_MASKED = 512
EDGE_PART = 640
EDGE_LANES = 768


DRAFT_ROWS = ((ROWS - 1, 0), (ROWS - 1, 1), (0, 0), (0, 1), (ROWS - 2, 0))


class Layout:
    def __init__(self, levels):
        self.tracer = (0, 3 * levels)
        self.merid = (2 * levels, 5 * levels)
        self.masked = 6 * levels
        self.part = 8 * levels
        self.corner = 10 * levels
        self.bottom = 11 * levels
        self.rows = (11 * levels + 1 + 15) // 16 * 16


def shift(block, amount, axis):
    return pltpu.roll(block, amount % block.shape[axis], axis)


def lanes_of(shape):
    return lax.broadcasted_iota(jnp.int32, shape, 1)


def rows_of(shape):
    return lax.broadcasted_iota(jnp.int32, shape, 0)


def strided(ref, start, count):
    return ref[pl.ds(start, count, stride=ROWS), :]


def request_kernel(
    slot_hbm, store_hbm, out_hbm, slot_ref, store_ref, wide_ref, pack_ref, slot_sem, in_sem, out_sem
):
    tile = lax.axis_index("lon")
    bands, steps, pieces, lanes = pack_ref.shape
    slots = store_ref.shape[0] // pieces
    length = store_ref.shape[0] // FIELDS
    table = pltpu.make_async_copy(slot_hbm, slot_ref, slot_sem)
    table.start()
    loads = []
    for field in range(FIELDS):
        here = pl.ds(field * length, length)
        load = pltpu.make_async_copy(store_hbm.at[here], store_ref.at[here], in_sem.at[field])
        load.start()
        loads.append(load)
    for field, load in enumerate(loads):
        load.wait()
        here = slice(field * length, (field + 1) * length)
        wide_ref[here] = store_ref[here].astype(jnp.float32)
    table.wait()
    stores = []
    for band in range(bands):
        for at, step in enumerate(STEP_ORDER):
            slot = slot_ref[step, band, tile]
            rows = wide_ref[pl.ds(slot, pieces, stride=slots), :]
            pack_ref[band, at] = rows.astype(jnp.bfloat16)
        store = pltpu.make_async_copy(pack_ref.at[band], out_hbm.at[band], out_sem.at[band])
        store.start()
        stores.append(store)
    for store in stores:
        store.wait()


def pick_columns(offset=0):
    place = (ROWS * LANES, LANES)
    row, source = rows_of(place) // LANES, rows_of(place) % LANES
    order = lanes_of(place) - (row + ROWS - offset) % ROWS
    chosen = (
        ((source == 0) & (order == 0))
        | ((source == LANES - 1) & (order == ROWS))
        | ((source == 1) & (order == 2 * ROWS))
        | ((source == LANES - 2) & (order == 3 * ROWS))
    )
    return jnp.where(chosen, 1.0, 0.0).astype(jnp.bfloat16)


def prepare_kernel(
    table_ref,
    offset_ref,
    adjoint_ref,
    bottom_ref,
    mix_ref,
    masked_ref,
    base_ref,
    kappa_ref,
    side_ref,
    pick_ref,
    holder_ref,
    column_ref,
):
    levels = adjoint_ref.shape[0] // (2 * ROWS)
    bottom = bottom_ref[...]
    edge = jnp.zeros((ROWS, LANES), jnp.float32)
    kappa_ref[0:ROWS] = edge
    kappa_ref[levels * ROWS : (levels + 1) * ROWS] = edge
    for level in range(levels - 1):
        classes = mix_ref[level * ROWS : (level + 1) * ROWS]
        kappa = jnp.full((ROWS, LANES), table_ref[0], jnp.float32)
        for index in range(1, table_ref.shape[0]):
            kappa = jnp.where(classes == index, table_ref[index], kappa)
        kappa_ref[(level + 1) * ROWS : (level + 2) * ROWS] = kappa
    for tracer in range(2):
        start = tracer * levels * ROWS
        for level in range(levels):
            here = slice(start + level * ROWS, start + (level + 1) * ROWS)
            masked_ref[here] = jnp.where(level < bottom, adjoint_ref[here], 0.0)
        for level in range(levels):
            base_ref[start + level * ROWS : start + (level + 1) * ROWS] = mixed(
                masked_ref, kappa_ref, start, level, levels
            )
    pick = pick_columns()
    offsets = []
    for at, step in enumerate(STEP_ORDER):
        offset = offset_ref[step, lax.axis_index("lat"), lax.axis_index("lon")]
        pick_ref[at] = pick_columns(offset)
        offsets.append(offset)
    for index, (row, at) in enumerate(DRAFT_ROWS):
        held = rows_of((ROWS, LANES)) == lax.rem(row + offsets[at], ROWS)
        holder_ref[index * ROWS : (index + 1) * ROWS] = jnp.where(held, 1.0, 0.0)
    column_ref[...] = jnp.zeros_like(column_ref)
    rows = 2 * levels
    for start, ref in ((0, masked_ref), (LANES, base_ref)):
        blocks = [strided(ref, row, rows).astype(jnp.bfloat16) for row in range(ROWS)]
        column_ref[start : start + rows] = jnp.dot(
            jnp.concatenate(blocks, axis=1), pick, preferred_element_type=jnp.float32
        )
    side = jnp.transpose(column_ref[...])[0 : 4 * ROWS]
    spot = lanes_of((ROWS, 2 * LANES)) == rows
    depth = bottom.astype(jnp.float32)
    side_ref[...] = side
    side_ref[0:ROWS] = jnp.where(spot, depth[:, 0:1], side[0:ROWS])
    side_ref[ROWS : 2 * ROWS] = jnp.where(spot, depth[:, LANES - 1 :], side[ROWS : 2 * ROWS])


def mixed(masked_ref, kappa_ref, start, level, levels):
    def at(index):
        return masked_ref[start + index * ROWS : start + (index + 1) * ROWS]

    masked = at(level)
    below = at(level + 1) if level + 1 < levels else jnp.zeros_like(masked)
    above = at(level - 1) if level > 0 else jnp.zeros_like(masked)
    kappa_above = kappa_ref[level * ROWS : (level + 1) * ROWS]
    kappa_below = kappa_ref[(level + 1) * ROWS : (level + 2) * ROWS]
    return masked + kappa_below * (below - masked) + kappa_above * (above - masked)


def edges_kernel(piece_ref, side_ref, pick_ref, outer_ref, inner_ref, column_ref):
    tile = lax.axis_index("lon")
    holders, steps, pieces, _ = piece_ref.shape
    levels = pieces // FIELDS
    column_ref[...] = jnp.zeros_like(column_ref)
    for at in range(steps):
        chunks = [piece_ref[holder, at] for holder in range(holders)]
        column_ref[EDGE_STATE[at] : EDGE_STATE[at] + pieces] = jnp.dot(
            jnp.concatenate(chunks, axis=1), pick_ref[at], preferred_element_type=jnp.float32
        )
    state = jnp.transpose(column_ref[...])
    lane = lanes_of((ROWS, 2 * LANES))
    sides = []
    for at, sign in ((0, 1.0), (1, -1.0)):
        edge = state[at * ROWS : (at + 1) * ROWS]
        zonal = edge if at == 0 else state[3 * ROWS : 4 * ROWS]
        zonal = zonal[:, 0 : 2 * LANES]
        zonal = jnp.where(lane < levels, shift(zonal, -2 * levels, 1), shift(zonal, -levels, 1))
        masked = side_ref[at * ROWS : (at + 1) * ROWS]
        beside = side_ref[(at + 2) * ROWS : (at + 3) * ROWS]
        face = (ADVECT_HALF * zonal + sign * DIFFUSE) * (sign * (beside - masked))
        part = masked[:, LANES:] + face[:, 0:LANES]
        side = jnp.concatenate([edge, masked[:, 0:LANES], part], axis=1)
        sides.append(side.astype(jnp.bfloat16))
    to_west, to_east = sides

    @pl.when(lax.rem(tile, 2) == 0)
    def _():
        inner_ref[...] = to_east
        outer_ref[...] = to_west

    @pl.when(lax.rem(tile, 2) == 1)
    def _():
        inner_ref[...] = to_west
        outer_ref[...] = to_east


def tiles_kernel(offset_ref, piece_ref, west_ref, state_ref):
    tile = lax.axis_index("lon")
    band = lax.axis_index("lat")
    holders, _, pieces, _ = piece_ref.shape
    for at, step in enumerate(STEP_ORDER):
        offset = offset_ref[step, band, tile]
        for row in range(ROWS):
            chunk = piece_ref[lax.rem(row + offset, holders), at]
            state_ref[pl.ds(at * pieces * ROWS + row, pieces, stride=ROWS), :] = chunk.astype(
                jnp.float32
            )


def drafts_kernel(
    piece_ref, holder_ref, masked_ref, base_ref, bottom_ref, top_ref, bot_ref, line_ref
):
    levels = masked_ref.shape[0] // (2 * ROWS)
    holders, steps, pieces, _ = piece_ref.shape
    for at in range(steps):
        wanted = [index for index, (_, step) in enumerate(DRAFT_ROWS) if step == at]
        found = [None] * len(wanted)
        for holder in range(holders):
            chunk = piece_ref[holder, at].astype(jnp.float32)
            for place, index in enumerate(wanted):
                if holder == 0:
                    found[place] = chunk
                    continue
                here = index * ROWS + holder
                held = jnp.broadcast_to(holder_ref[here : here + 1], chunk.shape) > 0.0
                found[place] = jnp.where(held, chunk, found[place])
        for place, index in enumerate(wanted):
            line_ref[index * pieces : (index + 1) * pieces] = found[place]
    bottom = bottom_ref[...].astype(jnp.float32)
    layout = Layout(levels)
    wide = lanes_of((levels, LANES))
    for row, inner, first, facing, draft_ref in (
        (ROWS - 1, ROWS - 2, 0, 4, top_ref),
        (0, 1, 2, 2, bot_ref),
    ):
        for at in range(2):
            begin = (first + at) * pieces
            draft_ref[layout.tracer[at] : layout.tracer[at] + 2 * levels] = line_ref[
                begin : begin + 2 * levels
            ]
            draft_ref[layout.merid[at] : layout.merid[at] + levels] = line_ref[
                begin + 3 * levels : begin + 4 * levels
            ]
        zonal = line_ref[first * pieces + 2 * levels : first * pieces + 3 * levels]
        merid = line_ref[facing * pieces + 3 * levels : facing * pieces + 4 * levels]
        east_factor = ADVECT_HALF * zonal + DIFFUSE
        west_factor = ADVECT_HALF * shift(zonal, 1, 1) - DIFFUSE
        for tracer in range(2):
            begin = tracer * levels * ROWS
            masked = strided(masked_ref, begin + row, levels)
            next_row = strided(masked_ref, begin + inner, levels)
            if row > inner:
                along = (ADVECT_HALF * merid - DIFFUSE) * (masked - next_row)
            else:
                along = (ADVECT_HALF * merid + DIFFUSE) * (next_row - masked)
            east = east_factor * (shift(masked, -1, 1) - masked)
            west = west_factor * (masked - shift(masked, 1, 1))
            part = strided(base_ref, begin + row, levels) + along
            part = part + jnp.where(wide < LANES - 1, east, 0.0) + jnp.where(wide > 0, west, 0.0)
            at_masked = layout.masked + tracer * levels
            at_part = layout.part + tracer * levels
            draft_ref[at_masked : at_masked + levels] = masked
            draft_ref[at_part : at_part + levels] = part
        draft_ref[layout.corner : layout.corner + levels] = zonal
        draft_ref[layout.bottom : layout.rows] = jnp.broadcast_to(
            bottom[row : row + 1], (layout.rows - layout.bottom, LANES)
        )


def complete_kernel(
    levels,
    outer_ref,
    inner_ref,
    top_draft_ref,
    bot_draft_ref,
    far_ref,
    near_ref,
    west_ref,
    east_ref,
    pack_ref,
    edge_ref,
    column_ref,
    top_ref,
    bot_ref,
):
    layout = Layout(levels)
    odd_tile = lax.rem(lax.axis_index("lon"), 2) == 1
    odd_band = lax.rem(lax.axis_index("lat"), 2) == 1

    @pl.when(odd_tile)
    def _():
        west_ref[...] = inner_ref[...]
        east_ref[...] = outer_ref[...]

    @pl.when(jnp.logical_not(odd_tile))
    def _():
        west_ref[...] = outer_ref[...]
        east_ref[...] = inner_ref[...]

    top_ref[...] = top_draft_ref[...]
    bot_ref[...] = bot_draft_ref[...]
    edge_ref[...] = jnp.zeros_like(edge_ref)
    edge_ref[0:ROWS] = west_ref[...].astype(jnp.float32)
    edge_ref[ROWS : 2 * ROWS] = east_ref[...].astype(jnp.float32)
    column_ref[...] = jnp.transpose(edge_ref[...])
    lane = lanes_of((levels, LANES))

    def pair(start, row):
        block = column_ref[start : start + levels]
        return block[:, row : row + 1], block[:, ROWS + row : ROWS + row + 1]

    for row, draft_ref in ((ROWS - 1, top_ref), (0, bot_ref)):
        zonal = draft_ref[layout.corner : layout.corner + levels]
        zonal_west, _ = pair(EDGE_STATE[0] + 2 * levels, row)
        merid_west, merid_east = pair(EDGE_STATE[0] + 3 * levels, row)
        east_factor = ADVECT_HALF * zonal + DIFFUSE
        west_factor = ADVECT_HALF * zonal_west - DIFFUSE
        corner = jnp.where((lane == 32) | (lane == 96), merid_west, 0.0)
        corner = jnp.where((lane == 31) | (lane == 95), merid_east, corner)
        for tracer in range(2):
            west, east = pair(EDGE_MASKED + tracer * levels, row)
            at_masked = layout.masked + tracer * levels
            at_part = layout.part + tracer * levels
            masked = draft_ref[at_masked : at_masked + levels]
            face = jnp.where(lane == LANES - 1, east_factor * (east - masked), 0.0)
            face = jnp.where(lane == 0, west_factor * (masked - west), face)
            draft_ref[at_part : at_part + levels] = draft_ref[at_part : at_part + levels] + face
            corner = jnp.where(lane == (0, LANES // 2)[tracer], west, corner)
            corner = jnp.where(lane == (LANES - 1, LANES // 2 - 1)[tracer], east, corner)
        draft_ref[layout.corner : layout.corner + levels] = corner
        begin = 0 if row else 4 * levels
        pack_ref[begin : begin + levels] = corner
        zonal_west, _ = pair(EDGE_STATE[1] + 2 * levels, row)
        pack_ref[begin + levels : begin + 2 * levels] = jnp.broadcast_to(
            zonal_west, (levels, LANES)
        )
        for tracer in range(2):
            _, east = pair(EDGE_STATE[1] + tracer * levels, row)
            here = begin + (2 + tracer) * levels
            pack_ref[here : here + levels] = jnp.broadcast_to(east, (levels, LANES))

    @pl.when(odd_band)
    def _():
        near_ref[...] = bot_ref[...].astype(jnp.bfloat16)
        far_ref[...] = top_ref[...].astype(jnp.bfloat16)

    @pl.when(jnp.logical_not(odd_band))
    def _():
        near_ref[...] = top_ref[...].astype(jnp.bfloat16)
        far_ref[...] = bot_ref[...].astype(jnp.bfloat16)


class Tile:
    def __init__(self, levels, west_ref, east_ref, state_ref):
        self.levels = levels
        self.west_ref, self.east_ref, self.state_ref = west_ref, east_ref, state_ref
        self.shape = (ROWS, LANES)
        lane, row = lanes_of(self.shape), rows_of(self.shape)
        self.first_lane, self.last_lane = lane == 0, lane == LANES - 1
        self.bottom_row, self.top_row = row == 0, row == ROWS - 1

    def spread(self, ref, index):
        return jnp.broadcast_to(ref[:, index : index + 1].astype(jnp.float32), self.shape)

    def line(self, ref, index):
        return jnp.broadcast_to(ref[index : index + 1], self.shape)

    def side(self, index):
        return jnp.where(
            self.first_lane, self.spread(self.west_ref, index), self.spread(self.east_ref, index)
        )

    def velocities(self, at, level):
        begin = at * FIELDS * self.levels
        zonal = tile_of(self.state_ref, begin + 2 * self.levels + level)
        merid = tile_of(self.state_ref, begin + 3 * self.levels + level)
        zonal_west = jnp.where(
            self.first_lane,
            self.spread(self.west_ref, EDGE_STATE[at] + 2 * self.levels + level),
            shift(zonal, 1, 1),
        )
        return ADVECT_HALF * zonal, ADVECT_HALF * zonal_west, merid

    def tracer(self, at, level, tracer):
        field = tile_of(self.state_ref, (at * FIELDS + tracer) * self.levels + level)
        east = jnp.where(
            self.last_lane,
            self.spread(self.east_ref, EDGE_STATE[at] + tracer * self.levels + level),
            shift(field, -1, 1),
        )
        return field, east


def tile_of(ref, index):
    return ref[index * ROWS : (index + 1) * ROWS]


def steps_kernel(
    west_ref,
    east_ref,
    state_ref,
    masked_ref,
    base_ref,
    kappa_ref,
    bottom_ref,
    adjoint_ref,
    velocity_ref,
    next_ref,
    side_ref,
):
    levels = masked_ref.shape[0] // (2 * ROWS)
    tile = Tile(levels, west_ref, east_ref, state_ref)
    first_lane, last_lane = tile.first_lane, tile.last_lane
    top_row, bottom_row = tile.top_row, tile.bottom_row
    bottom = bottom_ref[...]
    side_bottom = tile.side(EDGE_MASKED + 2 * levels)
    for level in range(levels):
        zonal, zonal_west, merid = tile.velocities(0, level)
        north_factor = ADVECT_HALF * merid + DIFFUSE
        south_factor = ADVECT_HALF * shift(merid, 1, 0) - DIFFUSE
        side_merid = tile.side(EDGE_STATE[0] + 3 * levels + level)
        side_north = ADVECT_HALF * side_merid + DIFFUSE
        side_south = ADVECT_HALF * shift(side_merid, 1, 0) - DIFFUSE
        zonal_total = jnp.zeros(tile.shape, jnp.float32)
        merid_total = jnp.zeros(tile.shape, jnp.float32)
        for tracer in range(2):
            index = tracer * levels + level
            masked = tile_of(masked_ref, index)
            west = tile.spread(west_ref, EDGE_MASKED + index)
            east = tile.spread(east_ref, EDGE_MASKED + index)
            side = jnp.where(first_lane, west, east)
            to_east = jnp.where(last_lane, east, shift(masked, -1, 1)) - masked
            to_west = masked - jnp.where(first_lane, west, shift(masked, 1, 1))
            to_north = jnp.where(top_row, 0.0, shift(masked, -1, 0) - masked)
            to_south = jnp.where(bottom_row, 0.0, masked - shift(masked, 1, 0))
            result = (
                tile_of(base_ref, index)
                + (zonal + DIFFUSE) * to_east
                + (zonal_west - DIFFUSE) * to_west
                + north_factor * to_north
                + south_factor * to_south
            )
            next_ref[index * ROWS : (index + 1) * ROWS] = jnp.where(level < bottom, result, 0.0)
            field, field_east = tile.tracer(0, level, tracer)
            zonal_total = zonal_total + (field + field_east) * to_east
            merid_total = merid_total + (field + shift(field, -1, 0)) * to_north
            face = jnp.where(
                first_lane,
                (zonal_west + DIFFUSE) * (masked - side),
                (zonal - DIFFUSE) * (side - masked),
            )
            upper = jnp.where(top_row, 0.0, shift(side, -1, 0) - side)
            lower = jnp.where(bottom_row, 0.0, side - shift(side, 1, 0))
            result = (
                tile.side(EDGE_PART + index) + face + side_north * upper + side_south * lower
            )
            side_ref[index * ROWS : (index + 1) * ROWS] = jnp.where(
                side_bottom > level, result, 0.0
            )
        velocity_ref[level * ROWS : (level + 1) * ROWS] = ADVECT_HALF * zonal_total
        velocity_ref[(levels + level) * ROWS : (levels + level + 1) * ROWS] = (
            ADVECT_HALF * merid_total
        )

    for level in range(levels):
        zonal, zonal_west, merid = tile.velocities(1, level)
        north_factor = ADVECT_HALF * merid + DIFFUSE
        south_factor = ADVECT_HALF * shift(merid, 1, 0) - DIFFUSE
        zonal_total = jnp.zeros(tile.shape, jnp.float32)
        merid_total = jnp.zeros(tile.shape, jnp.float32)
        for tracer in range(2):
            index = tracer * levels + level
            masked = tile_of(next_ref, index)
            side = tile_of(side_ref, index)
            to_east = jnp.where(last_lane, side, shift(masked, -1, 1)) - masked
            to_west = masked - jnp.where(first_lane, side, shift(masked, 1, 1))
            to_north = jnp.where(top_row, 0.0, shift(masked, -1, 0) - masked)
            to_south = jnp.where(bottom_row, 0.0, masked - shift(masked, 1, 0))
            adjoint_ref[index * ROWS : (index + 1) * ROWS] = (
                mixed(next_ref, kappa_ref, tracer * levels * ROWS, level, levels)
                + (zonal + DIFFUSE) * to_east
                + (zonal_west - DIFFUSE) * to_west
                + north_factor * to_north
                + south_factor * to_south
            )
            field, field_east = tile.tracer(1, level, tracer)
            zonal_total = zonal_total + (field + field_east) * to_east
            merid_total = merid_total + (field + shift(field, -1, 0)) * to_north
        for total, begin in ((zonal_total, 0), (merid_total, levels)):
            here = slice((begin + level) * ROWS, (begin + level + 1) * ROWS)
            velocity_ref[here] = velocity_ref[here] + ADVECT_HALF * total


def finish_kernel(
    far_ref,
    near_ref,
    pack_ref,
    west_ref,
    east_ref,
    state_ref,
    masked_ref,
    kappa_ref,
    bottom_ref,
    next_ref,
    adjoint_in,
    velocity_in,
    adjoint_hbm,
    velocity_hbm,
    adjoint_ref,
    velocity_ref,
    north_ref,
    south_ref,
    guard_ref,
    out_sem,
):
    levels = masked_ref.shape[0] // (2 * ROWS)
    layout = Layout(levels)
    top = ROWS - 1
    band = lax.axis_index("lat")
    odd_band = lax.rem(band, 2) == 1
    top_band = (band == lax.axis_size("lat") - 1).astype(jnp.int32)
    folded = top_band.astype(jnp.float32)
    open_south = jnp.where(band > 0, DIFFUSE, 0.0)
    square = (LANES, LANES)
    from_lane = rows_of(square)
    turned = from_lane + top_band * (LANES - 1 - 2 * from_lane)
    turn = jnp.where(lanes_of(square) == turned, 1.0, 0.0).astype(jnp.bfloat16)

    @pl.when(odd_band)
    def _():
        north_ref[...] = jnp.dot(far_ref[...], turn, preferred_element_type=jnp.float32)
        south_ref[...] = near_ref[...].astype(jnp.float32)

    @pl.when(jnp.logical_not(odd_band))
    def _():
        north_ref[...] = jnp.dot(near_ref[...], turn, preferred_element_type=jnp.float32)
        south_ref[...] = far_ref[...].astype(jnp.float32)

    copies = []

    def send(source, target, part):
        here = pl.ds(part * levels * ROWS, levels * ROWS)
        copy = pltpu.make_async_copy(source.at[here], target.at[here], out_sem.at[len(copies)])
        copy.start()
        copies.append(copy)

    guard_ref[...] = jnp.zeros_like(guard_ref)

    def rows_at(ref, begin):
        return ref[begin : begin + levels]

    def unpacked(packed):
        return packed, shift(packed, LANES // 2, 1), shift(packed, 96, 1)

    def state_row(at, field, row):
        return strided(state_ref, (at * FIELDS + field) * levels * ROWS + row, levels)

    def add_rows(ref, begin, value):
        here = pl.ds(begin, levels, stride=ROWS)
        ref[here, :] = ref[here, :] + value

    level_of = rows_of((levels, LANES)).astype(jnp.float32)
    lane = lanes_of((levels, LANES))
    first_lane, last_lane = lane == 0, lane == LANES - 1

    def side_depth(row):
        spot = slice(EDGE_MASKED + 2 * levels, EDGE_MASKED + 2 * levels + 1)
        west = west_ref[...].astype(jnp.float32)[row : row + 1, spot]
        east = east_ref[...].astype(jnp.float32)[row : row + 1, spot]
        return jnp.where(lane < LANES // 2, west, east)

    depth = bottom_ref[...].astype(jnp.float32)
    merid_top = state_row(0, 3, top)
    north_merid = rows_at(north_ref, layout.merid[0]) * folded
    south_merid = rows_at(south_ref, layout.merid[0])
    top_factor = ADVECT_HALF * (merid_top - north_merid) + DIFFUSE
    bottom_factor = ADVECT_HALF * south_merid - open_south
    own_corner = (unpacked(rows_at(pack_ref, 4 * levels)), unpacked(rows_at(pack_ref, 0)))
    north_corner = unpacked(rows_at(north_ref, layout.corner))
    south_corner = unpacked(rows_at(south_ref, layout.corner))
    side_top = ADVECT_HALF * (own_corner[1][2] - folded * north_corner[2]) + DIFFUSE
    side_bottom = ADVECT_HALF * south_corner[2] - open_south

    merids = {row: state_row(1, 3, row) for row in (0, top - 1, top)}
    next_north = ADVECT_HALF * (merids[top] - folded * rows_at(north_ref, layout.merid[1])) + DIFFUSE
    next_south = ADVECT_HALF * rows_at(south_ref, layout.merid[1]) - open_south
    east_factors, west_factors, kappas = [], [], []
    for row, begin in ((0, 4 * levels), (top, 0)):
        zonal = state_row(1, 2, row)
        zonal_west = jnp.where(first_lane, rows_at(pack_ref, begin + levels), shift(zonal, 1, 1))
        east_factors.append(ADVECT_HALF * zonal + DIFFUSE)
        west_factors.append(ADVECT_HALF * zonal_west - DIFFUSE)
        kappas.append(
            (strided(kappa_ref, row, levels), strided(kappa_ref, ROWS + row, levels))
        )

    zonal_totals = [jnp.zeros((levels, LANES), jnp.float32) for _ in range(2)]
    merid_totals = {row: jnp.zeros((levels, LANES), jnp.float32) for row in (0, top - 1, top)}
    for tracer in range(2):
        start = tracer * levels * ROWS
        own_top = strided(masked_ref, start + top, levels)
        own_bottom = strided(masked_ref, start, levels)
        north = rows_at(north_ref, layout.masked + tracer * levels)
        south = rows_at(south_ref, layout.masked + tracer * levels)
        north_step, south_step = north - own_top, own_bottom - south
        wet = level_of < north_ref[layout.bottom : layout.bottom + 1]
        ring_north = rows_at(north_ref, layout.part + tracer * levels)
        ring_north = ring_north - (ADVECT_HALF * (north_merid - merid_top) + DIFFUSE) * north_step
        ring_north = jnp.where(wet, ring_north, 0.0)
        wet = level_of < south_ref[layout.bottom : layout.bottom + 1]
        ring_south = rows_at(south_ref, layout.part + tracer * levels)
        ring_south = ring_south + (ADVECT_HALF * south_merid + DIFFUSE) * south_step
        ring_south = jnp.where(wet, ring_south, 0.0)
        first_field = state_row(0, tracer, top) + rows_at(
            north_ref, layout.tracer[0] + tracer * levels
        )
        merid_totals[top] = merid_totals[top] + first_field * north_step
        changes = (
            jnp.where(level_of < depth[0:1], bottom_factor * south_step, 0.0),
            jnp.where(level_of < depth[top:], top_factor * north_step, 0.0),
        )
        side_changes = (
            side_bottom * (own_corner[0][tracer] - south_corner[tracer]),
            side_top * (north_corner[tracer] - own_corner[1][tracer]),
        )
        fields = {row: state_row(1, tracer, row) for row in (0, 1, top - 1, top)}
        for at, row in enumerate((0, top)):
            change = changes[at]
            side = jnp.where(level_of < side_depth(row), side_changes[at], 0.0)
            guard_ref[ROWS : ROWS + levels] = change
            above = guard_ref[ROWS - 1 : ROWS - 1 + levels]
            below = guard_ref[ROWS + 1 : ROWS + 1 + levels]
            kappa_above, kappa_below = kappas[at]
            to_east = jnp.where(last_lane, side, shift(change, -1, 1)) - change
            to_west = change - jnp.where(first_lane, side, shift(change, 1, 1))
            value = (
                change
                + kappa_below * (below - change)
                + kappa_above * (above - change)
                + east_factors[at] * to_east
                + west_factors[at] * to_west
            )
            begin = (4 * levels if row == 0 else 0) + (2 + tracer) * levels
            field_east = jnp.where(
                last_lane, rows_at(pack_ref, begin), shift(fields[row], -1, 1)
            )
            zonal_totals[at] = zonal_totals[at] + (fields[row] + field_east) * to_east
            full = strided(next_ref, start + row, levels) + change
            if row == 0:
                value = value - (ADVECT_HALF * merids[0] + DIFFUSE) * change
                value = value + next_south * (full - ring_south)
                add_rows(adjoint_ref, start + 1, -(ADVECT_HALF * merids[0] - DIFFUSE) * change)
                merid_totals[0] = merid_totals[0] - (fields[0] + fields[1]) * change
            else:
                value = value + (ADVECT_HALF * merids[top - 1] - DIFFUSE) * change
                value = value + next_north * (ring_north - full)
                inner = (ADVECT_HALF * merids[top - 1] + DIFFUSE) * change
                add_rows(adjoint_ref, start + top - 1, inner)
                merid_totals[top - 1] = (
                    merid_totals[top - 1] + (fields[top - 1] + fields[top]) * change
                )
                field_north = rows_at(north_ref, layout.tracer[1] + tracer * levels)
                merid_totals[top] = merid_totals[top] + (fields[top] + field_north) * (
                    ring_north - full
                )
            add_rows(adjoint_ref, start + row, value)
        send(adjoint_ref, adjoint_hbm, tracer)
    for at, row in enumerate((0, top)):
        add_rows(velocity_ref, row, ADVECT_HALF * zonal_totals[at])
    send(velocity_ref, velocity_hbm, 0)
    for row, total in merid_totals.items():
        add_rows(velocity_ref, levels * ROWS + row, ADVECT_HALF * total)
    send(velocity_ref, velocity_hbm, 1)
    for copy in copies:
        copy.wait()


def swaps(pairs):
    return [pair for low, high in pairs for pair in ((low, high), (high, low))]


def ring_routes(tiles):
    inner = swaps((tile, tile + 1) for tile in range(0, tiles, 2))
    outer = swaps((tile, (tile + 1) % tiles) for tile in range(1, tiles, 2))
    return inner, outer


def line_routes(tiles, bands):
    near, far = [], []
    for tile in range(tiles):
        start = tile * bands
        near += [(start + band, start + band + 1) for band in range(0, bands, 2)]
        far += [(start + band, start + band + 1) for band in range(1, bands - 1, 2)]
        if tile < tiles // 2:
            far.append((start + bands - 1, (tiles - tile) * bands - 1))
    return swaps(near), swaps(far)


def call(kernel, outputs, scratch, scalars, arrays):
    vmem = pl.BlockSpec(memory_space=pltpu.VMEM)
    smem = pl.BlockSpec(memory_space=pltpu.SMEM)
    return pl.pallas_call(
        kernel,
        out_shape=[jax.ShapeDtypeStruct(shape, dtype) for shape, dtype in outputs],
        in_specs=[smem] * len(scalars) + [vmem] * len(arrays),
        out_specs=[vmem] * len(outputs),
        scratch_shapes=[pltpu.VMEM(shape, jnp.float32) for shape in scratch],
        compiler_params=pltpu.CompilerParams(vmem_limit_bytes=32 * 1024 * 1024),
    )(*scalars, *arrays)


def shards(final_adjoint, store, holder_offset, holder_slot, bottom_level, mix_class, mix_table):
    bands = lax.axis_size("lat")
    tiles = lax.axis_size("lon")
    levels = final_adjoint.shape[1]
    slots = store.shape[2]
    steps = len(STEP_ORDER)
    pieces = FIELDS * levels
    full = levels * ROWS
    layout = Layout(levels)
    narrow, wide = jnp.bfloat16, jnp.float32
    hbm = pl.BlockSpec(memory_space=pltpu.HBM)
    request = pl.pallas_call(
        request_kernel,
        out_shape=jax.ShapeDtypeStruct((bands, steps, pieces, LANES), narrow),
        in_specs=[hbm, hbm],
        out_specs=hbm,
        scratch_shapes=[
            pltpu.SMEM(holder_slot.shape, jnp.int32),
            pltpu.VMEM((pieces * slots, LANES), narrow),
            pltpu.VMEM((pieces * slots, LANES), wide),
            pltpu.VMEM((bands, steps, pieces, LANES), narrow),
            pltpu.SemaphoreType.DMA,
            pltpu.SemaphoreType.DMA((FIELDS,)),
            pltpu.SemaphoreType.DMA((bands,)),
        ],
        compiler_params=pltpu.CompilerParams(vmem_limit_bytes=32 * 1024 * 1024),
    )(
        pltpu.with_memory_space_constraint(holder_slot, pltpu.HBM),
        pltpu.with_memory_space_constraint(store.reshape(pieces * slots, LANES), pltpu.HBM),
    )
    received = lax.all_to_all(request, "lat", split_axis=0, concat_axis=0, tiled=True)
    masked, base, kappa, side, pick, holder = call(
        prepare_kernel,
        [
            ((2 * full, LANES), wide),
            ((2 * full, LANES), wide),
            ((full + ROWS, LANES), wide),
            ((4 * ROWS, 2 * LANES), wide),
            ((steps, ROWS * LANES, LANES), narrow),
            ((len(DRAFT_ROWS) * ROWS, LANES), wide),
        ],
        [(2 * LANES, LANES)],
        [mix_table, holder_offset],
        [
            final_adjoint.reshape(2 * full, LANES),
            bottom_level,
            mix_class.reshape((levels - 1) * ROWS, LANES),
        ],
    )
    outer, inner = call(
        edges_kernel,
        [((ROWS, EDGE_LANES), narrow), ((ROWS, EDGE_LANES), narrow)],
        [(EDGE_MASKED, LANES)],
        [],
        [received, side, pick],
    )
    inner_routes, outer_routes = ring_routes(tiles)
    near_routes, far_routes = line_routes(tiles, bands)
    outer = lax.ppermute(outer, "lon", outer_routes)
    inner = lax.ppermute(inner, "lon", inner_routes)
    top, bot = call(
        drafts_kernel,
        [((layout.rows, LANES), wide), ((layout.rows, LANES), wide)],
        [(len(DRAFT_ROWS) * pieces, LANES)],
        [],
        [received, holder, masked, base, bottom_level],
    )
    far, near, west, east, pack = call(
        functools.partial(complete_kernel, levels),
        [
            ((layout.rows, LANES), narrow),
            ((layout.rows, LANES), narrow),
            ((ROWS, EDGE_LANES), narrow),
            ((ROWS, EDGE_LANES), narrow),
            ((8 * levels, LANES), wide),
        ],
        [(LANES, EDGE_LANES), (EDGE_LANES, LANES), (layout.rows, LANES), (layout.rows, LANES)],
        [],
        [outer, inner, top, bot],
    )
    far = lax.ppermute(far, ("lon", "lat"), far_routes)
    near = lax.ppermute(near, ("lon", "lat"), near_routes)
    (state,) = call(
        tiles_kernel,
        [((steps * FIELDS * full, LANES), wide)],
        [],
        [holder_offset],
        [received, west],
    )
    adjoint, velocity, following = call(
        steps_kernel,
        [((2 * full, LANES), wide)] * 3,
        [(2 * full, LANES)],
        [],
        [west, east, state, masked, base, kappa, bottom_level],
    )
    arrays = (far, near, pack, west, east, state, masked, kappa, bottom_level, following)
    arrays += (adjoint, velocity)
    vmem = pl.BlockSpec(memory_space=pltpu.VMEM)
    adjoint, velocity, _, _ = pl.pallas_call(
        finish_kernel,
        out_shape=[jax.ShapeDtypeStruct((2 * full, LANES), wide)] * 4,
        in_specs=[vmem] * len(arrays),
        out_specs=[hbm, hbm, vmem, vmem],
        input_output_aliases={len(arrays) - 2: 2, len(arrays) - 1: 3},
        scratch_shapes=[
            pltpu.VMEM((layout.rows, LANES), wide),
            pltpu.VMEM((layout.rows, LANES), wide),
            pltpu.VMEM(((levels + 2 * ROWS + ROWS - 1) // ROWS * ROWS, LANES), wide),
            pltpu.SemaphoreType.DMA((4,)),
        ],
        compiler_params=pltpu.CompilerParams(vmem_limit_bytes=32 * 1024 * 1024),
    )(*arrays)
    shape = (2, levels, ROWS, LANES)
    return adjoint.reshape(shape), velocity.reshape(shape)


def solution(mesh):
    return jax.shard_map(
        shards,
        mesh=mesh,
        in_specs=(
            P(None, None, "lat", "lon"),
            P(None, None, None, "lat", "lon"),
            P(),
            P(),
            P("lat", "lon"),
            P(None, "lat", "lon"),
            P(),
        ),
        out_specs=(P(None, None, "lat", "lon"), P(None, None, "lat", "lon")),
        check_vma=False,
    )
```

```python
import functools

import jax
import jax.numpy as jnp
from jax import lax
from jax.experimental import pallas as pl
from jax.experimental.pallas import tpu as pltpu
from jax.sharding import PartitionSpec as P

STEP_ORDER = (1, 0)
FIELDS = 4
ADVECT_HALF = 0.125
DIFFUSE = 0.1

ROWS = 8
LANES = 128

EDGE_STATE = (0, 256)
EDGE_MASKED = 512
EDGE_PART = 640
EDGE_LANES = 768


DRAFT_ROWS = ((ROWS - 1, 0), (ROWS - 1, 1), (0, 0), (0, 1), (ROWS - 2, 0))


class Layout:
    def __init__(self, levels):
        self.tracer = (0, 3 * levels)
        self.merid = (2 * levels, 5 * levels)
        self.masked = 6 * levels
        self.part = 8 * levels
        self.corner = 10 * levels
        self.bottom = 11 * levels
        self.rows = (11 * levels + 1 + 15) // 16 * 16


def shift(block, amount, axis):
    return pltpu.roll(block, amount % block.shape[axis], axis)


def lanes_of(shape):
    return lax.broadcasted_iota(jnp.int32, shape, 1)


def rows_of(shape):
    return lax.broadcasted_iota(jnp.int32, shape, 0)


def strided(ref, start, count):
    return ref[pl.ds(start, count, stride=ROWS), :]


def request_kernel(
    slot_hbm, store_hbm, out_hbm, slot_ref, store_ref, wide_ref, pack_ref, slot_sem, in_sem, out_sem
):
    tile = lax.axis_index("lon")
    bands, steps, pieces, lanes = pack_ref.shape
    slots = store_ref.shape[0] // pieces
    length = store_ref.shape[0] // FIELDS
    table = pltpu.make_async_copy(slot_hbm, slot_ref, slot_sem)
    table.start()
    loads = []
    for field in range(FIELDS):
        here = pl.ds(field * length, length)
        load = pltpu.make_async_copy(store_hbm.at[here], store_ref.at[here], in_sem.at[field])
        load.start()
        loads.append(load)
    for field, load in enumerate(loads):
        load.wait()
        here = slice(field * length, (field + 1) * length)
        wide_ref[here] = store_ref[here].astype(jnp.float32)
    table.wait()
    stores = []
    for band in range(bands):
        for at, step in enumerate(STEP_ORDER):
            slot = slot_ref[step, band, tile]
            rows = wide_ref[pl.ds(slot, pieces, stride=slots), :]
            pack_ref[band, at] = rows.astype(jnp.bfloat16)
        store = pltpu.make_async_copy(pack_ref.at[band], out_hbm.at[band], out_sem.at[band])
        store.start()
        stores.append(store)
    for store in stores:
        store.wait()


def pick_columns(offset=0):
    place = (ROWS * LANES, LANES)
    row, source = rows_of(place) // LANES, rows_of(place) % LANES
    order = lanes_of(place) - (row + ROWS - offset) % ROWS
    chosen = (
        ((source == 0) & (order == 0))
        | ((source == LANES - 1) & (order == ROWS))
        | ((source == 1) & (order == 2 * ROWS))
        | ((source == LANES - 2) & (order == 3 * ROWS))
    )
    return jnp.where(chosen, 1.0, 0.0).astype(jnp.bfloat16)


def prepare_kernel(
    table_ref,
    offset_ref,
    adjoint_ref,
    bottom_ref,
    mix_ref,
    masked_ref,
    base_ref,
    kappa_ref,
    side_ref,
    pick_ref,
    holder_ref,
    column_ref,
):
    levels = adjoint_ref.shape[0] // (2 * ROWS)
    bottom = bottom_ref[...]
    edge = jnp.zeros((ROWS, LANES), jnp.float32)
    kappa_ref[0:ROWS] = edge
    kappa_ref[levels * ROWS : (levels + 1) * ROWS] = edge
    for level in range(levels - 1):
        classes = mix_ref[level * ROWS : (level + 1) * ROWS]
        kappa = jnp.full((ROWS, LANES), table_ref[0], jnp.float32)
        for index in range(1, table_ref.shape[0]):
            kappa = jnp.where(classes == index, table_ref[index], kappa)
        kappa_ref[(level + 1) * ROWS : (level + 2) * ROWS] = kappa
    for tracer in range(2):
        start = tracer * levels * ROWS
        for level in range(levels):
            here = slice(start + level * ROWS, start + (level + 1) * ROWS)
            masked_ref[here] = jnp.where(level < bottom, adjoint_ref[here], 0.0)
        for level in range(levels):
            base_ref[start + level * ROWS : start + (level + 1) * ROWS] = mixed(
                masked_ref, kappa_ref, start, level, levels
            )
    pick = pick_columns()
    offsets = []
    for at, step in enumerate(STEP_ORDER):
        offset = offset_ref[step, lax.axis_index("lat"), lax.axis_index("lon")]
        pick_ref[at] = pick_columns(offset)
        offsets.append(offset)
    for index, (row, at) in enumerate(DRAFT_ROWS):
        held = rows_of((ROWS, LANES)) == lax.rem(row + offsets[at], ROWS)
        holder_ref[index * ROWS : (index + 1) * ROWS] = jnp.where(held, 1.0, 0.0)
    column_ref[...] = jnp.zeros_like(column_ref)
    rows = 2 * levels
    for start, ref in ((0, masked_ref), (LANES, base_ref)):
        blocks = [strided(ref, row, rows).astype(jnp.bfloat16) for row in range(ROWS)]
        column_ref[start : start + rows] = jnp.dot(
            jnp.concatenate(blocks, axis=1), pick, preferred_element_type=jnp.float32
        )
    side = jnp.transpose(column_ref[...])[0 : 4 * ROWS]
    spot = lanes_of((ROWS, 2 * LANES)) == rows
    depth = bottom.astype(jnp.float32)
    side_ref[...] = side
    side_ref[0:ROWS] = jnp.where(spot, depth[:, 0:1], side[0:ROWS])
    side_ref[ROWS : 2 * ROWS] = jnp.where(spot, depth[:, LANES - 1 :], side[ROWS : 2 * ROWS])


def mixed(masked_ref, kappa_ref, start, level, levels):
    def at(index):
        return masked_ref[start + index * ROWS : start + (index + 1) * ROWS]

    masked = at(level)
    below = at(level + 1) if level + 1 < levels else jnp.zeros_like(masked)
    above = at(level - 1) if level > 0 else jnp.zeros_like(masked)
    kappa_above = kappa_ref[level * ROWS : (level + 1) * ROWS]
    kappa_below = kappa_ref[(level + 1) * ROWS : (level + 2) * ROWS]
    return masked + kappa_below * (below - masked) + kappa_above * (above - masked)


def edges_kernel(piece_ref, side_ref, pick_ref, outer_ref, inner_ref, column_ref):
    tile = lax.axis_index("lon")
    holders, steps, pieces, _ = piece_ref.shape
    levels = pieces // FIELDS
    column_ref[...] = jnp.zeros_like(column_ref)
    for at in range(steps):
        chunks = [piece_ref[holder, at] for holder in range(holders)]
        column_ref[EDGE_STATE[at] : EDGE_STATE[at] + pieces] = jnp.dot(
            jnp.concatenate(chunks, axis=1), pick_ref[at], preferred_element_type=jnp.float32
        )
    state = jnp.transpose(column_ref[...])
    lane = lanes_of((ROWS, 2 * LANES))
    sides = []
    for at, sign in ((0, 1.0), (1, -1.0)):
        edge = state[at * ROWS : (at + 1) * ROWS]
        zonal = edge if at == 0 else state[3 * ROWS : 4 * ROWS]
        zonal = zonal[:, 0 : 2 * LANES]
        zonal = jnp.where(lane < levels, shift(zonal, -2 * levels, 1), shift(zonal, -levels, 1))
        masked = side_ref[at * ROWS : (at + 1) * ROWS]
        beside = side_ref[(at + 2) * ROWS : (at + 3) * ROWS]
        face = (ADVECT_HALF * zonal + sign * DIFFUSE) * (sign * (beside - masked))
        part = masked[:, LANES:] + face[:, 0:LANES]
        side = jnp.concatenate([edge, masked[:, 0:LANES], part], axis=1)
        sides.append(side.astype(jnp.bfloat16))
    to_west, to_east = sides

    @pl.when(lax.rem(tile, 2) == 0)
    def _():
        inner_ref[...] = to_east
        outer_ref[...] = to_west

    @pl.when(lax.rem(tile, 2) == 1)
    def _():
        inner_ref[...] = to_west
        outer_ref[...] = to_east


def tiles_kernel(offset_ref, piece_ref, west_ref, state_ref):
    tile = lax.axis_index("lon")
    band = lax.axis_index("lat")
    holders, _, pieces, _ = piece_ref.shape
    for at, step in enumerate(STEP_ORDER):
        offset = offset_ref[step, band, tile]
        for row in range(ROWS):
            chunk = piece_ref[lax.rem(row + offset, holders), at]
            state_ref[pl.ds(at * pieces * ROWS + row, pieces, stride=ROWS), :] = chunk.astype(
                jnp.float32
            )


def drafts_kernel(
    piece_ref, holder_ref, masked_ref, base_ref, bottom_ref, top_ref, bot_ref, line_ref
):
    levels = masked_ref.shape[0] // (2 * ROWS)
    holders, steps, pieces, _ = piece_ref.shape
    for at in range(steps):
        wanted = [index for index, (_, step) in enumerate(DRAFT_ROWS) if step == at]
        found = [None] * len(wanted)
        for holder in range(holders):
            chunk = piece_ref[holder, at].astype(jnp.float32)
            for place, index in enumerate(wanted):
                if holder == 0:
                    found[place] = chunk
                    continue
                here = index * ROWS + holder
                held = jnp.broadcast_to(holder_ref[here : here + 1], chunk.shape) > 0.0
                found[place] = jnp.where(held, chunk, found[place])
        for place, index in enumerate(wanted):
            line_ref[index * pieces : (index + 1) * pieces] = found[place]
    bottom = bottom_ref[...].astype(jnp.float32)
    layout = Layout(levels)
    wide = lanes_of((levels, LANES))
    for row, inner, first, facing, draft_ref in (
        (ROWS - 1, ROWS - 2, 0, 4, top_ref),
        (0, 1, 2, 2, bot_ref),
    ):
        for at in range(2):
            begin = (first + at) * pieces
            draft_ref[layout.tracer[at] : layout.tracer[at] + 2 * levels] = line_ref[
                begin : begin + 2 * levels
            ]
            draft_ref[layout.merid[at] : layout.merid[at] + levels] = line_ref[
                begin + 3 * levels : begin + 4 * levels
            ]
        zonal = line_ref[first * pieces + 2 * levels : first * pieces + 3 * levels]
        merid = line_ref[facing * pieces + 3 * levels : facing * pieces + 4 * levels]
        east_factor = ADVECT_HALF * zonal + DIFFUSE
        west_factor = ADVECT_HALF * shift(zonal, 1, 1) - DIFFUSE
        for tracer in range(2):
            begin = tracer * levels * ROWS
            masked = strided(masked_ref, begin + row, levels)
            next_row = strided(masked_ref, begin + inner, levels)
            if row > inner:
                along = (ADVECT_HALF * merid - DIFFUSE) * (masked - next_row)
            else:
                along = (ADVECT_HALF * merid + DIFFUSE) * (next_row - masked)
            east = east_factor * (shift(masked, -1, 1) - masked)
            west = west_factor * (masked - shift(masked, 1, 1))
            part = strided(base_ref, begin + row, levels) + along
            part = part + jnp.where(wide < LANES - 1, east, 0.0) + jnp.where(wide > 0, west, 0.0)
            at_masked = layout.masked + tracer * levels
            at_part = layout.part + tracer * levels
            draft_ref[at_masked : at_masked + levels] = masked
            draft_ref[at_part : at_part + levels] = part
        draft_ref[layout.corner : layout.corner + levels] = zonal
        draft_ref[layout.bottom : layout.rows] = jnp.broadcast_to(
            bottom[row : row + 1], (layout.rows - layout.bottom, LANES)
        )


def complete_kernel(
    levels,
    inner_ref,
    outer_ref,
    top_draft_ref,
    bot_draft_ref,
    far_ref,
    near_ref,
    west_ref,
    east_ref,
    pack_ref,
    edge_ref,
    column_ref,
    top_ref,
    bot_ref,
):
    layout = Layout(levels)
    odd_tile = lax.rem(lax.axis_index("lon"), 2) == 1
    odd_band = lax.rem(lax.axis_index("lat"), 2) == 1

    @pl.when(odd_tile)
    def _():
        west_ref[...] = inner_ref[...]
        east_ref[...] = outer_ref[...]

    @pl.when(jnp.logical_not(odd_tile))
    def _():
        west_ref[...] = outer_ref[...]
        east_ref[...] = inner_ref[...]

    top_ref[...] = top_draft_ref[...]
    bot_ref[...] = bot_draft_ref[...]
    edge_ref[...] = jnp.zeros_like(edge_ref)
    edge_ref[0:ROWS] = west_ref[...].astype(jnp.float32)
    edge_ref[ROWS : 2 * ROWS] = east_ref[...].astype(jnp.float32)
    column_ref[...] = jnp.transpose(edge_ref[...])
    lane = lanes_of((levels, LANES))

    def pair(start, row):
        block = column_ref[start : start + levels]
        return block[:, row : row + 1], block[:, ROWS + row : ROWS + row + 1]

    for row, draft_ref in ((ROWS - 1, top_ref), (0, bot_ref)):
        zonal = draft_ref[layout.corner : layout.corner + levels]
        zonal_west, _ = pair(EDGE_STATE[0] + 2 * levels, row)
        merid_west, merid_east = pair(EDGE_STATE[0] + 3 * levels, row)
        east_factor = ADVECT_HALF * zonal + DIFFUSE
        west_factor = ADVECT_HALF * zonal_west - DIFFUSE
        corner = jnp.where((lane == 32) | (lane == 96), merid_west, 0.0)
        corner = jnp.where((lane == 31) | (lane == 95), merid_east, corner)
        for tracer in range(2):
            west, east = pair(EDGE_MASKED + tracer * levels, row)
            at_masked = layout.masked + tracer * levels
            at_part = layout.part + tracer * levels
            masked = draft_ref[at_masked : at_masked + levels]
            face = jnp.where(lane == LANES - 1, east_factor * (east - masked), 0.0)
            face = jnp.where(lane == 0, west_factor * (masked - west), face)
            draft_ref[at_part : at_part + levels] = draft_ref[at_part : at_part + levels] + face
            corner = jnp.where(lane == (0, LANES // 2)[tracer], west, corner)
            corner = jnp.where(lane == (LANES - 1, LANES // 2 - 1)[tracer], east, corner)
        draft_ref[layout.corner : layout.corner + levels] = corner
        begin = 0 if row else 4 * levels
        pack_ref[begin : begin + levels] = corner
        zonal_west, _ = pair(EDGE_STATE[1] + 2 * levels, row)
        pack_ref[begin + levels : begin + 2 * levels] = jnp.broadcast_to(
            zonal_west, (levels, LANES)
        )
        for tracer in range(2):
            _, east = pair(EDGE_STATE[1] + tracer * levels, row)
            here = begin + (2 + tracer) * levels
            pack_ref[here : here + levels] = jnp.broadcast_to(east, (levels, LANES))

    @pl.when(odd_band)
    def _():
        near_ref[...] = bot_ref[...].astype(jnp.bfloat16)
        far_ref[...] = top_ref[...].astype(jnp.bfloat16)

    @pl.when(jnp.logical_not(odd_band))
    def _():
        near_ref[...] = top_ref[...].astype(jnp.bfloat16)
        far_ref[...] = bot_ref[...].astype(jnp.bfloat16)


class Tile:
    def __init__(self, levels, west_ref, east_ref, state_ref):
        self.levels = levels
        self.west_ref, self.east_ref, self.state_ref = west_ref, east_ref, state_ref
        self.shape = (ROWS, LANES)
        lane, row = lanes_of(self.shape), rows_of(self.shape)
        self.first_lane, self.last_lane = lane == 0, lane == LANES - 1
        self.bottom_row, self.top_row = row == 0, row == ROWS - 1

    def spread(self, ref, index):
        return jnp.broadcast_to(ref[:, index : index + 1].astype(jnp.float32), self.shape)

    def line(self, ref, index):
        return jnp.broadcast_to(ref[index : index + 1], self.shape)

    def side(self, index):
        return jnp.where(
            self.first_lane, self.spread(self.west_ref, index), self.spread(self.east_ref, index)
        )

    def velocities(self, at, level):
        begin = at * FIELDS * self.levels
        zonal = tile_of(self.state_ref, begin + 2 * self.levels + level)
        merid = tile_of(self.state_ref, begin + 3 * self.levels + level)
        zonal_west = jnp.where(
            self.first_lane,
            self.spread(self.west_ref, EDGE_STATE[at] + 2 * self.levels + level),
            shift(zonal, 1, 1),
        )
        return ADVECT_HALF * zonal, ADVECT_HALF * zonal_west, merid

    def tracer(self, at, level, tracer):
        field = tile_of(self.state_ref, (at * FIELDS + tracer) * self.levels + level)
        east = jnp.where(
            self.last_lane,
            self.spread(self.east_ref, EDGE_STATE[at] + tracer * self.levels + level),
            shift(field, -1, 1),
        )
        return field, east


def tile_of(ref, index):
    return ref[index * ROWS : (index + 1) * ROWS]


def steps_kernel(
    west_ref,
    east_ref,
    state_ref,
    masked_ref,
    base_ref,
    kappa_ref,
    bottom_ref,
    adjoint_ref,
    velocity_ref,
    next_ref,
    side_ref,
):
    levels = masked_ref.shape[0] // (2 * ROWS)
    tile = Tile(levels, west_ref, east_ref, state_ref)
    first_lane, last_lane = tile.first_lane, tile.last_lane
    top_row, bottom_row = tile.top_row, tile.bottom_row
    bottom = bottom_ref[...]
    side_bottom = tile.side(EDGE_MASKED + 2 * levels)
    for level in range(levels):
        zonal, zonal_west, merid = tile.velocities(0, level)
        north_factor = ADVECT_HALF * merid + DIFFUSE
        south_factor = ADVECT_HALF * shift(merid, 1, 0) - DIFFUSE
        side_merid = tile.side(EDGE_STATE[0] + 3 * levels + level)
        side_north = ADVECT_HALF * side_merid + DIFFUSE
        side_south = ADVECT_HALF * shift(side_merid, 1, 0) - DIFFUSE
        zonal_total = jnp.zeros(tile.shape, jnp.float32)
        merid_total = jnp.zeros(tile.shape, jnp.float32)
        for tracer in range(2):
            index = tracer * levels + level
            masked = tile_of(masked_ref, index)
            west = tile.spread(west_ref, EDGE_MASKED + index)
            east = tile.spread(east_ref, EDGE_MASKED + index)
            side = jnp.where(first_lane, west, east)
            to_east = jnp.where(last_lane, east, shift(masked, -1, 1)) - masked
            to_west = masked - jnp.where(first_lane, west, shift(masked, 1, 1))
            to_north = jnp.where(top_row, 0.0, shift(masked, -1, 0) - masked)
            to_south = jnp.where(bottom_row, 0.0, masked - shift(masked, 1, 0))
            result = (
                tile_of(base_ref, index)
                + (zonal + DIFFUSE) * to_east
                + (zonal_west - DIFFUSE) * to_west
                + north_factor * to_north
                + south_factor * to_south
            )
            next_ref[index * ROWS : (index + 1) * ROWS] = jnp.where(level < bottom, result, 0.0)
            field, field_east = tile.tracer(0, level, tracer)
            zonal_total = zonal_total + (field + field_east) * to_east
            merid_total = merid_total + (field + shift(field, -1, 0)) * to_north
            face = jnp.where(
                first_lane,
                (zonal_west + DIFFUSE) * (masked - side),
                (zonal - DIFFUSE) * (side - masked),
            )
            upper = jnp.where(top_row, 0.0, shift(side, -1, 0) - side)
            lower = jnp.where(bottom_row, 0.0, side - shift(side, 1, 0))
            result = (
                tile.side(EDGE_PART + index) + face + side_north * upper + side_south * lower
            )
            side_ref[index * ROWS : (index + 1) * ROWS] = jnp.where(
                side_bottom > level, result, 0.0
            )
        velocity_ref[level * ROWS : (level + 1) * ROWS] = ADVECT_HALF * zonal_total
        velocity_ref[(levels + level) * ROWS : (levels + level + 1) * ROWS] = (
            ADVECT_HALF * merid_total
        )

    for level in range(levels):
        zonal, zonal_west, merid = tile.velocities(1, level)
        north_factor = ADVECT_HALF * merid + DIFFUSE
        south_factor = ADVECT_HALF * shift(merid, 1, 0) - DIFFUSE
        zonal_total = jnp.zeros(tile.shape, jnp.float32)
        merid_total = jnp.zeros(tile.shape, jnp.float32)
        for tracer in range(2):
            index = tracer * levels + level
            masked = tile_of(next_ref, index)
            side = tile_of(side_ref, index)
            to_east = jnp.where(last_lane, side, shift(masked, -1, 1)) - masked
            to_west = masked - jnp.where(first_lane, side, shift(masked, 1, 1))
            to_north = jnp.where(top_row, 0.0, shift(masked, -1, 0) - masked)
            to_south = jnp.where(bottom_row, 0.0, masked - shift(masked, 1, 0))
            adjoint_ref[index * ROWS : (index + 1) * ROWS] = (
                mixed(next_ref, kappa_ref, tracer * levels * ROWS, level, levels)
                + (zonal + DIFFUSE) * to_east
                + (zonal_west - DIFFUSE) * to_west
                + north_factor * to_north
                + south_factor * to_south
            )
            field, field_east = tile.tracer(1, level, tracer)
            zonal_total = zonal_total + (field + field_east) * to_east
            merid_total = merid_total + (field + shift(field, -1, 0)) * to_north
        for total, begin in ((zonal_total, 0), (merid_total, levels)):
            here = slice((begin + level) * ROWS, (begin + level + 1) * ROWS)
            velocity_ref[here] = velocity_ref[here] + ADVECT_HALF * total


def finish_kernel(
    far_ref,
    near_ref,
    pack_ref,
    west_ref,
    east_ref,
    state_ref,
    masked_ref,
    kappa_ref,
    bottom_ref,
    next_ref,
    adjoint_in,
    velocity_in,
    adjoint_hbm,
    velocity_hbm,
    adjoint_ref,
    velocity_ref,
    north_ref,
    south_ref,
    guard_ref,
    out_sem,
):
    levels = masked_ref.shape[0] // (2 * ROWS)
    layout = Layout(levels)
    top = ROWS - 1
    band = lax.axis_index("lat")
    odd_band = lax.rem(band, 2) == 1
    top_band = (band == lax.axis_size("lat") - 1).astype(jnp.int32)
    folded = top_band.astype(jnp.float32)
    open_south = jnp.where(band > 0, DIFFUSE, 0.0)
    square = (LANES, LANES)
    from_lane = rows_of(square)
    turned = from_lane + top_band * (LANES - 1 - 2 * from_lane)
    turn = jnp.where(lanes_of(square) == turned, 1.0, 0.0).astype(jnp.bfloat16)

    @pl.when(odd_band)
    def _():
        north_ref[...] = jnp.dot(far_ref[...], turn, preferred_element_type=jnp.float32)
        south_ref[...] = near_ref[...].astype(jnp.float32)

    @pl.when(jnp.logical_not(odd_band))
    def _():
        north_ref[...] = jnp.dot(near_ref[...], turn, preferred_element_type=jnp.float32)
        south_ref[...] = far_ref[...].astype(jnp.float32)

    copies = []

    def send(source, target, part):
        here = pl.ds(part * levels * ROWS, levels * ROWS)
        copy = pltpu.make_async_copy(source.at[here], target.at[here], out_sem.at[len(copies)])
        copy.start()
        copies.append(copy)

    guard_ref[...] = jnp.zeros_like(guard_ref)

    def rows_at(ref, begin):
        return ref[begin : begin + levels]

    def unpacked(packed):
        return packed, shift(packed, LANES // 2, 1), shift(packed, 96, 1)

    def state_row(at, field, row):
        return strided(state_ref, (at * FIELDS + field) * levels * ROWS + row, levels)

    def add_rows(ref, begin, value):
        here = pl.ds(begin, levels, stride=ROWS)
        ref[here, :] = ref[here, :] + value

    level_of = rows_of((levels, LANES)).astype(jnp.float32)
    lane = lanes_of((levels, LANES))
    first_lane, last_lane = lane == 0, lane == LANES - 1

    def side_depth(row):
        spot = slice(EDGE_MASKED + 2 * levels, EDGE_MASKED + 2 * levels + 1)
        west = west_ref[...].astype(jnp.float32)[row : row + 1, spot]
        east = east_ref[...].astype(jnp.float32)[row : row + 1, spot]
        return jnp.where(lane < LANES // 2, west, east)

    depth = bottom_ref[...].astype(jnp.float32)
    merid_top = state_row(0, 3, top)
    north_merid = rows_at(north_ref, layout.merid[0]) * folded
    south_merid = rows_at(south_ref, layout.merid[0])
    top_factor = ADVECT_HALF * (merid_top - north_merid) + DIFFUSE
    bottom_factor = ADVECT_HALF * south_merid - open_south
    own_corner = (unpacked(rows_at(pack_ref, 4 * levels)), unpacked(rows_at(pack_ref, 0)))
    north_corner = unpacked(rows_at(north_ref, layout.corner))
    south_corner = unpacked(rows_at(south_ref, layout.corner))
    side_top = ADVECT_HALF * (own_corner[1][2] - folded * north_corner[2]) + DIFFUSE
    side_bottom = ADVECT_HALF * south_corner[2] - open_south

    merids = {row: state_row(1, 3, row) for row in (0, top - 1, top)}
    next_north = ADVECT_HALF * (merids[top] - folded * rows_at(north_ref, layout.merid[1])) + DIFFUSE
    next_south = ADVECT_HALF * rows_at(south_ref, layout.merid[1]) - open_south
    east_factors, west_factors, kappas = [], [], []
    for row, begin in ((0, 4 * levels), (top, 0)):
        zonal = state_row(1, 2, row)
        zonal_west = jnp.where(first_lane, rows_at(pack_ref, begin + levels), shift(zonal, 1, 1))
        east_factors.append(ADVECT_HALF * zonal + DIFFUSE)
        west_factors.append(ADVECT_HALF * zonal_west - DIFFUSE)
        kappas.append(
            (strided(kappa_ref, row, levels), strided(kappa_ref, ROWS + row, levels))
        )

    zonal_totals = [jnp.zeros((levels, LANES), jnp.float32) for _ in range(2)]
    merid_totals = {row: jnp.zeros((levels, LANES), jnp.float32) for row in (0, top - 1, top)}
    for tracer in range(2):
        start = tracer * levels * ROWS
        own_top = strided(masked_ref, start + top, levels)
        own_bottom = strided(masked_ref, start, levels)
        north = rows_at(north_ref, layout.masked + tracer * levels)
        south = rows_at(south_ref, layout.masked + tracer * levels)
        north_step, south_step = north - own_top, own_bottom - south
        wet = level_of < north_ref[layout.bottom : layout.bottom + 1]
        ring_north = rows_at(north_ref, layout.part + tracer * levels)
        ring_north = ring_north - (ADVECT_HALF * (north_merid - merid_top) + DIFFUSE) * north_step
        ring_north = jnp.where(wet, ring_north, 0.0)
        wet = level_of < south_ref[layout.bottom : layout.bottom + 1]
        ring_south = rows_at(south_ref, layout.part + tracer * levels)
        ring_south = ring_south + (ADVECT_HALF * south_merid + DIFFUSE) * south_step
        ring_south = jnp.where(wet, ring_south, 0.0)
        first_field = state_row(0, tracer, top) + rows_at(
            north_ref, layout.tracer[0] + tracer * levels
        )
        merid_totals[top] = merid_totals[top] + first_field * north_step
        changes = (
            jnp.where(level_of < depth[0:1], bottom_factor * south_step, 0.0),
            jnp.where(level_of < depth[top:], top_factor * north_step, 0.0),
        )
        side_changes = (
            side_bottom * (own_corner[0][tracer] - south_corner[tracer]),
            side_top * (north_corner[tracer] - own_corner[1][tracer]),
        )
        fields = {row: state_row(1, tracer, row) for row in (0, 1, top - 1, top)}
        for at, row in enumerate((0, top)):
            change = changes[at]
            side = jnp.where(level_of < side_depth(row), side_changes[at], 0.0)
            guard_ref[ROWS : ROWS + levels] = change
            above = guard_ref[ROWS - 1 : ROWS - 1 + levels]
            below = guard_ref[ROWS + 1 : ROWS + 1 + levels]
            kappa_above, kappa_below = kappas[at]
            to_east = jnp.where(last_lane, side, shift(change, -1, 1)) - change
            to_west = change - jnp.where(first_lane, side, shift(change, 1, 1))
            value = (
                change
                + kappa_below * (below - change)
                + kappa_above * (above - change)
                + east_factors[at] * to_east
                + west_factors[at] * to_west
            )
            begin = (4 * levels if row == 0 else 0) + (2 + tracer) * levels
            field_east = jnp.where(
                last_lane, rows_at(pack_ref, begin), shift(fields[row], -1, 1)
            )
            zonal_totals[at] = zonal_totals[at] + (fields[row] + field_east) * to_east
            full = strided(next_ref, start + row, levels) + change
            if row == 0:
                value = value - (ADVECT_HALF * merids[0] + DIFFUSE) * change
                value = value + next_south * (full - ring_south)
                add_rows(adjoint_ref, start + 1, -(ADVECT_HALF * merids[0] - DIFFUSE) * change)
                merid_totals[0] = merid_totals[0] - (fields[0] + fields[1]) * change
            else:
                value = value + (ADVECT_HALF * merids[top - 1] - DIFFUSE) * change
                value = value + next_north * (ring_north - full)
                inner = (ADVECT_HALF * merids[top - 1] + DIFFUSE) * change
                add_rows(adjoint_ref, start + top - 1, inner)
                merid_totals[top - 1] = (
                    merid_totals[top - 1] + (fields[top - 1] + fields[top]) * change
                )
                field_north = rows_at(north_ref, layout.tracer[1] + tracer * levels)
                merid_totals[top] = merid_totals[top] + (fields[top] + field_north) * (
                    ring_north - full
                )
            add_rows(adjoint_ref, start + row, value)
        send(adjoint_ref, adjoint_hbm, tracer)
    for at, row in enumerate((0, top)):
        add_rows(velocity_ref, row, ADVECT_HALF * zonal_totals[at])
    send(velocity_ref, velocity_hbm, 0)
    for row, total in merid_totals.items():
        add_rows(velocity_ref, levels * ROWS + row, ADVECT_HALF * total)
    send(velocity_ref, velocity_hbm, 1)
    for copy in copies:
        copy.wait()


def swaps(pairs):
    return [pair for low, high in pairs for pair in ((low, high), (high, low))]


def ring_routes(tiles):
    inner = swaps((tile, tile + 1) for tile in range(0, tiles, 2))
    outer = swaps((tile, (tile + 1) % tiles) for tile in range(1, tiles, 2))
    return inner, outer


def line_routes(tiles, bands):
    near, far = [], []
    for tile in range(tiles):
        start = tile * bands
        near += [(start + band, start + band + 1) for band in range(0, bands, 2)]
        far += [(start + band, start + band + 1) for band in range(1, bands - 1, 2)]
        if tile < tiles // 2:
            far.append((start + bands - 1, (tiles - tile) * bands - 1))
    return swaps(near), swaps(far)


def call(kernel, outputs, scratch, scalars, arrays):
    vmem = pl.BlockSpec(memory_space=pltpu.VMEM)
    smem = pl.BlockSpec(memory_space=pltpu.SMEM)
    return pl.pallas_call(
        kernel,
        out_shape=[jax.ShapeDtypeStruct(shape, dtype) for shape, dtype in outputs],
        in_specs=[smem] * len(scalars) + [vmem] * len(arrays),
        out_specs=[vmem] * len(outputs),
        scratch_shapes=[pltpu.VMEM(shape, jnp.float32) for shape in scratch],
        compiler_params=pltpu.CompilerParams(vmem_limit_bytes=32 * 1024 * 1024),
    )(*scalars, *arrays)


def shards(final_adjoint, store, holder_offset, holder_slot, bottom_level, mix_class, mix_table):
    bands = lax.axis_size("lat")
    tiles = lax.axis_size("lon")
    levels = final_adjoint.shape[1]
    slots = store.shape[2]
    steps = len(STEP_ORDER)
    pieces = FIELDS * levels
    full = levels * ROWS
    layout = Layout(levels)
    narrow, wide = jnp.bfloat16, jnp.float32
    hbm = pl.BlockSpec(memory_space=pltpu.HBM)
    request = pl.pallas_call(
        request_kernel,
        out_shape=jax.ShapeDtypeStruct((bands, steps, pieces, LANES), narrow),
        in_specs=[hbm, hbm],
        out_specs=hbm,
        scratch_shapes=[
            pltpu.SMEM(holder_slot.shape, jnp.int32),
            pltpu.VMEM((pieces * slots, LANES), narrow),
            pltpu.VMEM((pieces * slots, LANES), wide),
            pltpu.VMEM((bands, steps, pieces, LANES), narrow),
            pltpu.SemaphoreType.DMA,
            pltpu.SemaphoreType.DMA((FIELDS,)),
            pltpu.SemaphoreType.DMA((bands,)),
        ],
        compiler_params=pltpu.CompilerParams(vmem_limit_bytes=32 * 1024 * 1024),
    )(
        pltpu.with_memory_space_constraint(holder_slot, pltpu.HBM),
        pltpu.with_memory_space_constraint(store.reshape(pieces * slots, LANES), pltpu.HBM),
    )
    received = lax.all_to_all(request, "lat", split_axis=0, concat_axis=0, tiled=True)
    masked, base, kappa, side, pick, holder = call(
        prepare_kernel,
        [
            ((2 * full, LANES), wide),
            ((2 * full, LANES), wide),
            ((full + ROWS, LANES), wide),
            ((4 * ROWS, 2 * LANES), wide),
            ((steps, ROWS * LANES, LANES), narrow),
            ((len(DRAFT_ROWS) * ROWS, LANES), wide),
        ],
        [(2 * LANES, LANES)],
        [mix_table, holder_offset],
        [
            final_adjoint.reshape(2 * full, LANES),
            bottom_level,
            mix_class.reshape((levels - 1) * ROWS, LANES),
        ],
    )
    outer, inner = call(
        edges_kernel,
        [((ROWS, EDGE_LANES), narrow), ((ROWS, EDGE_LANES), narrow)],
        [(EDGE_MASKED, LANES)],
        [],
        [received, side, pick],
    )
    inner_routes, outer_routes = ring_routes(tiles)
    near_routes, far_routes = line_routes(tiles, bands)
    outer = lax.ppermute(outer, "lon", outer_routes)
    inner = lax.ppermute(inner, "lon", inner_routes)
    top, bot = call(
        drafts_kernel,
        [((layout.rows, LANES), wide), ((layout.rows, LANES), wide)],
        [(len(DRAFT_ROWS) * pieces, LANES)],
        [],
        [received, holder, masked, base, bottom_level],
    )
    far, near, west, east, pack = call(
        functools.partial(complete_kernel, levels),
        [
            ((layout.rows, LANES), narrow),
            ((layout.rows, LANES), narrow),
            ((ROWS, EDGE_LANES), narrow),
            ((ROWS, EDGE_LANES), narrow),
            ((8 * levels, LANES), wide),
        ],
        [(LANES, EDGE_LANES), (EDGE_LANES, LANES), (layout.rows, LANES), (layout.rows, LANES)],
        [],
        [inner, outer, top, bot],
    )
    far = lax.ppermute(far, ("lon", "lat"), far_routes)
    near = lax.ppermute(near, ("lon", "lat"), near_routes)
    (state,) = call(
        tiles_kernel,
        [((steps * FIELDS * full, LANES), wide)],
        [],
        [holder_offset],
        [received, west],
    )
    adjoint, velocity, following = call(
        steps_kernel,
        [((2 * full, LANES), wide)] * 3,
        [(2 * full, LANES)],
        [],
        [west, east, state, masked, base, kappa, bottom_level],
    )
    arrays = (far, near, pack, west, east, state, masked, kappa, bottom_level, following)
    arrays += (adjoint, velocity)
    vmem = pl.BlockSpec(memory_space=pltpu.VMEM)
    adjoint, velocity, _, _ = pl.pallas_call(
        finish_kernel,
        out_shape=[jax.ShapeDtypeStruct((2 * full, LANES), wide)] * 4,
        in_specs=[vmem] * len(arrays),
        out_specs=[hbm, hbm, vmem, vmem],
        input_output_aliases={len(arrays) - 2: 2, len(arrays) - 1: 3},
        scratch_shapes=[
            pltpu.VMEM((layout.rows, LANES), wide),
            pltpu.VMEM((layout.rows, LANES), wide),
            pltpu.VMEM(((levels + 2 * ROWS + ROWS - 1) // ROWS * ROWS, LANES), wide),
            pltpu.SemaphoreType.DMA((4,)),
        ],
        compiler_params=pltpu.CompilerParams(vmem_limit_bytes=32 * 1024 * 1024),
    )(*arrays)
    shape = (2, levels, ROWS, LANES)
    return adjoint.reshape(shape), velocity.reshape(shape)


def solution(mesh):
    return jax.shard_map(
        shards,
        mesh=mesh,
        in_specs=(
            P(None, None, "lat", "lon"),
            P(None, None, None, "lat", "lon"),
            P(),
            P(),
            P("lat", "lon"),
            P(None, "lat", "lon"),
            P(),
        ),
        out_specs=(P(None, None, "lat", "lon"), P(None, None, "lat", "lon")),
        check_vma=False,
    )
```

```python
import functools

import jax
import jax.numpy as jnp
from jax import lax
from jax.experimental import pallas as pl
from jax.experimental.pallas import tpu as pltpu
from jax.sharding import PartitionSpec as P

STEP_ORDER = (1, 0)
FIELDS = 4
ADVECT_HALF = 0.125
DIFFUSE = 0.1

ROWS = 8
LANES = 128

EDGE_STATE = (0, 256)
EDGE_MASKED = 512
EDGE_PART = 640
EDGE_LANES = 768


DRAFT_ROWS = ((ROWS - 1, 0), (ROWS - 1, 1), (0, 0), (0, 1), (ROWS - 2, 0))


class Layout:
    def __init__(self, levels):
        self.tracer = (0, 3 * levels)
        self.merid = (2 * levels, 5 * levels)
        self.masked = 6 * levels
        self.part = 8 * levels
        self.corner = 10 * levels
        self.bottom = 11 * levels
        self.rows = (11 * levels + 1 + 15) // 16 * 16


def shift(block, amount, axis):
    return pltpu.roll(block, amount % block.shape[axis], axis)


def lanes_of(shape):
    return lax.broadcasted_iota(jnp.int32, shape, 1)


def rows_of(shape):
    return lax.broadcasted_iota(jnp.int32, shape, 0)


def strided(ref, start, count):
    return ref[pl.ds(start, count, stride=ROWS), :]


def request_kernel(
    slot_hbm, store_hbm, out_hbm, slot_ref, store_ref, wide_ref, pack_ref, slot_sem, in_sem, out_sem
):
    tile = lax.axis_index("lon")
    bands, steps, pieces, lanes = pack_ref.shape
    slots = store_ref.shape[0] // pieces
    length = store_ref.shape[0] // FIELDS
    table = pltpu.make_async_copy(slot_hbm, slot_ref, slot_sem)
    table.start()
    loads = []
    for field in range(FIELDS):
        here = pl.ds(field * length, length)
        load = pltpu.make_async_copy(store_hbm.at[here], store_ref.at[here], in_sem.at[field])
        load.start()
        loads.append(load)
    for field, load in enumerate(loads):
        load.wait()
        here = slice(field * length, (field + 1) * length)
        wide_ref[here] = store_ref[here].astype(jnp.float32)
    table.wait()
    stores = []
    for band in range(bands):
        for at, step in enumerate(STEP_ORDER):
            slot = slot_ref[step, band, tile]
            rows = wide_ref[pl.ds(slot, pieces, stride=slots), :]
            pack_ref[band, at] = rows.astype(jnp.bfloat16)
        store = pltpu.make_async_copy(pack_ref.at[band], out_hbm.at[band], out_sem.at[band])
        store.start()
        stores.append(store)
    for store in stores:
        store.wait()


def pick_columns(offset=0):
    place = (ROWS * LANES, LANES)
    row, source = rows_of(place) // LANES, rows_of(place) % LANES
    order = lanes_of(place) - (row + ROWS - offset) % ROWS
    chosen = (
        ((source == 0) & (order == 0))
        | ((source == LANES - 1) & (order == ROWS))
        | ((source == 1) & (order == 2 * ROWS))
        | ((source == LANES - 2) & (order == 3 * ROWS))
    )
    return jnp.where(chosen, 1.0, 0.0).astype(jnp.bfloat16)


def prepare_kernel(
    table_ref,
    offset_ref,
    adjoint_ref,
    bottom_ref,
    mix_ref,
    masked_ref,
    base_ref,
    kappa_ref,
    side_ref,
    pick_ref,
    holder_ref,
    column_ref,
):
    levels = adjoint_ref.shape[0] // (2 * ROWS)
    bottom = bottom_ref[...]
    edge = jnp.zeros((ROWS, LANES), jnp.float32)
    kappa_ref[0:ROWS] = edge
    kappa_ref[levels * ROWS : (levels + 1) * ROWS] = edge
    for level in range(levels - 1):
        classes = mix_ref[level * ROWS : (level + 1) * ROWS]
        kappa = jnp.full((ROWS, LANES), table_ref[0], jnp.float32)
        for index in range(1, table_ref.shape[0]):
            kappa = jnp.where(classes == index, table_ref[index], kappa)
        kappa_ref[(level + 1) * ROWS : (level + 2) * ROWS] = kappa
    for tracer in range(2):
        start = tracer * levels * ROWS
        for level in range(levels):
            here = slice(start + level * ROWS, start + (level + 1) * ROWS)
            masked_ref[here] = jnp.where(level < bottom, adjoint_ref[here], 0.0)
        for level in range(levels):
            base_ref[start + level * ROWS : start + (level + 1) * ROWS] = mixed(
                masked_ref, kappa_ref, start, level, levels
            )
    pick = pick_columns()
    offsets = []
    for at, step in enumerate(STEP_ORDER):
        offset = offset_ref[step, lax.axis_index("lat"), lax.axis_index("lon")]
        pick_ref[at] = pick_columns(offset)
        offsets.append(offset)
    for index, (row, at) in enumerate(DRAFT_ROWS):
        held = rows_of((ROWS, LANES)) == lax.rem(row + offsets[at], ROWS)
        holder_ref[index * ROWS : (index + 1) * ROWS] = jnp.where(held, 1.0, 0.0)
    column_ref[...] = jnp.zeros_like(column_ref)
    rows = 2 * levels
    for start, ref in ((0, masked_ref), (LANES, base_ref)):
        blocks = [strided(ref, row, rows).astype(jnp.bfloat16) for row in range(ROWS)]
        column_ref[start : start + rows] = jnp.dot(
            jnp.concatenate(blocks, axis=1), pick, preferred_element_type=jnp.float32
        )
    side = jnp.transpose(column_ref[...])[0 : 4 * ROWS]
    spot = lanes_of((ROWS, 2 * LANES)) == rows
    depth = bottom.astype(jnp.float32)
    side_ref[...] = side
    side_ref[0:ROWS] = jnp.where(spot, depth[:, 0:1], side[0:ROWS])
    side_ref[ROWS : 2 * ROWS] = jnp.where(spot, depth[:, LANES - 1 :], side[ROWS : 2 * ROWS])


def mixed(masked_ref, kappa_ref, start, level, levels):
    def at(index):
        return masked_ref[start + index * ROWS : start + (index + 1) * ROWS]

    masked = at(level)
    below = at(level + 1) if level + 1 < levels else jnp.zeros_like(masked)
    above = at(level - 1) if level > 0 else jnp.zeros_like(masked)
    kappa_above = kappa_ref[level * ROWS : (level + 1) * ROWS]
    kappa_below = kappa_ref[(level + 1) * ROWS : (level + 2) * ROWS]
    return masked + kappa_below * (below - masked) + kappa_above * (above - masked)


def edges_kernel(piece_ref, side_ref, pick_ref, outer_ref, inner_ref, column_ref):
    tile = lax.axis_index("lon")
    holders, steps, pieces, _ = piece_ref.shape
    levels = pieces // FIELDS
    column_ref[...] = jnp.zeros_like(column_ref)
    for at in range(steps):
        chunks = [piece_ref[holder, at] for holder in range(holders)]
        column_ref[EDGE_STATE[at] : EDGE_STATE[at] + pieces] = jnp.dot(
            jnp.concatenate(chunks, axis=1), pick_ref[at], preferred_element_type=jnp.float32
        )
    state = jnp.transpose(column_ref[...])
    lane = lanes_of((ROWS, 2 * LANES))
    sides = []
    for at, sign in ((0, 1.0), (1, -1.0)):
        edge = state[at * ROWS : (at + 1) * ROWS]
        zonal = edge if at == 0 else state[3 * ROWS : 4 * ROWS]
        zonal = zonal[:, 0 : 2 * LANES]
        zonal = jnp.where(lane < levels, shift(zonal, -2 * levels, 1), shift(zonal, -levels, 1))
        masked = side_ref[at * ROWS : (at + 1) * ROWS]
        beside = side_ref[(at + 2) * ROWS : (at + 3) * ROWS]
        face = (ADVECT_HALF * zonal + sign * DIFFUSE) * (sign * (beside - masked))
        part = masked[:, LANES:] + face[:, 0:LANES]
        side = jnp.concatenate([edge, masked[:, 0:LANES], part], axis=1)
        sides.append(side.astype(jnp.bfloat16))
    to_west, to_east = sides

    @pl.when(lax.rem(tile, 2) == 0)
    def _():
        inner_ref[...] = to_east
        outer_ref[...] = to_west

    @pl.when(lax.rem(tile, 2) == 1)
    def _():
        inner_ref[...] = to_west
        outer_ref[...] = to_east


def tiles_kernel(offset_ref, piece_ref, west_ref, state_ref):
    tile = lax.axis_index("lon")
    band = lax.axis_index("lat")
    holders, _, pieces, _ = piece_ref.shape
    for at, step in enumerate(STEP_ORDER):
        offset = offset_ref[step, band, tile]
        for row in range(ROWS):
            chunk = piece_ref[lax.rem(row + offset, holders), at]
            state_ref[pl.ds(at * pieces * ROWS + row, pieces, stride=ROWS), :] = chunk.astype(
                jnp.float32
            )


def drafts_kernel(
    piece_ref, holder_ref, masked_ref, base_ref, bottom_ref, top_ref, bot_ref, line_ref
):
    levels = masked_ref.shape[0] // (2 * ROWS)
    holders, steps, pieces, _ = piece_ref.shape
    for at in range(steps):
        wanted = [index for index, (_, step) in enumerate(DRAFT_ROWS) if step == at]
        found = [None] * len(wanted)
        for holder in range(holders):
            chunk = piece_ref[holder, at].astype(jnp.float32)
            for place, index in enumerate(wanted):
                if holder == 0:
                    found[place] = chunk
                    continue
                here = index * ROWS + holder
                held = jnp.broadcast_to(holder_ref[here : here + 1], chunk.shape) > 0.0
                found[place] = jnp.where(held, chunk, found[place])
        for place, index in enumerate(wanted):
            line_ref[index * pieces : (index + 1) * pieces] = found[place]
    bottom = bottom_ref[...].astype(jnp.float32)
    layout = Layout(levels)
    wide = lanes_of((levels, LANES))
    for row, inner, first, facing, draft_ref in (
        (ROWS - 1, ROWS - 2, 0, 4, top_ref),
        (0, 1, 2, 2, bot_ref),
    ):
        for at in range(2):
            begin = (first + at) * pieces
            draft_ref[layout.tracer[at] : layout.tracer[at] + 2 * levels] = line_ref[
                begin : begin + 2 * levels
            ]
            draft_ref[layout.merid[at] : layout.merid[at] + levels] = line_ref[
                begin + 3 * levels : begin + 4 * levels
            ]
        zonal = line_ref[first * pieces + 2 * levels : first * pieces + 3 * levels]
        merid = line_ref[facing * pieces + 3 * levels : facing * pieces + 4 * levels]
        east_factor = ADVECT_HALF * zonal + DIFFUSE
        west_factor = ADVECT_HALF * shift(zonal, 1, 1) - DIFFUSE
        for tracer in range(2):
            begin = tracer * levels * ROWS
            masked = strided(masked_ref, begin + row, levels)
            next_row = strided(masked_ref, begin + inner, levels)
            if row > inner:
                along = (ADVECT_HALF * merid - DIFFUSE) * (masked - next_row)
            else:
                along = (ADVECT_HALF * merid + DIFFUSE) * (next_row - masked)
            east = east_factor * (shift(masked, -1, 1) - masked)
            west = west_factor * (masked - shift(masked, 1, 1))
            part = strided(base_ref, begin + row, levels) + along
            part = part + jnp.where(wide < LANES - 1, east, 0.0) + jnp.where(wide > 0, west, 0.0)
            at_masked = layout.masked + tracer * levels
            at_part = layout.part + tracer * levels
            draft_ref[at_masked : at_masked + levels] = masked
            draft_ref[at_part : at_part + levels] = part
        draft_ref[layout.corner : layout.corner + levels] = zonal
        draft_ref[layout.bottom : layout.rows] = jnp.broadcast_to(
            bottom[row : row + 1], (layout.rows - layout.bottom, LANES)
        )


def complete_kernel(
    levels,
    outer_ref,
    inner_ref,
    top_draft_ref,
    bot_draft_ref,
    far_ref,
    near_ref,
    west_ref,
    east_ref,
    pack_ref,
    edge_ref,
    column_ref,
    top_ref,
    bot_ref,
):
    layout = Layout(levels)
    odd_tile = lax.rem(lax.axis_index("lon"), 2) == 1
    odd_band = lax.rem(lax.axis_index("lat"), 2) == 1

    @pl.when(odd_tile)
    def _():
        west_ref[...] = inner_ref[...]
        east_ref[...] = outer_ref[...]

    @pl.when(jnp.logical_not(odd_tile))
    def _():
        west_ref[...] = outer_ref[...]
        east_ref[...] = inner_ref[...]

    top_ref[...] = top_draft_ref[...]
    bot_ref[...] = bot_draft_ref[...]
    edge_ref[...] = jnp.zeros_like(edge_ref)
    edge_ref[0:ROWS] = west_ref[...].astype(jnp.float32)
    edge_ref[ROWS : 2 * ROWS] = east_ref[...].astype(jnp.float32)
    column_ref[...] = jnp.transpose(edge_ref[...])
    lane = lanes_of((levels, LANES))

    def pair(start, row):
        block = column_ref[start : start + levels]
        return block[:, row : row + 1], block[:, ROWS + row : ROWS + row + 1]

    for row, draft_ref in ((ROWS - 1, top_ref), (0, bot_ref)):
        zonal = draft_ref[layout.corner : layout.corner + levels]
        zonal_west, _ = pair(EDGE_STATE[0] + 2 * levels, row)
        merid_west, merid_east = pair(EDGE_STATE[0] + 3 * levels, row)
        east_factor = ADVECT_HALF * zonal + DIFFUSE
        west_factor = ADVECT_HALF * zonal_west - DIFFUSE
        corner = jnp.where((lane == 32) | (lane == 96), merid_west, 0.0)
        corner = jnp.where((lane == 31) | (lane == 95), merid_east, corner)
        for tracer in range(2):
            west, east = pair(EDGE_MASKED + tracer * levels, row)
            at_masked = layout.masked + tracer * levels
            at_part = layout.part + tracer * levels
            masked = draft_ref[at_masked : at_masked + levels]
            face = jnp.where(lane == LANES - 1, east_factor * (east - masked), 0.0)
            face = jnp.where(lane == 0, west_factor * (masked - west), face)
            draft_ref[at_part : at_part + levels] = draft_ref[at_part : at_part + levels] + face
            corner = jnp.where(lane == (0, LANES // 2)[tracer], west, corner)
            corner = jnp.where(lane == (LANES - 1, LANES // 2 - 1)[tracer], east, corner)
        draft_ref[layout.corner : layout.corner + levels] = corner
        begin = 0 if row else 4 * levels
        pack_ref[begin : begin + levels] = corner
        zonal_west, _ = pair(EDGE_STATE[1] + 2 * levels, row)
        pack_ref[begin + levels : begin + 2 * levels] = jnp.broadcast_to(
            zonal_west, (levels, LANES)
        )
        for tracer in range(2):
            _, east = pair(EDGE_STATE[1] + tracer * levels, row)
            here = begin + (2 + tracer) * levels
            pack_ref[here : here + levels] = jnp.broadcast_to(east, (levels, LANES))

    @pl.when(odd_band)
    def _():
        near_ref[...] = bot_ref[...].astype(jnp.bfloat16)
        far_ref[...] = top_ref[...].astype(jnp.bfloat16)

    @pl.when(jnp.logical_not(odd_band))
    def _():
        near_ref[...] = top_ref[...].astype(jnp.bfloat16)
        far_ref[...] = bot_ref[...].astype(jnp.bfloat16)


class Tile:
    def __init__(self, levels, west_ref, east_ref, state_ref):
        self.levels = levels
        self.west_ref, self.east_ref, self.state_ref = west_ref, east_ref, state_ref
        self.shape = (ROWS, LANES)
        lane, row = lanes_of(self.shape), rows_of(self.shape)
        self.first_lane, self.last_lane = lane == 0, lane == LANES - 1
        self.bottom_row, self.top_row = row == 0, row == ROWS - 1

    def spread(self, ref, index):
        return jnp.broadcast_to(ref[:, index : index + 1].astype(jnp.float32), self.shape)

    def line(self, ref, index):
        return jnp.broadcast_to(ref[index : index + 1], self.shape)

    def side(self, index):
        return jnp.where(
            self.first_lane, self.spread(self.west_ref, index), self.spread(self.east_ref, index)
        )

    def velocities(self, at, level):
        begin = at * FIELDS * self.levels
        zonal = tile_of(self.state_ref, begin + 2 * self.levels + level)
        merid = tile_of(self.state_ref, begin + 3 * self.levels + level)
        zonal_west = jnp.where(
            self.first_lane,
            self.spread(self.west_ref, EDGE_STATE[at] + 2 * self.levels + level),
            shift(zonal, 1, 1),
        )
        return ADVECT_HALF * zonal, ADVECT_HALF * zonal_west, merid

    def tracer(self, at, level, tracer):
        field = tile_of(self.state_ref, (at * FIELDS + tracer) * self.levels + level)
        east = jnp.where(
            self.last_lane,
            self.spread(self.east_ref, EDGE_STATE[at] + tracer * self.levels + level),
            shift(field, -1, 1),
        )
        return field, east


def tile_of(ref, index):
    return ref[index * ROWS : (index + 1) * ROWS]


def steps_kernel(
    west_ref,
    east_ref,
    state_ref,
    masked_ref,
    base_ref,
    kappa_ref,
    bottom_ref,
    adjoint_ref,
    velocity_ref,
    next_ref,
    side_ref,
):
    levels = masked_ref.shape[0] // (2 * ROWS)
    tile = Tile(levels, west_ref, east_ref, state_ref)
    first_lane, last_lane = tile.first_lane, tile.last_lane
    top_row, bottom_row = tile.top_row, tile.bottom_row
    bottom = bottom_ref[...]
    side_bottom = tile.side(EDGE_MASKED + 2 * levels)
    for level in range(levels):
        zonal, zonal_west, merid = tile.velocities(0, level)
        north_factor = ADVECT_HALF * merid + DIFFUSE
        south_factor = ADVECT_HALF * shift(merid, 1, 0) - DIFFUSE
        side_merid = tile.side(EDGE_STATE[0] + 3 * levels + level)
        side_north = ADVECT_HALF * side_merid + DIFFUSE
        side_south = ADVECT_HALF * shift(side_merid, 1, 0) - DIFFUSE
        zonal_total = jnp.zeros(tile.shape, jnp.float32)
        merid_total = jnp.zeros(tile.shape, jnp.float32)
        for tracer in range(2):
            index = tracer * levels + level
            masked = tile_of(masked_ref, index)
            west = tile.spread(west_ref, EDGE_MASKED + index)
            east = tile.spread(east_ref, EDGE_MASKED + index)
            side = jnp.where(first_lane, west, east)
            to_east = jnp.where(last_lane, east, shift(masked, -1, 1)) - masked
            to_west = masked - jnp.where(first_lane, west, shift(masked, 1, 1))
            to_north = jnp.where(top_row, 0.0, shift(masked, -1, 0) - masked)
            to_south = jnp.where(bottom_row, 0.0, masked - shift(masked, 1, 0))
            result = (
                tile_of(base_ref, index)
                + (zonal + DIFFUSE) * to_east
                + (zonal_west - DIFFUSE) * to_west
                + north_factor * to_north
                + south_factor * to_south
            )
            next_ref[index * ROWS : (index + 1) * ROWS] = jnp.where(level < bottom, result, 0.0)
            field, field_east = tile.tracer(0, level, tracer)
            zonal_total = zonal_total + (field + field_east) * to_east
            merid_total = merid_total + (field + shift(field, -1, 0)) * to_north
            face = jnp.where(
                first_lane,
                (zonal_west + DIFFUSE) * (masked - side),
                (zonal - DIFFUSE) * (side - masked),
            )
            upper = jnp.where(top_row, 0.0, shift(side, -1, 0) - side)
            lower = jnp.where(bottom_row, 0.0, side - shift(side, 1, 0))
            result = (
                tile.side(EDGE_PART + index) + face + side_north * upper + side_south * lower
            )
            side_ref[index * ROWS : (index + 1) * ROWS] = jnp.where(
                side_bottom > level, result, 0.0
            )
        velocity_ref[level * ROWS : (level + 1) * ROWS] = ADVECT_HALF * zonal_total
        velocity_ref[(levels + level) * ROWS : (levels + level + 1) * ROWS] = (
            ADVECT_HALF * merid_total
        )

    for level in range(levels):
        zonal, zonal_west, merid = tile.velocities(1, level)
        north_factor = ADVECT_HALF * merid + DIFFUSE
        south_factor = ADVECT_HALF * shift(merid, 1, 0) - DIFFUSE
        zonal_total = jnp.zeros(tile.shape, jnp.float32)
        merid_total = jnp.zeros(tile.shape, jnp.float32)
        for tracer in range(2):
            index = tracer * levels + level
            masked = tile_of(next_ref, index)
            side = tile_of(side_ref, index)
            to_east = jnp.where(last_lane, side, shift(masked, -1, 1)) - masked
            to_west = masked - jnp.where(first_lane, side, shift(masked, 1, 1))
            to_north = jnp.where(top_row, 0.0, shift(masked, -1, 0) - masked)
            to_south = jnp.where(bottom_row, 0.0, masked - shift(masked, 1, 0))
            adjoint_ref[index * ROWS : (index + 1) * ROWS] = (
                mixed(next_ref, kappa_ref, tracer * levels * ROWS, level, levels)
                + (zonal + DIFFUSE) * to_east
                + (zonal_west - DIFFUSE) * to_west
                + north_factor * to_north
                + south_factor * to_south
            )
            field, field_east = tile.tracer(1, level, tracer)
            zonal_total = zonal_total + (field + field_east) * to_east
            merid_total = merid_total + (field + shift(field, -1, 0)) * to_north
        for total, begin in ((zonal_total, 0), (merid_total, levels)):
            here = slice((begin + level) * ROWS, (begin + level + 1) * ROWS)
            velocity_ref[here] = velocity_ref[here] + ADVECT_HALF * total


def finish_kernel(
    far_ref,
    near_ref,
    pack_ref,
    west_ref,
    east_ref,
    state_ref,
    masked_ref,
    kappa_ref,
    bottom_ref,
    next_ref,
    adjoint_in,
    velocity_in,
    adjoint_hbm,
    velocity_hbm,
    adjoint_ref,
    velocity_ref,
    north_ref,
    south_ref,
    guard_ref,
    out_sem,
):
    levels = masked_ref.shape[0] // (2 * ROWS)
    layout = Layout(levels)
    top = ROWS - 1
    band = lax.axis_index("lat")
    odd_band = lax.rem(band, 2) == 1
    top_band = (band == lax.axis_size("lat") - 1).astype(jnp.int32)
    folded = top_band.astype(jnp.float32)
    open_south = jnp.where(band > 0, DIFFUSE, 0.0)

    @pl.when(odd_band & (top_band == 0))
    def _():
        north_ref[...] = far_ref[...].astype(jnp.float32)

    @pl.when(odd_band & (top_band == 1))
    def _():
        square = (LANES, LANES)
        turn = lanes_of(square) + rows_of(square) == LANES - 1
        turn = jnp.where(turn, 1.0, 0.0).astype(jnp.bfloat16)
        north_ref[...] = jnp.dot(far_ref[...], turn, preferred_element_type=jnp.float32)

    @pl.when(odd_band)
    def _():
        south_ref[...] = near_ref[...].astype(jnp.float32)

    @pl.when(jnp.logical_not(odd_band))
    def _():
        north_ref[...] = near_ref[...].astype(jnp.float32)
        south_ref[...] = far_ref[...].astype(jnp.float32)

    copies = []

    def send(source, target, part):
        here = pl.ds(part * levels * ROWS, levels * ROWS)
        copy = pltpu.make_async_copy(source.at[here], target.at[here], out_sem.at[len(copies)])
        copy.start()
        copies.append(copy)

    guard_ref[...] = jnp.zeros_like(guard_ref)

    def rows_at(ref, begin):
        return ref[begin : begin + levels]

    def unpacked(packed):
        return packed, shift(packed, LANES // 2, 1), shift(packed, 96, 1)

    def state_row(at, field, row):
        return strided(state_ref, (at * FIELDS + field) * levels * ROWS + row, levels)

    def add_rows(ref, begin, value):
        here = pl.ds(begin, levels, stride=ROWS)
        ref[here, :] = ref[here, :] + value

    level_of = rows_of((levels, LANES)).astype(jnp.float32)
    lane = lanes_of((levels, LANES))
    first_lane, last_lane = lane == 0, lane == LANES - 1

    def side_depth(row):
        spot = slice(EDGE_MASKED + 2 * levels, EDGE_MASKED + 2 * levels + 1)
        west = west_ref[...].astype(jnp.float32)[row : row + 1, spot]
        east = east_ref[...].astype(jnp.float32)[row : row + 1, spot]
        return jnp.where(lane < LANES // 2, west, east)

    depth = bottom_ref[...].astype(jnp.float32)
    merid_top = state_row(0, 3, top)
    north_merid = rows_at(north_ref, layout.merid[0]) * folded
    south_merid = rows_at(south_ref, layout.merid[0])
    top_factor = ADVECT_HALF * (merid_top - north_merid) + DIFFUSE
    bottom_factor = ADVECT_HALF * south_merid - open_south
    own_corner = (unpacked(rows_at(pack_ref, 4 * levels)), unpacked(rows_at(pack_ref, 0)))
    north_corner = unpacked(rows_at(north_ref, layout.corner))
    south_corner = unpacked(rows_at(south_ref, layout.corner))
    side_top = ADVECT_HALF * (own_corner[1][2] - folded * north_corner[2]) + DIFFUSE
    side_bottom = ADVECT_HALF * south_corner[2] - open_south

    merids = {row: state_row(1, 3, row) for row in (0, top - 1, top)}
    next_north = ADVECT_HALF * (merids[top] - folded * rows_at(north_ref, layout.merid[1])) + DIFFUSE
    next_south = ADVECT_HALF * rows_at(south_ref, layout.merid[1]) - open_south
    east_factors, west_factors, kappas = [], [], []
    for row, begin in ((0, 4 * levels), (top, 0)):
        zonal = state_row(1, 2, row)
        zonal_west = jnp.where(first_lane, rows_at(pack_ref, begin + levels), shift(zonal, 1, 1))
        east_factors.append(ADVECT_HALF * zonal + DIFFUSE)
        west_factors.append(ADVECT_HALF * zonal_west - DIFFUSE)
        kappas.append(
            (strided(kappa_ref, row, levels), strided(kappa_ref, ROWS + row, levels))
        )

    zonal_totals = [jnp.zeros((levels, LANES), jnp.float32) for _ in range(2)]
    merid_totals = {row: jnp.zeros((levels, LANES), jnp.float32) for row in (0, top - 1, top)}
    for tracer in range(2):
        start = tracer * levels * ROWS
        own_top = strided(masked_ref, start + top, levels)
        own_bottom = strided(masked_ref, start, levels)
        north = rows_at(north_ref, layout.masked + tracer * levels)
        south = rows_at(south_ref, layout.masked + tracer * levels)
        north_step, south_step = north - own_top, own_bottom - south
        wet = level_of < north_ref[layout.bottom : layout.bottom + 1]
        ring_north = rows_at(north_ref, layout.part + tracer * levels)
        ring_north = ring_north - (ADVECT_HALF * (north_merid - merid_top) + DIFFUSE) * north_step
        ring_north = jnp.where(wet, ring_north, 0.0)
        wet = level_of < south_ref[layout.bottom : layout.bottom + 1]
        ring_south = rows_at(south_ref, layout.part + tracer * levels)
        ring_south = ring_south + (ADVECT_HALF * south_merid + DIFFUSE) * south_step
        ring_south = jnp.where(wet, ring_south, 0.0)
        first_field = state_row(0, tracer, top) + rows_at(
            north_ref, layout.tracer[0] + tracer * levels
        )
        merid_totals[top] = merid_totals[top] + first_field * north_step
        changes = (
            jnp.where(level_of < depth[0:1], bottom_factor * south_step, 0.0),
            jnp.where(level_of < depth[top:], top_factor * north_step, 0.0),
        )
        side_changes = (
            side_bottom * (own_corner[0][tracer] - south_corner[tracer]),
            side_top * (north_corner[tracer] - own_corner[1][tracer]),
        )
        fields = {row: state_row(1, tracer, row) for row in (0, 1, top - 1, top)}
        for at, row in enumerate((0, top)):
            change = changes[at]
            side = jnp.where(level_of < side_depth(row), side_changes[at], 0.0)
            guard_ref[ROWS : ROWS + levels] = change
            above = guard_ref[ROWS - 1 : ROWS - 1 + levels]
            below = guard_ref[ROWS + 1 : ROWS + 1 + levels]
            kappa_above, kappa_below = kappas[at]
            to_east = jnp.where(last_lane, side, shift(change, -1, 1)) - change
            to_west = change - jnp.where(first_lane, side, shift(change, 1, 1))
            value = (
                change
                + kappa_below * (below - change)
                + kappa_above * (above - change)
                + east_factors[at] * to_east
                + west_factors[at] * to_west
            )
            begin = (4 * levels if row == 0 else 0) + (2 + tracer) * levels
            field_east = jnp.where(
                last_lane, rows_at(pack_ref, begin), shift(fields[row], -1, 1)
            )
            zonal_totals[at] = zonal_totals[at] + (fields[row] + field_east) * to_east
            full = strided(next_ref, start + row, levels) + change
            if row == 0:
                value = value - (ADVECT_HALF * merids[0] + DIFFUSE) * change
                value = value + next_south * (full - ring_south)
                add_rows(adjoint_ref, start + 1, -(ADVECT_HALF * merids[0] - DIFFUSE) * change)
                merid_totals[0] = merid_totals[0] - (fields[0] + fields[1]) * change
            else:
                value = value + (ADVECT_HALF * merids[top - 1] - DIFFUSE) * change
                value = value + next_north * (ring_north - full)
                inner = (ADVECT_HALF * merids[top - 1] + DIFFUSE) * change
                add_rows(adjoint_ref, start + top - 1, inner)
                merid_totals[top - 1] = (
                    merid_totals[top - 1] + (fields[top - 1] + fields[top]) * change
                )
                field_north = rows_at(north_ref, layout.tracer[1] + tracer * levels)
                merid_totals[top] = merid_totals[top] + (fields[top] + field_north) * (
                    ring_north - full
                )
            add_rows(adjoint_ref, start + row, value)
        send(adjoint_ref, adjoint_hbm, tracer)
    for at, row in enumerate((0, top)):
        add_rows(velocity_ref, row, ADVECT_HALF * zonal_totals[at])
    send(velocity_ref, velocity_hbm, 0)
    for row, total in merid_totals.items():
        add_rows(velocity_ref, levels * ROWS + row, ADVECT_HALF * total)
    send(velocity_ref, velocity_hbm, 1)
    for copy in copies:
        copy.wait()


def swaps(pairs):
    return [pair for low, high in pairs for pair in ((low, high), (high, low))]


def ring_routes(tiles):
    inner = swaps((tile, tile + 1) for tile in range(0, tiles, 2))
    outer = swaps((tile, (tile + 1) % tiles) for tile in range(1, tiles, 2))
    return inner, outer


def line_routes(tiles, bands):
    near, far = [], []
    for tile in range(tiles):
        start = tile * bands
        near += [(start + band, start + band + 1) for band in range(0, bands, 2)]
        far += [(start + band, start + band + 1) for band in range(1, bands - 1, 2)]
        if tile < tiles // 2:
            far.append((start + bands - 1, (tiles - tile) * bands - 1))
    return swaps(near), swaps(far)


def call(kernel, outputs, scratch, scalars, arrays):
    vmem = pl.BlockSpec(memory_space=pltpu.VMEM)
    smem = pl.BlockSpec(memory_space=pltpu.SMEM)
    return pl.pallas_call(
        kernel,
        out_shape=[jax.ShapeDtypeStruct(shape, dtype) for shape, dtype in outputs],
        in_specs=[smem] * len(scalars) + [vmem] * len(arrays),
        out_specs=[vmem] * len(outputs),
        scratch_shapes=[pltpu.VMEM(shape, jnp.float32) for shape in scratch],
        compiler_params=pltpu.CompilerParams(vmem_limit_bytes=32 * 1024 * 1024),
    )(*scalars, *arrays)


def shards(final_adjoint, store, holder_offset, holder_slot, bottom_level, mix_class, mix_table):
    bands = lax.axis_size("lat")
    tiles = lax.axis_size("lon")
    levels = final_adjoint.shape[1]
    slots = store.shape[2]
    steps = len(STEP_ORDER)
    pieces = FIELDS * levels
    full = levels * ROWS
    layout = Layout(levels)
    narrow, wide = jnp.bfloat16, jnp.float32
    hbm = pl.BlockSpec(memory_space=pltpu.HBM)
    request = pl.pallas_call(
        request_kernel,
        out_shape=jax.ShapeDtypeStruct((bands, steps, pieces, LANES), narrow),
        in_specs=[hbm, hbm],
        out_specs=hbm,
        scratch_shapes=[
            pltpu.SMEM(holder_slot.shape, jnp.int32),
            pltpu.VMEM((pieces * slots, LANES), narrow),
            pltpu.VMEM((pieces * slots, LANES), wide),
            pltpu.VMEM((bands, steps, pieces, LANES), narrow),
            pltpu.SemaphoreType.DMA,
            pltpu.SemaphoreType.DMA((FIELDS,)),
            pltpu.SemaphoreType.DMA((bands,)),
        ],
        compiler_params=pltpu.CompilerParams(vmem_limit_bytes=32 * 1024 * 1024),
    )(
        pltpu.with_memory_space_constraint(holder_slot, pltpu.HBM),
        pltpu.with_memory_space_constraint(store.reshape(pieces * slots, LANES), pltpu.HBM),
    )
    received = lax.all_to_all(request, "lat", split_axis=0, concat_axis=0, tiled=True)
    masked, base, kappa, side, pick, holder = call(
        prepare_kernel,
        [
            ((2 * full, LANES), wide),
            ((2 * full, LANES), wide),
            ((full + ROWS, LANES), wide),
            ((4 * ROWS, 2 * LANES), wide),
            ((steps, ROWS * LANES, LANES), narrow),
            ((len(DRAFT_ROWS) * ROWS, LANES), wide),
        ],
        [(2 * LANES, LANES)],
        [mix_table, holder_offset],
        [
            final_adjoint.reshape(2 * full, LANES),
            bottom_level,
            mix_class.reshape((levels - 1) * ROWS, LANES),
        ],
    )
    outer, inner = call(
        edges_kernel,
        [((ROWS, EDGE_LANES), narrow), ((ROWS, EDGE_LANES), narrow)],
        [(EDGE_MASKED, LANES)],
        [],
        [received, side, pick],
    )
    inner_routes, outer_routes = ring_routes(tiles)
    near_routes, far_routes = line_routes(tiles, bands)
    outer = lax.ppermute(outer, "lon", outer_routes)
    inner = lax.ppermute(inner, "lon", inner_routes)
    top, bot = call(
        drafts_kernel,
        [((layout.rows, LANES), wide), ((layout.rows, LANES), wide)],
        [(len(DRAFT_ROWS) * pieces, LANES)],
        [],
        [received, holder, masked, base, bottom_level],
    )
    far, near, west, east, pack = call(
        functools.partial(complete_kernel, levels),
        [
            ((layout.rows, LANES), narrow),
            ((layout.rows, LANES), narrow),
            ((ROWS, EDGE_LANES), narrow),
            ((ROWS, EDGE_LANES), narrow),
            ((8 * levels, LANES), wide),
        ],
        [(LANES, EDGE_LANES), (EDGE_LANES, LANES), (layout.rows, LANES), (layout.rows, LANES)],
        [],
        [outer, inner, top, bot],
    )
    far = lax.ppermute(far, ("lon", "lat"), far_routes)
    near = lax.ppermute(near, ("lon", "lat"), near_routes)
    (state,) = call(
        tiles_kernel,
        [((steps * FIELDS * full, LANES), wide)],
        [],
        [holder_offset],
        [received, west],
    )
    adjoint, velocity, following = call(
        steps_kernel,
        [((2 * full, LANES), wide)] * 3,
        [(2 * full, LANES)],
        [],
        [west, east, state, masked, base, kappa, bottom_level],
    )
    arrays = (far, near, pack, west, east, state, masked, kappa, bottom_level, following)
    arrays += (adjoint, velocity)
    vmem = pl.BlockSpec(memory_space=pltpu.VMEM)
    adjoint, velocity, _, _ = pl.pallas_call(
        finish_kernel,
        out_shape=[jax.ShapeDtypeStruct((2 * full, LANES), wide)] * 4,
        in_specs=[vmem] * len(arrays),
        out_specs=[hbm, hbm, vmem, vmem],
        input_output_aliases={len(arrays) - 2: 2, len(arrays) - 1: 3},
        scratch_shapes=[
            pltpu.VMEM((layout.rows, LANES), wide),
            pltpu.VMEM((layout.rows, LANES), wide),
            pltpu.VMEM(((levels + 2 * ROWS + ROWS - 1) // ROWS * ROWS, LANES), wide),
            pltpu.SemaphoreType.DMA((4,)),
        ],
        compiler_params=pltpu.CompilerParams(vmem_limit_bytes=32 * 1024 * 1024),
    )(*arrays)
    shape = (2, levels, ROWS, LANES)
    return adjoint.reshape(shape), velocity.reshape(shape)


def solution(mesh):
    return jax.shard_map(
        shards,
        mesh=mesh,
        in_specs=(
            P(None, None, "lat", "lon"),
            P(None, None, None, "lat", "lon"),
            P(),
            P(),
            P("lat", "lon"),
            P(None, "lat", "lon"),
            P(),
        ),
        out_specs=(P(None, None, "lat", "lon"), P(None, None, "lat", "lon")),
        check_vma=False,
    )
```

```python
import functools

import jax
import jax.numpy as jnp
from jax import lax
from jax.experimental import pallas as pl
from jax.experimental.pallas import tpu as pltpu
from jax.sharding import PartitionSpec as P

STEP_ORDER = (1, 0)
FIELDS = 4
ADVECT_HALF = 0.125
DIFFUSE = 0.1

ROWS = 8
LANES = 128

EDGE_STATE = (0, 256)
EDGE_MASKED = 512
EDGE_PART = 640
EDGE_LANES = 768


DRAFT_ROWS = ((ROWS - 1, 0), (ROWS - 1, 1), (0, 0), (0, 1), (ROWS - 2, 0))


class Layout:
    def __init__(self, levels):
        self.tracer = (0, 3 * levels)
        self.merid = (2 * levels, 5 * levels)
        self.masked = 6 * levels
        self.part = 8 * levels
        self.corner = 10 * levels
        self.bottom = 11 * levels
        self.rows = (11 * levels + 1 + 15) // 16 * 16


def shift(block, amount, axis):
    return pltpu.roll(block, amount % block.shape[axis], axis)


def lanes_of(shape):
    return lax.broadcasted_iota(jnp.int32, shape, 1)


def rows_of(shape):
    return lax.broadcasted_iota(jnp.int32, shape, 0)


def strided(ref, start, count):
    return ref[pl.ds(start, count, stride=ROWS), :]


def request_kernel(
    slot_hbm, store_hbm, out_hbm, slot_ref, store_ref, wide_ref, pack_ref, slot_sem, in_sem, out_sem
):
    tile = lax.axis_index("lon")
    bands, steps, pieces, lanes = pack_ref.shape
    slots = store_ref.shape[0] // pieces
    parts = 2 * FIELDS
    length = store_ref.shape[0] // parts
    table = pltpu.make_async_copy(slot_hbm, slot_ref, slot_sem)
    table.start()
    loads = []
    for part in range(parts):
        here = pl.ds(part * length, length)
        load = pltpu.make_async_copy(store_hbm.at[here], store_ref.at[here], in_sem.at[part])
        load.start()
        loads.append(load)
    for part, load in enumerate(loads):
        load.wait()
        here = slice(part * length, (part + 1) * length)
        wide_ref[here] = store_ref[here].astype(jnp.float32)
    table.wait()
    stores = []
    for band in range(bands):
        for at, step in enumerate(STEP_ORDER):
            slot = slot_ref[step, band, tile]
            rows = wide_ref[pl.ds(slot, pieces, stride=slots), :]
            pack_ref[band, at] = rows.astype(jnp.bfloat16)
        store = pltpu.make_async_copy(pack_ref.at[band], out_hbm.at[band], out_sem.at[band])
        store.start()
        stores.append(store)
    for store in stores:
        store.wait()


def pick_columns(offset=0):
    place = (ROWS * LANES, LANES)
    row, source = rows_of(place) // LANES, rows_of(place) % LANES
    order = lanes_of(place) - (row + ROWS - offset) % ROWS
    chosen = (
        ((source == 0) & (order == 0))
        | ((source == LANES - 1) & (order == ROWS))
        | ((source == 1) & (order == 2 * ROWS))
        | ((source == LANES - 2) & (order == 3 * ROWS))
    )
    return jnp.where(chosen, 1.0, 0.0).astype(jnp.bfloat16)


def prepare_kernel(
    table_ref,
    offset_ref,
    adjoint_ref,
    bottom_ref,
    mix_ref,
    masked_ref,
    base_ref,
    kappa_ref,
    side_ref,
    pick_ref,
    holder_ref,
    column_ref,
):
    levels = adjoint_ref.shape[0] // (2 * ROWS)
    bottom = bottom_ref[...]
    edge = jnp.zeros((ROWS, LANES), jnp.float32)
    kappa_ref[0:ROWS] = edge
    kappa_ref[levels * ROWS : (levels + 1) * ROWS] = edge
    for level in range(levels - 1):
        classes = mix_ref[level * ROWS : (level + 1) * ROWS]
        kappa = jnp.full((ROWS, LANES), table_ref[0], jnp.float32)
        for index in range(1, table_ref.shape[0]):
            kappa = jnp.where(classes == index, table_ref[index], kappa)
        kappa_ref[(level + 1) * ROWS : (level + 2) * ROWS] = kappa
    for tracer in range(2):
        start = tracer * levels * ROWS
        for level in range(levels):
            here = slice(start + level * ROWS, start + (level + 1) * ROWS)
            masked_ref[here] = jnp.where(level < bottom, adjoint_ref[here], 0.0)
        for level in range(levels):
            base_ref[start + level * ROWS : start + (level + 1) * ROWS] = mixed(
                masked_ref, kappa_ref, start, level, levels
            )
    pick = pick_columns()
    offsets = []
    for at, step in enumerate(STEP_ORDER):
        offset = offset_ref[step, lax.axis_index("lat"), lax.axis_index("lon")]
        pick_ref[at] = pick_columns(offset)
        offsets.append(offset)
    for index, (row, at) in enumerate(DRAFT_ROWS):
        held = rows_of((ROWS, LANES)) == lax.rem(row + offsets[at], ROWS)
        holder_ref[index * ROWS : (index + 1) * ROWS] = jnp.where(held, 1.0, 0.0)
    column_ref[...] = jnp.zeros_like(column_ref)
    rows = 2 * levels
    for start, ref in ((0, masked_ref), (LANES, base_ref)):
        blocks = [strided(ref, row, rows).astype(jnp.bfloat16) for row in range(ROWS)]
        column_ref[start : start + rows] = jnp.dot(
            jnp.concatenate(blocks, axis=1), pick, preferred_element_type=jnp.float32
        )
    side = jnp.transpose(column_ref[...])[0 : 4 * ROWS]
    spot = lanes_of((ROWS, 2 * LANES)) == rows
    depth = bottom.astype(jnp.float32)
    side_ref[...] = side
    side_ref[0:ROWS] = jnp.where(spot, depth[:, 0:1], side[0:ROWS])
    side_ref[ROWS : 2 * ROWS] = jnp.where(spot, depth[:, LANES - 1 :], side[ROWS : 2 * ROWS])


def mixed(masked_ref, kappa_ref, start, level, levels):
    def at(index):
        return masked_ref[start + index * ROWS : start + (index + 1) * ROWS]

    masked = at(level)
    below = at(level + 1) if level + 1 < levels else jnp.zeros_like(masked)
    above = at(level - 1) if level > 0 else jnp.zeros_like(masked)
    kappa_above = kappa_ref[level * ROWS : (level + 1) * ROWS]
    kappa_below = kappa_ref[(level + 1) * ROWS : (level + 2) * ROWS]
    return masked + kappa_below * (below - masked) + kappa_above * (above - masked)


def edges_kernel(piece_ref, side_ref, pick_ref, outer_ref, inner_ref, column_ref):
    tile = lax.axis_index("lon")
    holders, steps, pieces, _ = piece_ref.shape
    levels = pieces // FIELDS
    column_ref[...] = jnp.zeros_like(column_ref)
    for at in range(steps):
        chunks = [piece_ref[holder, at] for holder in range(holders)]
        column_ref[EDGE_STATE[at] : EDGE_STATE[at] + pieces] = jnp.dot(
            jnp.concatenate(chunks, axis=1), pick_ref[at], preferred_element_type=jnp.float32
        )
    state = jnp.transpose(column_ref[...])
    lane = lanes_of((ROWS, 2 * LANES))
    sides = []
    for at, sign in ((0, 1.0), (1, -1.0)):
        edge = state[at * ROWS : (at + 1) * ROWS]
        zonal = edge if at == 0 else state[3 * ROWS : 4 * ROWS]
        zonal = zonal[:, 0 : 2 * LANES]
        zonal = jnp.where(lane < levels, shift(zonal, -2 * levels, 1), shift(zonal, -levels, 1))
        masked = side_ref[at * ROWS : (at + 1) * ROWS]
        beside = side_ref[(at + 2) * ROWS : (at + 3) * ROWS]
        face = (ADVECT_HALF * zonal + sign * DIFFUSE) * (sign * (beside - masked))
        part = masked[:, LANES:] + face[:, 0:LANES]
        side = jnp.concatenate([edge, masked[:, 0:LANES], part], axis=1)
        sides.append(side.astype(jnp.bfloat16))
    to_west, to_east = sides

    @pl.when(lax.rem(tile, 2) == 0)
    def _():
        inner_ref[...] = to_east
        outer_ref[...] = to_west

    @pl.when(lax.rem(tile, 2) == 1)
    def _():
        inner_ref[...] = to_west
        outer_ref[...] = to_east


def tiles_kernel(offset_ref, piece_ref, west_ref, state_ref):
    tile = lax.axis_index("lon")
    band = lax.axis_index("lat")
    holders, _, pieces, _ = piece_ref.shape
    for at, step in enumerate(STEP_ORDER):
        offset = offset_ref[step, band, tile]
        for row in range(ROWS):
            chunk = piece_ref[lax.rem(row + offset, holders), at]
            state_ref[pl.ds(at * pieces * ROWS + row, pieces, stride=ROWS), :] = chunk.astype(
                jnp.float32
            )


def drafts_kernel(
    piece_ref, holder_ref, masked_ref, base_ref, bottom_ref, top_ref, bot_ref, line_ref
):
    levels = masked_ref.shape[0] // (2 * ROWS)
    holders, steps, pieces, _ = piece_ref.shape
    for at in range(steps):
        wanted = [index for index, (_, step) in enumerate(DRAFT_ROWS) if step == at]
        found = [None] * len(wanted)
        for holder in range(holders):
            chunk = piece_ref[holder, at].astype(jnp.float32)
            for place, index in enumerate(wanted):
                if holder == 0:
                    found[place] = chunk
                    continue
                here = index * ROWS + holder
                held = jnp.broadcast_to(holder_ref[here : here + 1], chunk.shape) > 0.0
                found[place] = jnp.where(held, chunk, found[place])
        for place, index in enumerate(wanted):
            line_ref[index * pieces : (index + 1) * pieces] = found[place]
    bottom = bottom_ref[...].astype(jnp.float32)
    layout = Layout(levels)
    wide = lanes_of((levels, LANES))
    for row, inner, first, facing, draft_ref in (
        (ROWS - 1, ROWS - 2, 0, 4, top_ref),
        (0, 1, 2, 2, bot_ref),
    ):
        for at in range(2):
            begin = (first + at) * pieces
            draft_ref[layout.tracer[at] : layout.tracer[at] + 2 * levels] = line_ref[
                begin : begin + 2 * levels
            ]
            draft_ref[layout.merid[at] : layout.merid[at] + levels] = line_ref[
                begin + 3 * levels : begin + 4 * levels
            ]
        zonal = line_ref[first * pieces + 2 * levels : first * pieces + 3 * levels]
        merid = line_ref[facing * pieces + 3 * levels : facing * pieces + 4 * levels]
        east_factor = ADVECT_HALF * zonal + DIFFUSE
        west_factor = ADVECT_HALF * shift(zonal, 1, 1) - DIFFUSE
        for tracer in range(2):
            begin = tracer * levels * ROWS
            masked = strided(masked_ref, begin + row, levels)
            next_row = strided(masked_ref, begin + inner, levels)
            if row > inner:
                along = (ADVECT_HALF * merid - DIFFUSE) * (masked - next_row)
            else:
                along = (ADVECT_HALF * merid + DIFFUSE) * (next_row - masked)
            east = east_factor * (shift(masked, -1, 1) - masked)
            west = west_factor * (masked - shift(masked, 1, 1))
            part = strided(base_ref, begin + row, levels) + along
            part = part + jnp.where(wide < LANES - 1, east, 0.0) + jnp.where(wide > 0, west, 0.0)
            at_masked = layout.masked + tracer * levels
            at_part = layout.part + tracer * levels
            draft_ref[at_masked : at_masked + levels] = masked
            draft_ref[at_part : at_part + levels] = part
        draft_ref[layout.corner : layout.corner + levels] = zonal
        draft_ref[layout.bottom : layout.rows] = jnp.broadcast_to(
            bottom[row : row + 1], (layout.rows - layout.bottom, LANES)
        )


def complete_kernel(
    levels,
    outer_ref,
    inner_ref,
    top_draft_ref,
    bot_draft_ref,
    far_ref,
    near_ref,
    west_ref,
    east_ref,
    pack_ref,
    edge_ref,
    column_ref,
    top_ref,
    bot_ref,
):
    layout = Layout(levels)
    odd_tile = lax.rem(lax.axis_index("lon"), 2) == 1
    odd_band = lax.rem(lax.axis_index("lat"), 2) == 1

    @pl.when(odd_tile)
    def _():
        west_ref[...] = inner_ref[...]
        east_ref[...] = outer_ref[...]

    @pl.when(jnp.logical_not(odd_tile))
    def _():
        west_ref[...] = outer_ref[...]
        east_ref[...] = inner_ref[...]

    top_ref[...] = top_draft_ref[...]
    bot_ref[...] = bot_draft_ref[...]
    edge_ref[0:ROWS] = west_ref[...].astype(jnp.float32)
    edge_ref[ROWS : 2 * ROWS] = east_ref[...].astype(jnp.float32)
    column_ref[...] = jnp.transpose(edge_ref[...])
    lane = lanes_of((levels, LANES))

    def pair(start, row):
        block = column_ref[start : start + levels]
        return block[:, row : row + 1], block[:, ROWS + row : ROWS + row + 1]

    for row, draft_ref in ((ROWS - 1, top_ref), (0, bot_ref)):
        zonal = draft_ref[layout.corner : layout.corner + levels]
        zonal_west, _ = pair(EDGE_STATE[0] + 2 * levels, row)
        merid_west, merid_east = pair(EDGE_STATE[0] + 3 * levels, row)
        east_factor = ADVECT_HALF * zonal + DIFFUSE
        west_factor = ADVECT_HALF * zonal_west - DIFFUSE
        corner = jnp.where((lane == 32) | (lane == 96), merid_west, 0.0)
        corner = jnp.where((lane == 31) | (lane == 95), merid_east, corner)
        for tracer in range(2):
            west, east = pair(EDGE_MASKED + tracer * levels, row)
            at_masked = layout.masked + tracer * levels
            at_part = layout.part + tracer * levels
            masked = draft_ref[at_masked : at_masked + levels]
            face = jnp.where(lane == LANES - 1, east_factor * (east - masked), 0.0)
            face = jnp.where(lane == 0, west_factor * (masked - west), face)
            draft_ref[at_part : at_part + levels] = draft_ref[at_part : at_part + levels] + face
            corner = jnp.where(lane == (0, LANES // 2)[tracer], west, corner)
            corner = jnp.where(lane == (LANES - 1, LANES // 2 - 1)[tracer], east, corner)
        draft_ref[layout.corner : layout.corner + levels] = corner
        begin = 0 if row else 4 * levels
        pack_ref[begin : begin + levels] = corner
        zonal_west, _ = pair(EDGE_STATE[1] + 2 * levels, row)
        pack_ref[begin + levels : begin + 2 * levels] = jnp.broadcast_to(
            zonal_west, (levels, LANES)
        )
        for tracer in range(2):
            _, east = pair(EDGE_STATE[1] + tracer * levels, row)
            here = begin + (2 + tracer) * levels
            pack_ref[here : here + levels] = jnp.broadcast_to(east, (levels, LANES))

    @pl.when(odd_band)
    def _():
        near_ref[...] = bot_ref[...].astype(jnp.bfloat16)
        far_ref[...] = top_ref[...].astype(jnp.bfloat16)

    @pl.when(jnp.logical_not(odd_band))
    def _():
        near_ref[...] = top_ref[...].astype(jnp.bfloat16)
        far_ref[...] = bot_ref[...].astype(jnp.bfloat16)


class Tile:
    def __init__(self, levels, west_ref, east_ref, state_ref):
        self.levels = levels
        self.west_ref, self.east_ref, self.state_ref = west_ref, east_ref, state_ref
        self.shape = (ROWS, LANES)
        lane, row = lanes_of(self.shape), rows_of(self.shape)
        self.first_lane, self.last_lane = lane == 0, lane == LANES - 1
        self.bottom_row, self.top_row = row == 0, row == ROWS - 1

    def spread(self, ref, index):
        return jnp.broadcast_to(ref[:, index : index + 1].astype(jnp.float32), self.shape)

    def line(self, ref, index):
        return jnp.broadcast_to(ref[index : index + 1], self.shape)

    def side(self, index):
        return jnp.where(
            self.first_lane, self.spread(self.west_ref, index), self.spread(self.east_ref, index)
        )

    def velocities(self, at, level):
        begin = at * FIELDS * self.levels
        zonal = tile_of(self.state_ref, begin + 2 * self.levels + level)
        merid = tile_of(self.state_ref, begin + 3 * self.levels + level)
        zonal_west = jnp.where(
            self.first_lane,
            self.spread(self.west_ref, EDGE_STATE[at] + 2 * self.levels + level),
            shift(zonal, 1, 1),
        )
        return ADVECT_HALF * zonal, ADVECT_HALF * zonal_west, merid

    def tracer(self, at, level, tracer):
        field = tile_of(self.state_ref, (at * FIELDS + tracer) * self.levels + level)
        east = jnp.where(
            self.last_lane,
            self.spread(self.east_ref, EDGE_STATE[at] + tracer * self.levels + level),
            shift(field, -1, 1),
        )
        return field, east


def tile_of(ref, index):
    return ref[index * ROWS : (index + 1) * ROWS]


def steps_kernel(
    west_ref,
    east_ref,
    state_ref,
    masked_ref,
    base_ref,
    kappa_ref,
    bottom_ref,
    adjoint_ref,
    velocity_ref,
    next_ref,
    side_ref,
):
    levels = masked_ref.shape[0] // (2 * ROWS)
    tile = Tile(levels, west_ref, east_ref, state_ref)
    first_lane, last_lane = tile.first_lane, tile.last_lane
    top_row, bottom_row = tile.top_row, tile.bottom_row
    bottom = bottom_ref[...]
    side_bottom = tile.side(EDGE_MASKED + 2 * levels)
    for level in range(levels):
        zonal, zonal_west, merid = tile.velocities(0, level)
        north_factor = ADVECT_HALF * merid + DIFFUSE
        south_factor = ADVECT_HALF * shift(merid, 1, 0) - DIFFUSE
        side_merid = tile.side(EDGE_STATE[0] + 3 * levels + level)
        side_north = ADVECT_HALF * side_merid + DIFFUSE
        side_south = ADVECT_HALF * shift(side_merid, 1, 0) - DIFFUSE
        zonal_total = jnp.zeros(tile.shape, jnp.float32)
        merid_total = jnp.zeros(tile.shape, jnp.float32)
        for tracer in range(2):
            index = tracer * levels + level
            masked = tile_of(masked_ref, index)
            west = tile.spread(west_ref, EDGE_MASKED + index)
            east = tile.spread(east_ref, EDGE_MASKED + index)
            side = jnp.where(first_lane, west, east)
            to_east = jnp.where(last_lane, east, shift(masked, -1, 1)) - masked
            to_west = masked - jnp.where(first_lane, west, shift(masked, 1, 1))
            to_north = jnp.where(top_row, 0.0, shift(masked, -1, 0) - masked)
            to_south = jnp.where(bottom_row, 0.0, masked - shift(masked, 1, 0))
            result = (
                tile_of(base_ref, index)
                + (zonal + DIFFUSE) * to_east
                + (zonal_west - DIFFUSE) * to_west
                + north_factor * to_north
                + south_factor * to_south
            )
            next_ref[index * ROWS : (index + 1) * ROWS] = jnp.where(level < bottom, result, 0.0)
            field, field_east = tile.tracer(0, level, tracer)
            zonal_total = zonal_total + (field + field_east) * to_east
            merid_total = merid_total + (field + shift(field, -1, 0)) * to_north
            face = jnp.where(
                first_lane,
                (zonal_west + DIFFUSE) * (masked - side),
                (zonal - DIFFUSE) * (side - masked),
            )
            upper = jnp.where(top_row, 0.0, shift(side, -1, 0) - side)
            lower = jnp.where(bottom_row, 0.0, side - shift(side, 1, 0))
            result = (
                tile.side(EDGE_PART + index) + face + side_north * upper + side_south * lower
            )
            side_ref[index * ROWS : (index + 1) * ROWS] = jnp.where(
                side_bottom > level, result, 0.0
            )
        velocity_ref[level * ROWS : (level + 1) * ROWS] = ADVECT_HALF * zonal_total
        velocity_ref[(levels + level) * ROWS : (levels + level + 1) * ROWS] = (
            ADVECT_HALF * merid_total
        )

    for level in range(levels):
        zonal, zonal_west, merid = tile.velocities(1, level)
        north_factor = ADVECT_HALF * merid + DIFFUSE
        south_factor = ADVECT_HALF * shift(merid, 1, 0) - DIFFUSE
        zonal_total = jnp.zeros(tile.shape, jnp.float32)
        merid_total = jnp.zeros(tile.shape, jnp.float32)
        for tracer in range(2):
            index = tracer * levels + level
            masked = tile_of(next_ref, index)
            side = tile_of(side_ref, index)
            to_east = jnp.where(last_lane, side, shift(masked, -1, 1)) - masked
            to_west = masked - jnp.where(first_lane, side, shift(masked, 1, 1))
            to_north = jnp.where(top_row, 0.0, shift(masked, -1, 0) - masked)
            to_south = jnp.where(bottom_row, 0.0, masked - shift(masked, 1, 0))
            adjoint_ref[index * ROWS : (index + 1) * ROWS] = (
                mixed(next_ref, kappa_ref, tracer * levels * ROWS, level, levels)
                + (zonal + DIFFUSE) * to_east
                + (zonal_west - DIFFUSE) * to_west
                + north_factor * to_north
                + south_factor * to_south
            )
            field, field_east = tile.tracer(1, level, tracer)
            zonal_total = zonal_total + (field + field_east) * to_east
            merid_total = merid_total + (field + shift(field, -1, 0)) * to_north
        for total, begin in ((zonal_total, 0), (merid_total, levels)):
            here = slice((begin + level) * ROWS, (begin + level + 1) * ROWS)
            velocity_ref[here] = velocity_ref[here] + ADVECT_HALF * total


def finish_kernel(
    far_ref,
    near_ref,
    pack_ref,
    west_ref,
    east_ref,
    state_ref,
    masked_ref,
    kappa_ref,
    bottom_ref,
    next_ref,
    adjoint_in,
    velocity_in,
    adjoint_hbm,
    velocity_hbm,
    adjoint_ref,
    velocity_ref,
    north_ref,
    south_ref,
    guard_ref,
    out_sem,
):
    levels = masked_ref.shape[0] // (2 * ROWS)
    layout = Layout(levels)
    top = ROWS - 1
    band = lax.axis_index("lat")
    odd_band = lax.rem(band, 2) == 1
    top_band = (band == lax.axis_size("lat") - 1).astype(jnp.int32)
    folded = top_band.astype(jnp.float32)
    open_south = jnp.where(band > 0, DIFFUSE, 0.0)

    @pl.when(odd_band & (top_band == 0))
    def _():
        north_ref[...] = far_ref[...].astype(jnp.float32)

    @pl.when(odd_band & (top_band == 1))
    def _():
        square = (LANES, LANES)
        turn = lanes_of(square) + rows_of(square) == LANES - 1
        turn = jnp.where(turn, 1.0, 0.0).astype(jnp.bfloat16)
        north_ref[...] = jnp.dot(far_ref[...], turn, preferred_element_type=jnp.float32)

    @pl.when(odd_band)
    def _():
        south_ref[...] = near_ref[...].astype(jnp.float32)

    @pl.when(jnp.logical_not(odd_band))
    def _():
        north_ref[...] = near_ref[...].astype(jnp.float32)
        south_ref[...] = far_ref[...].astype(jnp.float32)

    copies = []

    def send(source, target, part):
        here = pl.ds(part * levels * ROWS, levels * ROWS)
        copy = pltpu.make_async_copy(source.at[here], target.at[here], out_sem.at[len(copies)])
        copy.start()
        copies.append(copy)

    guard_ref[...] = jnp.zeros_like(guard_ref)

    def rows_at(ref, begin):
        return ref[begin : begin + levels]

    def unpacked(packed):
        return packed, shift(packed, LANES // 2, 1), shift(packed, 96, 1)

    def state_row(at, field, row):
        return strided(state_ref, (at * FIELDS + field) * levels * ROWS + row, levels)

    def add_rows(ref, begin, value):
        here = pl.ds(begin, levels, stride=ROWS)
        ref[here, :] = ref[here, :] + value

    level_of = rows_of((levels, LANES)).astype(jnp.float32)
    lane = lanes_of((levels, LANES))
    first_lane, last_lane = lane == 0, lane == LANES - 1

    def side_depth(row):
        spot = slice(EDGE_MASKED + 2 * levels, EDGE_MASKED + 2 * levels + 1)
        west = west_ref[...].astype(jnp.float32)[row : row + 1, spot]
        east = east_ref[...].astype(jnp.float32)[row : row + 1, spot]
        return jnp.where(lane < LANES // 2, west, east)

    depth = bottom_ref[...].astype(jnp.float32)
    merid_top = state_row(0, 3, top)
    north_merid = rows_at(north_ref, layout.merid[0]) * folded
    south_merid = rows_at(south_ref, layout.merid[0])
    top_factor = ADVECT_HALF * (merid_top - north_merid) + DIFFUSE
    bottom_factor = ADVECT_HALF * south_merid - open_south
    own_corner = (unpacked(rows_at(pack_ref, 4 * levels)), unpacked(rows_at(pack_ref, 0)))
    north_corner = unpacked(rows_at(north_ref, layout.corner))
    south_corner = unpacked(rows_at(south_ref, layout.corner))
    side_top = ADVECT_HALF * (own_corner[1][2] - folded * north_corner[2]) + DIFFUSE
    side_bottom = ADVECT_HALF * south_corner[2] - open_south

    merids = {row: state_row(1, 3, row) for row in (0, top - 1, top)}
    next_north = ADVECT_HALF * (merids[top] - folded * rows_at(north_ref, layout.merid[1])) + DIFFUSE
    next_south = ADVECT_HALF * rows_at(south_ref, layout.merid[1]) - open_south
    east_factors, west_factors, kappas = [], [], []
    for row, begin in ((0, 4 * levels), (top, 0)):
        zonal = state_row(1, 2, row)
        zonal_west = jnp.where(first_lane, rows_at(pack_ref, begin + levels), shift(zonal, 1, 1))
        east_factors.append(ADVECT_HALF * zonal + DIFFUSE)
        west_factors.append(ADVECT_HALF * zonal_west - DIFFUSE)
        kappas.append(
            (strided(kappa_ref, row, levels), strided(kappa_ref, ROWS + row, levels))
        )

    zonal_totals = [jnp.zeros((levels, LANES), jnp.float32) for _ in range(2)]
    merid_totals = {row: jnp.zeros((levels, LANES), jnp.float32) for row in (0, top - 1, top)}
    for tracer in range(2):
        start = tracer * levels * ROWS
        own_top = strided(masked_ref, start + top, levels)
        own_bottom = strided(masked_ref, start, levels)
        north = rows_at(north_ref, layout.masked + tracer * levels)
        south = rows_at(south_ref, layout.masked + tracer * levels)
        north_step, south_step = north - own_top, own_bottom - south
        wet = level_of < north_ref[layout.bottom : layout.bottom + 1]
        ring_north = rows_at(north_ref, layout.part + tracer * levels)
        ring_north = ring_north - (ADVECT_HALF * (north_merid - merid_top) + DIFFUSE) * north_step
        ring_north = jnp.where(wet, ring_north, 0.0)
        wet = level_of < south_ref[layout.bottom : layout.bottom + 1]
        ring_south = rows_at(south_ref, layout.part + tracer * levels)
        ring_south = ring_south + (ADVECT_HALF * south_merid + DIFFUSE) * south_step
        ring_south = jnp.where(wet, ring_south, 0.0)
        first_field = state_row(0, tracer, top) + rows_at(
            north_ref, layout.tracer[0] + tracer * levels
        )
        merid_totals[top] = merid_totals[top] + first_field * north_step
        changes = (
            jnp.where(level_of < depth[0:1], bottom_factor * south_step, 0.0),
            jnp.where(level_of < depth[top:], top_factor * north_step, 0.0),
        )
        side_changes = (
            side_bottom * (own_corner[0][tracer] - south_corner[tracer]),
            side_top * (north_corner[tracer] - own_corner[1][tracer]),
        )
        fields = {row: state_row(1, tracer, row) for row in (0, 1, top - 1, top)}
        for at, row in enumerate((0, top)):
            change = changes[at]
            side = jnp.where(level_of < side_depth(row), side_changes[at], 0.0)
            guard_ref[ROWS : ROWS + levels] = change
            above = guard_ref[ROWS - 1 : ROWS - 1 + levels]
            below = guard_ref[ROWS + 1 : ROWS + 1 + levels]
            kappa_above, kappa_below = kappas[at]
            to_east = jnp.where(last_lane, side, shift(change, -1, 1)) - change
            to_west = change - jnp.where(first_lane, side, shift(change, 1, 1))
            value = (
                change
                + kappa_below * (below - change)
                + kappa_above * (above - change)
                + east_factors[at] * to_east
                + west_factors[at] * to_west
            )
            begin = (4 * levels if row == 0 else 0) + (2 + tracer) * levels
            field_east = jnp.where(
                last_lane, rows_at(pack_ref, begin), shift(fields[row], -1, 1)
            )
            zonal_totals[at] = zonal_totals[at] + (fields[row] + field_east) * to_east
            full = strided(next_ref, start + row, levels) + change
            if row == 0:
                value = value - (ADVECT_HALF * merids[0] + DIFFUSE) * change
                value = value + next_south * (full - ring_south)
                add_rows(adjoint_ref, start + 1, -(ADVECT_HALF * merids[0] - DIFFUSE) * change)
                merid_totals[0] = merid_totals[0] - (fields[0] + fields[1]) * change
            else:
                value = value + (ADVECT_HALF * merids[top - 1] - DIFFUSE) * change
                value = value + next_north * (ring_north - full)
                inner = (ADVECT_HALF * merids[top - 1] + DIFFUSE) * change
                add_rows(adjoint_ref, start + top - 1, inner)
                merid_totals[top - 1] = (
                    merid_totals[top - 1] + (fields[top - 1] + fields[top]) * change
                )
                field_north = rows_at(north_ref, layout.tracer[1] + tracer * levels)
                merid_totals[top] = merid_totals[top] + (fields[top] + field_north) * (
                    ring_north - full
                )
            add_rows(adjoint_ref, start + row, value)
        send(adjoint_ref, adjoint_hbm, tracer)
    for at, row in enumerate((0, top)):
        add_rows(velocity_ref, row, ADVECT_HALF * zonal_totals[at])
    send(velocity_ref, velocity_hbm, 0)
    for row, total in merid_totals.items():
        add_rows(velocity_ref, levels * ROWS + row, ADVECT_HALF * total)
    send(velocity_ref, velocity_hbm, 1)
    for copy in copies:
        copy.wait()


def swaps(pairs):
    return [pair for low, high in pairs for pair in ((low, high), (high, low))]


def ring_routes(tiles):
    inner = swaps((tile, tile + 1) for tile in range(0, tiles, 2))
    outer = swaps((tile, (tile + 1) % tiles) for tile in range(1, tiles, 2))
    return inner, outer


def line_routes(tiles, bands):
    near, far = [], []
    for tile in range(tiles):
        start = tile * bands
        near += [(start + band, start + band + 1) for band in range(0, bands, 2)]
        far += [(start + band, start + band + 1) for band in range(1, bands - 1, 2)]
        if tile < tiles // 2:
            far.append((start + bands - 1, (tiles - tile) * bands - 1))
    return swaps(near), swaps(far)


def call(kernel, outputs, scratch, scalars, arrays):
    vmem = pl.BlockSpec(memory_space=pltpu.VMEM)
    smem = pl.BlockSpec(memory_space=pltpu.SMEM)
    return pl.pallas_call(
        kernel,
        out_shape=[jax.ShapeDtypeStruct(shape, dtype) for shape, dtype in outputs],
        in_specs=[smem] * len(scalars) + [vmem] * len(arrays),
        out_specs=[vmem] * len(outputs),
        scratch_shapes=[pltpu.VMEM(shape, jnp.float32) for shape in scratch],
        compiler_params=pltpu.CompilerParams(vmem_limit_bytes=32 * 1024 * 1024),
    )(*scalars, *arrays)


def shards(final_adjoint, store, holder_offset, holder_slot, bottom_level, mix_class, mix_table):
    bands = lax.axis_size("lat")
    tiles = lax.axis_size("lon")
    levels = final_adjoint.shape[1]
    slots = store.shape[2]
    steps = len(STEP_ORDER)
    pieces = FIELDS * levels
    full = levels * ROWS
    layout = Layout(levels)
    narrow, wide = jnp.bfloat16, jnp.float32
    hbm = pl.BlockSpec(memory_space=pltpu.HBM)
    request = pl.pallas_call(
        request_kernel,
        out_shape=jax.ShapeDtypeStruct((bands, steps, pieces, LANES), narrow),
        in_specs=[hbm, hbm],
        out_specs=hbm,
        scratch_shapes=[
            pltpu.SMEM(holder_slot.shape, jnp.int32),
            pltpu.VMEM((pieces * slots, LANES), narrow),
            pltpu.VMEM((pieces * slots, LANES), wide),
            pltpu.VMEM((bands, steps, pieces, LANES), narrow),
            pltpu.SemaphoreType.DMA,
            pltpu.SemaphoreType.DMA((2 * FIELDS,)),
            pltpu.SemaphoreType.DMA((bands,)),
        ],
        compiler_params=pltpu.CompilerParams(vmem_limit_bytes=32 * 1024 * 1024),
    )(
        pltpu.with_memory_space_constraint(holder_slot, pltpu.HBM),
        pltpu.with_memory_space_constraint(store.reshape(pieces * slots, LANES), pltpu.HBM),
    )
    received = lax.all_to_all(request, "lat", split_axis=0, concat_axis=0, tiled=True)
    masked, base, kappa, side, pick, holder = call(
        prepare_kernel,
        [
            ((2 * full, LANES), wide),
            ((2 * full, LANES), wide),
            ((full + ROWS, LANES), wide),
            ((4 * ROWS, 2 * LANES), wide),
            ((steps, ROWS * LANES, LANES), narrow),
            ((len(DRAFT_ROWS) * ROWS, LANES), wide),
        ],
        [(2 * LANES, LANES)],
        [mix_table, holder_offset],
        [
            final_adjoint.reshape(2 * full, LANES),
            bottom_level,
            mix_class.reshape((levels - 1) * ROWS, LANES),
        ],
    )
    outer, inner = call(
        edges_kernel,
        [((ROWS, EDGE_LANES), narrow), ((ROWS, EDGE_LANES), narrow)],
        [(EDGE_MASKED, LANES)],
        [],
        [received, side, pick],
    )
    inner_routes, outer_routes = ring_routes(tiles)
    near_routes, far_routes = line_routes(tiles, bands)
    outer = lax.ppermute(outer, "lon", outer_routes)
    inner = lax.ppermute(inner, "lon", inner_routes)
    top, bot = call(
        drafts_kernel,
        [((layout.rows, LANES), wide), ((layout.rows, LANES), wide)],
        [(len(DRAFT_ROWS) * pieces, LANES)],
        [],
        [received, holder, masked, base, bottom_level],
    )
    far, near, west, east, pack = call(
        functools.partial(complete_kernel, levels),
        [
            ((layout.rows, LANES), narrow),
            ((layout.rows, LANES), narrow),
            ((ROWS, EDGE_LANES), narrow),
            ((ROWS, EDGE_LANES), narrow),
            ((8 * levels, LANES), wide),
        ],
        [(LANES, EDGE_LANES), (EDGE_LANES, LANES), (layout.rows, LANES), (layout.rows, LANES)],
        [],
        [outer, inner, top, bot],
    )
    far = lax.ppermute(far, ("lon", "lat"), far_routes)
    near = lax.ppermute(near, ("lon", "lat"), near_routes)
    (state,) = call(
        tiles_kernel,
        [((steps * FIELDS * full, LANES), wide)],
        [],
        [holder_offset],
        [received, west],
    )
    adjoint, velocity, following = call(
        steps_kernel,
        [((2 * full, LANES), wide)] * 3,
        [(2 * full, LANES)],
        [],
        [west, east, state, masked, base, kappa, bottom_level],
    )
    arrays = (far, near, pack, west, east, state, masked, kappa, bottom_level, following)
    arrays += (adjoint, velocity)
    vmem = pl.BlockSpec(memory_space=pltpu.VMEM)
    adjoint, velocity, _, _ = pl.pallas_call(
        finish_kernel,
        out_shape=[jax.ShapeDtypeStruct((2 * full, LANES), wide)] * 4,
        in_specs=[vmem] * len(arrays),
        out_specs=[hbm, hbm, vmem, vmem],
        input_output_aliases={len(arrays) - 2: 2, len(arrays) - 1: 3},
        scratch_shapes=[
            pltpu.VMEM((layout.rows, LANES), wide),
            pltpu.VMEM((layout.rows, LANES), wide),
            pltpu.VMEM(((levels + 2 * ROWS + ROWS - 1) // ROWS * ROWS, LANES), wide),
            pltpu.SemaphoreType.DMA((4,)),
        ],
        compiler_params=pltpu.CompilerParams(vmem_limit_bytes=32 * 1024 * 1024),
    )(*arrays)
    shape = (2, levels, ROWS, LANES)
    return adjoint.reshape(shape), velocity.reshape(shape)


def solution(mesh):
    return jax.shard_map(
        shards,
        mesh=mesh,
        in_specs=(
            P(None, None, "lat", "lon"),
            P(None, None, None, "lat", "lon"),
            P(),
            P(),
            P("lat", "lon"),
            P(None, "lat", "lon"),
            P(),
        ),
        out_specs=(P(None, None, "lat", "lon"), P(None, None, "lat", "lon")),
        check_vma=False,
    )
```
